32 devices in a mesh: blk: 8 (over z, x), head: 4 (over y, core).
Axes of the slice: x: 2, y: 2, z: 4, core: 2. Of those that a mesh axis runs over, the one named last changes fastest.
Arguments:
- states: bfloat16 [2048, 2, 2048], P(('blk', 'head')), may hold values from -6 to 6
- teacher: bfloat16 [2048, 2, 2048], P('blk'), may hold values from -6 to 6
- valid: int32 [2048, 2], P('blk'), may hold values from 0 to 1, as said below
- routes: int32 [2048, 2, 6], P('blk'), may hold values from 0 to 15, all different within a row; in each aligned block of 512 rows (0 to 511, 512 to 1023, ..., all dimensions but the last counted through in order) at most 256 rows name the same one
- norm_in: bfloat16 [2048], P('blk'), may hold values from 0.099609375 to 1.8984375
- w_query: bfloat16 [2048, 3072], P('blk', 'head'), may hold values from -0.125 to 0.125
- w_down_kv: bfloat16 [2048, 576], P('blk'), may hold values from -0.125 to 0.125
- norm_kv: bfloat16 [512], P('blk'), may hold values from 0.099609375 to 1.8984375
- w_up_kv: bfloat16 [512, 4096], P('blk', 'head'), may hold values from -0.25 to 0.25
- w_out: bfloat16 [2048, 2048], P('head', 'blk'), may hold values from -4 to 4
- norm_ffn: bfloat16 [2048], P('blk'), may hold values from 0.099609375 to 1.8984375
- w_router: bfloat16 [2048, 16], P('blk'), may hold values from -0.125 to 0.125
- shared_in: bfloat16 [2048, 2, 2816], P('blk', None, 'head'), may hold values from -0.125 to 0.125
- shared_out: bfloat16 [2816, 2048], P('head', 'blk'), may hold values from -0.109375 to 0.109375
- expert_in: bfloat16 [16, 2048, 2, 1408], P('blk', None, None, 'head'), may hold values from -0.125 to 0.125
- expert_out: bfloat16 [16, 1408, 2048], P('blk', 'head'), may hold values from -0.15625 to 0.15625
Outputs:
- layer_out: bfloat16 [2048, 2, 2048], P(('blk', 'head'))
- loss: float32 [], replicated
- grad_states: float32 [2048, 2, 2048], P(('blk', 'head'))
- grad_norm_in: float32 [2048], P('blk')
- grad_w_query: float32 [2048, 3072], P('blk', 'head')
- grad_w_down_kv: float32 [2048, 576], P('blk')
- grad_norm_kv: float32 [512], P('blk')
- grad_w_up_kv: float32 [512, 4096], P('blk', 'head')
- grad_w_out: float32 [2048, 2048], P('head', 'blk')
- grad_norm_ffn: float32 [2048], P('blk')
- grad_w_router: float32 [2048, 16], P('blk')
- grad_shared_in: float32 [2048, 2, 2816], P('blk', None, 'head')
- grad_shared_out: float32 [2816, 2048], P('head', 'blk')
- grad_expert_in: float32 [16, 2048, 2, 1408], P('blk', None, None, 'head')
- grad_expert_out: float32 [16, 1408, 2048], P('blk', 'head')
The draws below stay inside these ranges and needn't reach their ends.
Inputs may be any that keep to these rules, and one draw needn't show every extreme that they name: `routes`: in the 512 rows of one index of blk (one block of positions of all sequences), no expert is named more than 256 times, a bound that some expert reaches in some of these blocks. The last position of every sequence is valid.
All inputs are finite; a program needn't handle non-finite values.
Results may differ from the reference program's by a relative error of at most 0.022.
Values may be sent and summed in bfloat16 or wider, within the bound.
No kernel may reach another device: no remote copies, remote signals or barrier semaphores. Data moves between devices by JAX's collectives and lax.ppermute only.
A program may use at most 448 MiB of HBM per device.

```python
import math
import jax
import jax.numpy as jnp
import numpy as np
from jax import lax

D = 2048
HEADS = 16
UNROTATED_WIDTH = 128
ROPE = 64
VALUE_WIDTH = 128
RANK = 512
EFF = 1408
SHARED = 2816
TOP = 6
TOK_DEV = 128
SEQS = 2
BLOCK = 256
EXPERTS = 16
LENGTH = 2048
CAP = 256
N_BLK = 8
N_HEAD = 4


def draw_valid(key, part):
    level = jax.random.randint(key, (LENGTH, SEQS), 0, 1000)
    place = jnp.arange(LENGTH, dtype=jnp.int32)[:, None]
    limit = 300 + 700 * (place + 1) // LENGTH
    return (level < limit).astype(jnp.int32)


def shard_levels(rng, shape, shards, low, largest):
    factor_of = 1.0
    for dim, parts in shards:
        draws = jax.random.uniform(jax.random.fold_in(jax.random.fold_in(rng, 6), dim), (parts,), jnp.float32, low / len(shards), largest / len(shards))
        factor_of = factor_of * jnp.repeat(jnp.exp(draws), shape[dim] // parts).reshape((-1,) + (1,) * (len(shape) - 1 - dim))
    return factor_of


def routed_block(own_key, own, number, rows, number_of, top, bound, skew):
    order = jax.random.permutation(own_key, number_of)
    crowded, ordinary = portions_of(number_of, rows * top, bound, skew, True), portions_of(number_of, rows * top, bound, skew, False)
    places = jnp.arange(number_of)

    def named(tallies, turn):
        used = int((tallies > 0).sum())
        fixed = max(1, used // 4)
        shifted = fixed + (places - fixed + turn * (used - fixed)) % max(1, number_of - fixed)
        return jnp.zeros((number_of,), jnp.int32).at[order[jnp.where(places < fixed, places, shifted)]].set(jnp.asarray(tallies, jnp.int32))

    tallies = jnp.where(number % 4 == 0, named(crowded, number // 4), named(ordinary, number - number // 4 - 1))
    mixed = jax.random.permutation(jax.random.fold_in(own, 3), number_of)
    donor, sink = mixed[0:number_of // 2 * 2:2], mixed[1:number_of // 2 * 2:2]
    slack = jnp.minimum(tallies[donor] - 1, bound - tallies[sink]) // 2
    slack = jnp.where((donor == order[0]) | (sink == order[0]) | (tallies[sink] == 0), 0, jnp.maximum(slack, 0))
    shifted = jax.random.randint(jax.random.fold_in(own, 4), (number_of // 2,), 0, 1 << 20) % (slack + 1)
    tallies = tallies.at[donor].add(-shifted).at[sink].add(shifted)
    labels = jnp.searchsorted(jnp.cumsum(tallies), jnp.arange(rows * top), side="right").astype(jnp.int32)
    listing = labels.reshape(top, rows).T
    listing = listing[jax.random.permutation(jax.random.fold_in(own, 1), rows)]
    turn = jax.random.randint(jax.random.fold_in(own, 2), (rows, 1), 0, top)
    return jnp.take_along_axis(listing, (jnp.arange(top)[None, :] + turn) % top, axis=1)


def portions_of(number_of, total, bound, lean, full):
    loads = [(1 << 20) // math.isqrt(standing ** lean) + 1 for standing in range(1, number_of + 1)]
    largest = bound if full else min(bound, max(-(-total // number_of), total * loads[0] // sum(loads)))
    least = 1 if total - largest >= number_of - 1 else 0
    counts, surplus = [largest] + [least] * (number_of - 1), total - largest - least * (number_of - 1)
    while surplus > 0:
        candidates = [i for i in range(1, number_of) if counts[i] < largest] or [i for i in range(1, number_of) if counts[i] < bound]
        whole, left = sum([loads[i] for i in candidates]), surplus
        for i in candidates:
            extra = min(bound - counts[i], max(1, left * loads[i] // whole), surplus)
            counts[i] = counts[i] + extra
            surplus = surplus - extra
    return np.array(counts)


def gaussian(stream_key, extent, width, most, shards=(), kind=jnp.bfloat16):
    loudness = shard_levels(stream_key, extent, shards, -0.22, 0.18) if shards else 1.0
    values = jax.random.normal(stream_key, extent, jnp.float32) * width * loudness
    return jnp.minimum(jnp.maximum(values, -most), most).astype(kind)


def setup_inputs(seed: int = 0) -> dict:
    arg_keys = jax.random.split(jax.random.key(seed), 17)
    states = gaussian(arg_keys[0], (LENGTH, SEQS, D), 1.0, 6.0, ((0, 32),))
    teacher = gaussian(arg_keys[1], (LENGTH, SEQS, D), 1.0, 6.0, ((0, 8),))
    valid = draw_valid(jax.random.fold_in(arg_keys[16], 71), 0)
    routes_keys = jax.random.split(jax.random.fold_in(arg_keys[3], 1), LENGTH * SEQS // (TOK_DEV * N_HEAD))
    routes_turns = jax.random.permutation(jax.random.fold_in(arg_keys[3], 3), LENGTH * SEQS // (TOK_DEV * N_HEAD))
    routes = jax.vmap(lambda own, number: routed_block(jax.random.fold_in(arg_keys[3], 2), own, number, TOK_DEV * N_HEAD, EXPERTS, TOP, CAP, 2))(routes_keys, routes_turns).reshape((LENGTH, SEQS, TOP))
    norm_in = jnp.clip(1.0 + 0.18 * jax.random.normal(arg_keys[4], (D,), jnp.float32), 0.099609375, 1.8984375).astype(jnp.bfloat16)
    w_query = gaussian(arg_keys[5], (D, HEADS * (UNROTATED_WIDTH + ROPE)), D ** -0.5, 0.125, ((0, 8), (1, 4)))
    w_down_kv = gaussian(arg_keys[6], (D, RANK + ROPE), D ** -0.5, 0.125, ((0, 8),))
    norm_kv = jnp.clip(1.0 + 0.18 * jax.random.normal(arg_keys[7], (RANK,), jnp.float32), 0.099609375, 1.8984375).astype(jnp.bfloat16)
    w_up_kv = gaussian(arg_keys[8], (RANK, HEADS * (UNROTATED_WIDTH + VALUE_WIDTH)), RANK ** -0.5, 0.25, ((0, 8), (1, 4)))
    w_out = gaussian(arg_keys[9], (HEADS * VALUE_WIDTH, D), 0.7, 4.0, ((0, 4), (1, 8)))
    norm_ffn = jnp.clip(1.0 + 0.18 * jax.random.normal(arg_keys[10], (D,), jnp.float32), 0.099609375, 1.8984375).astype(jnp.bfloat16)
    w_router = gaussian(arg_keys[11], (D, EXPERTS), D ** -0.5, 0.125, ((0, 8),))
    shared_in = gaussian(arg_keys[12], (D, 2, SHARED), D ** -0.5, 0.125, ((0, 8), (2, 4)))
    shared_out = gaussian(arg_keys[13], (SHARED, D), SHARED ** -0.5, 0.109375, ((0, 4), (1, 8)))
    expert_in = gaussian(arg_keys[14], (EXPERTS, D, 2, EFF), D ** -0.5, 0.125, ((0, 8), (3, 4)))
    expert_out = gaussian(arg_keys[15], (EXPERTS, EFF, D), EFF ** -0.5, 0.15625, ((0, 8), (1, 4)))
    return {"states": states, "teacher": teacher, "valid": valid, "routes": routes, "norm_in": norm_in, "w_query": w_query, "w_down_kv": w_down_kv, "norm_kv": norm_kv, "w_up_kv": w_up_kv, "w_out": w_out, "norm_ffn": norm_ffn, "w_router": w_router, "shared_in": shared_in, "shared_out": shared_out, "expert_in": expert_in, "expert_out": expert_out}


@jax.custom_vjp
def reduced_precision(v):
    return lax.optimization_barrier(v.astype(jnp.bfloat16)).astype(jnp.float32)

@jax.custom_vjp
def reduced_backward(v):
    return v

def low_keep(v):
    return (reduced_precision(v), None)

def low_pass(kept, grad):
    return (grad,)

def back_keep(v):
    return (v, None)

def back_low(kept, grad):
    return (reduced_precision(grad),)
reduced_precision.defvjp(low_keep, low_pass)
reduced_backward.defvjp(back_keep, back_low)
precision_highest = lax.Precision.HIGHEST
epsilon = 1e-06

def normed(values, gain_vec):
    return values * lax.rsqrt(lax.optimization_barrier(jnp.mean(values * values, axis=-1, keepdims=True)) + epsilon) * gain_vec

def angles(position, rope_width):
    half_width = rope_width // 2
    frequency = 10000.0 ** (-2.0 * jnp.arange(half_width, dtype=jnp.float32) / rope_width)
    return position.astype(jnp.float32)[:, None] * frequency[None, :]

def rotate(values, angle_table):
    half_width = values.shape[-1] // 2
    bcast_shape = (angle_table.shape[0],) + (1,) * (values.ndim - 2) + (half_width,)
    cosine = jnp.cos(angle_table).reshape(bcast_shape)
    sine = jnp.sin(angle_table).reshape(bcast_shape)
    first_half = values[..., :half_width]
    second_half = values[..., half_width:]
    return jnp.concatenate([first_half * cosine - second_half * sine, second_half * cosine + first_half * sine], axis=-1)

def silu_gate(gate_up):
    return jax.nn.silu(gate_up[..., 0, :]) * gate_up[..., 1, :]

def reference(states, teacher, valid, routes, norm_in, w_query, w_down_kv, norm_kv, w_up_kv, w_out, norm_ffn, w_router, shared_in, shared_out, expert_in, expert_out):
    sequence_length, sequence_count, model_width = states.shape
    count_of_heads = w_query.shape[1] // (UNROTATED_WIDTH + ROPE)
    experts = w_router.shape[1]
    tokens = sequence_length * sequence_count
    slot_count = N_BLK * CAP
    query_span = min(512, sequence_length)
    position = jnp.arange(sequence_length, dtype=jnp.int32)
    angle_table = angles(position, ROPE)
    block_of = position // BLOCK
    score_scale = (UNROTATED_WIDTH + ROPE) ** (-0.5)
    valid_f = valid.astype(jnp.float32)
    valid_count = jnp.sum(valid_f)
    target = teacher.astype(jnp.float32)
    flat_routes = routes.reshape(-1).astype(jnp.int32)
    route_pick = (routes[..., None] == jnp.arange(experts, dtype=jnp.int32)).astype(jnp.float32)
    params = tuple((item.astype(jnp.float32) for item in (norm_in, w_query, w_down_kv, norm_kv, w_up_kv, w_out, norm_ffn, w_router, shared_in, shared_out, expert_in, expert_out)))

    def layer_forward(inputs, params):
        gain_in, query_w, down_w, gain_kv, up_weight, out_w, gain_ffn, router_w, shin_w, shared_output_weight, ein_w, eout_w = params
        normed_in = reduced_precision(normed(inputs, gain_in))
        query_raw = reduced_backward(jnp.einsum('lsd,dc->lsc', normed_in, query_w, precision=precision_highest)).reshape(sequence_length, sequence_count, count_of_heads, UNROTATED_WIDTH + ROPE)
        query_nope = reduced_precision(query_raw[..., :UNROTATED_WIDTH])
        query_rope = reduced_precision(rotate(query_raw[..., UNROTATED_WIDTH:], angle_table))
        latent = reduced_backward(jnp.einsum('lsd,dc->lsc', normed_in, down_w, precision=precision_highest))
        normed_latent = reduced_precision(normed(latent[..., :RANK], gain_kv))
        key_rope = reduced_precision(rotate(latent[..., RANK:], angle_table))
        key_value_rows = reduced_precision(jnp.einsum('zoe,eb->zob', normed_latent, up_weight, precision=precision_highest)).reshape(sequence_length, sequence_count, count_of_heads, UNROTATED_WIDTH + VALUE_WIDTH)
        key_nope = key_value_rows[..., :UNROTATED_WIDTH]
        value_part = key_value_rows[..., UNROTATED_WIDTH:]

        def attend(first_row):
            query_nope_block = lax.dynamic_slice_in_dim(query_nope, first_row, query_span, 0)
            query_rope_block = lax.dynamic_slice_in_dim(query_rope, first_row, query_span, 0)
            raw_score = jnp.einsum('qshd,kshd->shqk', query_nope_block, key_nope, precision=precision_highest) + jnp.einsum('qshr,ksr->shqk', query_rope_block, key_rope, precision=precision_highest)
            scores = reduced_backward(raw_score) * score_scale
            allowed = block_of[None, :] <= lax.dynamic_slice_in_dim(block_of, first_row, query_span, 0)[:, None]
            scores = jnp.where(allowed, scores, -1e+30)
            row_max = lax.optimization_barrier(jnp.max(scores, axis=-1, keepdims=True))
            exp_scores = jnp.where(allowed, jnp.exp(scores - row_max), 0.0)
            row_sum = lax.optimization_barrier(jnp.sum(exp_scores, axis=-1, keepdims=True))
            attn_mix = jnp.einsum('shqk,kshv->shqv', reduced_precision(exp_scores), value_part, precision=precision_highest) / row_sum
            return jnp.transpose(attn_mix, (2, 0, 1, 3))
        starts = jnp.arange(sequence_length // query_span, dtype=jnp.int32) * query_span
        attended = lax.map(jax.checkpoint(attend), starts).reshape(sequence_length, sequence_count, count_of_heads * VALUE_WIDTH)
        attended = reduced_precision(reduced_backward(attended))
        branch = reduced_backward(jnp.einsum('lsc,cd->lsd', attended, out_w, precision=precision_highest))
        residual = inputs + branch
        normed_ffn = reduced_precision(normed(residual, gain_ffn))
        logits = reduced_backward(jnp.einsum('lsd,de->lse', normed_ffn, router_w, precision=precision_highest))
        chosen = jnp.einsum('lse,lske->lsk', logits, route_pick, precision=precision_highest)
        gate_prob = jax.nn.softmax(chosen, axis=-1)
        gate_up = reduced_backward(jnp.einsum('lsd,dgf->lsgf', normed_ffn, shin_w, precision=precision_highest))
        shared_activation = reduced_precision(silu_gate(gate_up))
        shared_expert_branch = reduced_backward(jnp.einsum('pri,ic->prc', shared_activation, shared_output_weight, precision=precision_highest))
        normed_flat = normed_ffn.reshape(tokens, model_width)
        gate_flat = gate_prob.reshape(-1)

        def expert_step(routed_sum, expert):
            member = flat_routes == expert
            slot_rank = jnp.cumsum(member.astype(jnp.int32)) - 1
            slot_place = jnp.where(member, slot_rank, slot_count)
            slot_source = jnp.zeros((slot_count,), jnp.int32).at[slot_place].set(jnp.arange(tokens * TOP, dtype=jnp.int32), mode='drop')
            filled = jnp.arange(slot_count, dtype=jnp.int32) < jnp.sum(member.astype(jnp.int32))
            slot_token = slot_source // TOP
            weight = jnp.where(filled, gate_flat[slot_source], 0.0)
            row_values = normed_flat[slot_token]
            hidden = reduced_backward(jnp.einsum('rd,dgf->rgf', row_values, ein_w[expert], precision=precision_highest))
            activation = reduced_precision(silu_gate(hidden))
            result = reduced_backward(jnp.einsum('rf,fd->rd', activation, eout_w[expert], precision=precision_highest))
            return (routed_sum.at[slot_token].add(weight[:, None] * result), None)
        routed, unused = lax.scan(jax.checkpoint(expert_step), jnp.zeros((tokens, model_width), jnp.float32), jnp.arange(experts, dtype=jnp.int32))
        output = reduced_precision(residual + shared_expert_branch + routed.reshape(sequence_length, sequence_count, model_width))
        difference = output - target
        loss_value = jnp.sum(valid_f * lax.optimization_barrier(jnp.sum(difference * difference, axis=-1))) / (model_width * valid_count)
        return (loss_value * (tokens * model_width / 2.0), (output, loss_value))
    inputs = states.astype(jnp.float32)
    objective, pullback, (output, loss_value) = jax.vjp(layer_forward, inputs, params, has_aux=True)
    grad_inputs, grad_params = pullback(jnp.ones_like(objective))
    return (output.astype(jnp.bfloat16), loss_value, grad_inputs, grad_params[0], grad_params[1], grad_params[2], grad_params[3], grad_params[4], grad_params[5], grad_params[6], grad_params[7], grad_params[8], grad_params[9], grad_params[10], grad_params[11])
```

```python
import functools

import jax
import jax.numpy as jnp
from jax import lax
from jax.experimental import pallas as pl
from jax.experimental.pallas import tpu as pltpu
from jax.sharding import PartitionSpec as P

NOPE = 128
ROPE = 64
VALUE = 128
RANK = 512
BLOCK = 256
EPS = 1e-06
F32 = jnp.float32
BF16 = jnp.bfloat16
BOTH = ("blk", "head")


def angles(position):
    frequency = 10000.0 ** (-2.0 * jnp.arange(ROPE // 2, dtype=F32) / ROPE)
    return position.astype(F32)[:, None] * frequency[None, :]


def rotate(values, table):
    half = ROPE // 2
    cosine, sine = jnp.cos(table), jnp.sin(table)
    first, second = values[:, :half], values[:, half:]
    return jnp.concatenate([first * cosine - second * sine, second * cosine + first * sine], axis=1)


def normed(values, gain):
    rstd = lax.rsqrt(jnp.mean(values * values, axis=-1, keepdims=True) + EPS)
    return values * rstd * gain, rstd


def norm_back(grad, values, rstd, gain):
    scaled = grad * gain
    out = rstd * scaled - values * rstd**3 * jnp.mean(scaled * values, axis=-1, keepdims=True)
    return out, jnp.sum(grad * values * rstd, axis=0)


def dot(a, b):
    return jnp.dot(a, b, preferred_element_type=F32)


def dot_nt(a, b):
    return lax.dot_general(a, b, (((1,), (1,)), ((), ())), preferred_element_type=F32)


def dot_tn(a, b):
    return lax.dot_general(a, b, (((0,), (0,)), ((), ())), preferred_element_type=F32)


def blk_dims(n_blk):
    if n_blk == 8:
        return [("blk", 2, 4), ("blk", 1, 2)]
    if n_blk == 32:
        return [("blk", 8, 4), ("blk", 2, 4), ("blk", 1, 2)]
    return [("blk", 1, n_blk)]


def head_dims(n_head):
    return [("head", 2, n_head // 2), ("head", 1, 2)] if n_head % 2 == 0 else [("head", 1, n_head)]


def shift(x, dim, by):
    axis, stride, size = dim
    pairs = []
    for i in range(lax.axis_size(axis)):
        digit = i // stride % size
        pairs.append((i, i + ((digit + by) % size - digit) * stride))
    return lax.ppermute(x, axis, pairs)


def digit_of(dim):
    axis, stride, size = dim
    return lax.axis_index(axis) // stride % size


def ring_gather(x, dim):
    pieces = [x]
    for _ in range(dim[2] - 1):
        pieces.append(shift(pieces[-1], dim, -1))
    return pieces


def ring_scatter(pieces, dim):
    total = pieces[-1]
    for piece in pieces[-2::-1]:
        total = shift(total, dim, 1) + piece
    return total


def gather_dims(x, dims):
    for dim in dims:
        x = jnp.concatenate(ring_gather(x, dim), axis=0)
    return x


def scatter_dims(x, dims):
    for dim in reversed(dims):
        x = ring_scatter(jnp.split(x, dim[2], axis=0), dim)
    return x


def relative(dims, index):
    place, scale = 0, 1
    for dim in dims:
        place = place + (index // dim[1] % dim[2] - digit_of(dim)) % dim[2] * scale
        scale *= dim[2]
    return place


def absolute(dims, place):
    index = 0
    for dim in dims:
        index = index + (place % dim[2] + digit_of(dim)) % dim[2] * dim[1]
        place //= dim[2]
    return index


def gather_axis(x, dims):
    n = lax.axis_size(dims[0][0])
    stack = gather_dims(x[None], dims)
    return jnp.concatenate(
        [lax.dynamic_slice_in_dim(stack, relative(dims, i), 1, 0) for i in range(n)], axis=0
    )


def scatter_axis(x, dims):
    n = lax.axis_size(dims[0][0])
    stack = jnp.concatenate(
        [lax.dynamic_slice_in_dim(x, absolute(dims, i), 1, 0) for i in range(n)], axis=0
    )
    return scatter_dims(stack, dims)[0]


def gather_parts(x, n_blk, n_head):
    third = x.shape[0] * 5 // 16
    first = x.shape[0] - 2 * third
    blk, head = blk_dims(n_blk), head_dims(n_head)
    z, inner, y, core = blk[0], blk[1:], head[:-1], head[-1:]
    pieces = ring_gather(x[first:], z)
    b = gather_dims(jnp.concatenate([p[:third] for p in pieces], axis=0), y + inner + core)
    c = gather_dims(jnp.concatenate([p[third:] for p in pieces], axis=0), inner + y + core)
    a = gather_dims(x[:first], inner + y + [z] + core)
    return [b, c, a]


def scatter_parts(parts, n_blk, n_head):
    b, c, a = parts
    blk, head = blk_dims(n_blk), head_dims(n_head)
    z, inner, y, core = blk[0], blk[1:], head[:-1], head[-1:]
    b = scatter_dims(b, y + inner + core)
    c = scatter_dims(c, inner + y + core)
    a = scatter_dims(a, inner + y + [z] + core)
    pieces = [
        jnp.concatenate(both, axis=0)
        for both in zip(jnp.split(b, z[2], axis=0), jnp.split(c, z[2], axis=0))
    ]
    return jnp.concatenate([a, ring_scatter(pieces, z)], axis=0)


def gather_all(x):
    return lax.all_gather(x, BOTH, axis=0, tiled=True)


def scatter_all(x):
    return lax.psum_scatter(x, BOTH, scatter_dimension=0, tiled=True)


def gather_blk(x, axis=0):
    return lax.all_gather(x, "blk", axis=axis, tiled=True)


def scatter_blk(x, axis=0):
    return lax.psum_scatter(x, "blk", scatter_dimension=axis, tiled=True)


def head_lanes(heads, head):
    lane = lax.broadcasted_iota(jnp.int32, (1, heads * ROPE), 1) % (heads * ROPE // 2)
    return lane // (ROPE // 2) == head


def spread(heads):
    row = lax.broadcasted_iota(jnp.int32, (ROPE, heads * ROPE), 0)
    lane = lax.broadcasted_iota(jnp.int32, (ROPE, heads * ROPE), 1)
    width = heads * ROPE // 2
    return jnp.where(row == lane // width * (ROPE // 2) + lane % (ROPE // 2), 1.0, 0.0).astype(BF16)


def attention_kernel(heads, scale, blk_ref, q_ref, lat_ref, up_ref, out_ref, lse_ref, m_ref, l_ref, acc_ref):
    step = pl.program_id(1)

    @pl.when(step == 0)
    def _():
        m_ref[...] = jnp.full_like(m_ref, -1e30)
        l_ref[...] = jnp.zeros_like(l_ref)
        acc_ref[...] = jnp.zeros_like(acc_ref)

    @pl.when(step <= blk_ref[0])
    def _():
        lat = lat_ref[...].reshape(BLOCK, RANK + ROPE)
        kv = dot(lat[:, :RANK], up_ref[...]).astype(BF16)
        rope = dot(lat[:, RANK:], spread(heads)).astype(BF16)
        query = q_ref[...].reshape(BLOCK, heads * (NOPE + ROPE))
        query_rope = query[:, heads * NOPE :]
        for h in range(heads):
            at = h * (NOPE + VALUE)
            scores = dot_nt(query[:, h * NOPE : (h + 1) * NOPE], kv[:, at : at + NOPE])
            masked = jnp.where(head_lanes(heads, h), query_rope, jnp.zeros_like(query_rope))
            scores = (scores + dot_nt(masked, rope)) * scale
            old = m_ref[h][:, :1]
            new = jnp.maximum(old, jnp.max(scores, axis=1, keepdims=True))
            expo = jnp.exp(scores - new)
            factor = jnp.exp(old - new)
            l_ref[h] = l_ref[h] * factor + jnp.sum(expo, axis=1, keepdims=True)
            acc_ref[h] = acc_ref[h] * factor + dot(expo.astype(BF16), kv[:, at + NOPE : at + NOPE + VALUE])
            m_ref[h] = jnp.broadcast_to(new, m_ref.shape[1:])

    @pl.when(step == pl.num_programs(1) - 1)
    def _():
        lane = lax.broadcasted_iota(jnp.int32, (BLOCK, 128), 1)
        lse = jnp.zeros((BLOCK, 128), F32)
        for h in range(heads):
            out = acc_ref[h] / l_ref[h]
            out_ref[:, :, :, h * VALUE : (h + 1) * VALUE] = out.astype(BF16).reshape(
                out_ref.shape[:3] + (VALUE,)
            )
            lse = jnp.where(lane == h, m_ref[h] + jnp.log(l_ref[h]), lse)
        lse_ref[0] = lse


def attention(blk, query, lat, up, heads):
    n_head, seqs, own = query.shape[:3]
    n_blk = lat.shape[0] // n_head
    scale = (NOPE + ROPE) ** -0.5
    row = lambda width: pl.BlockSpec((n_head, 1, own, width), lambda s, b, r: (0, s, 0, 0))
    steps = n_blk * seqs
    return pl.pallas_call(
        functools.partial(attention_kernel, heads, scale),
        grid_spec=pltpu.PrefetchScalarGridSpec(
            num_scalar_prefetch=1,
            grid=(seqs, n_blk),
            in_specs=[
                row(query.shape[3]),
                pl.BlockSpec(
                    (n_head, 1, own, RANK + ROPE), lambda s, b, r: (jnp.minimum(b, r[0]), s, 0, 0)
                ),
                pl.BlockSpec(up.shape, lambda s, b, r: (0, 0)),
            ],
            out_specs=[row(heads * VALUE), pl.BlockSpec((1, BLOCK, 128), lambda s, b, r: (s, 0, 0))],
            scratch_shapes=[
                pltpu.VMEM((heads, BLOCK, 128), F32),
                pltpu.VMEM((heads, BLOCK, 128), F32),
                pltpu.VMEM((heads, BLOCK, VALUE), F32),
            ],
        ),
        out_shape=[
            jax.ShapeDtypeStruct((n_head, seqs, own, heads * VALUE), BF16),
            jax.ShapeDtypeStruct((seqs, BLOCK, 128), F32),
        ],
        cost_estimate=pl.CostEstimate(
            flops=steps * BLOCK * 2 * (RANK * up.shape[1] + heads * BLOCK * 640),
            bytes_accessed=lat.size * 2 + up.size * 2 + query.size * 4,
            transcendentals=steps * heads * BLOCK * BLOCK,
        ),
        name="attention",
    )(blk, query, lat, up)


def attention_back_kernel(
    heads, scale, blk_ref, q_ref, lat_ref, up_ref, att_ref, datt_ref, lse_ref, cos_ref, sin_ref,
    dq_ref, dlat_ref, dup_ref, delta_ref, dqn_ref, dqr_ref, up_acc,
):
    seq, step = pl.program_id(0), pl.program_id(1)
    last = pl.num_programs(1) - 1

    @pl.when((seq == 0) & (step == 0))
    def _():
        up_acc[...] = jnp.zeros_like(up_acc)

    @pl.when(step == 0)
    def _():
        dqn_ref[...] = jnp.zeros_like(dqn_ref)
        dqr_ref[...] = jnp.zeros_like(dqr_ref)
        prod = att_ref[...].astype(F32) * datt_ref[...].astype(F32)
        prod = prod.reshape(BLOCK, heads * VALUE)
        for h in range(heads):
            delta_ref[h] = jnp.broadcast_to(
                jnp.sum(prod[:, h * VALUE : (h + 1) * VALUE], axis=1, keepdims=True), (BLOCK, 128)
            )

    @pl.when(step <= blk_ref[0])
    def _():
        lat = lat_ref[...].reshape(BLOCK, RANK + ROPE)
        latn = lat[:, :RANK]
        kv = dot(latn, up_ref[...]).astype(BF16)
        copies = spread(heads)
        rope = dot(lat[:, RANK:], copies).astype(BF16)
        query = q_ref[...].reshape(BLOCK, heads * (NOPE + ROPE))
        query_rope = query[:, heads * NOPE :]
        d_att = datt_ref[...].reshape(BLOCK, heads * VALUE)
        d_rope = jnp.zeros((BLOCK, heads * ROPE), F32)
        d_kv = []
        for h in range(heads):
            at = h * (NOPE + VALUE)
            lanes = head_lanes(heads, h)
            q_h = query[:, h * NOPE : (h + 1) * NOPE]
            k_h = kv[:, at : at + NOPE]
            d_h = d_att[:, h * VALUE : (h + 1) * VALUE]
            masked = jnp.where(lanes, query_rope, jnp.zeros_like(query_rope))
            scores = (dot_nt(q_h, k_h) + dot_nt(masked, rope)) * scale
            prob = jnp.exp(scores - lse_ref[0][:, h : h + 1])
            d_prob = dot_nt(d_h, kv[:, at + NOPE : at + NOPE + VALUE])
            d_score = (prob * (d_prob - delta_ref[h][:, :1]) * scale).astype(BF16)
            dqn_ref[h] = dqn_ref[h] + dot(d_score, k_h)
            dqr_ref[...] = dqr_ref[...] + jnp.where(lanes, dot(d_score, rope), 0.0)
            d_kv.append(dot_tn(d_score, q_h))
            d_kv.append(dot_tn(prob.astype(BF16), d_h))
            d_rope = d_rope + dot_tn(d_score, masked)
        d_kv = jnp.concatenate(d_kv, axis=1).astype(BF16)
        up_acc[...] += dot_tn(latn, d_kv)
        shape = dlat_ref.shape[:3]
        dlat_ref[:, :, :, :RANK] = dot_nt(d_kv, up_ref[...]).astype(BF16).reshape(shape + (RANK,))
        dlat_ref[:, :, :, RANK:] = (
            dot_nt(d_rope.astype(BF16), copies).astype(BF16).reshape(shape + (ROPE,))
        )

    @pl.when(step > blk_ref[0])
    def _():
        dlat_ref[...] = jnp.zeros_like(dlat_ref)

    @pl.when(step == last)
    def _():
        shape = dq_ref.shape[:3]
        for h in range(heads):
            dq_ref[:, :, :, h * NOPE : (h + 1) * NOPE] = dqn_ref[h].astype(BF16).reshape(shape + (NOPE,))
        half = heads * ROPE // 2
        cosine, sine = cos_ref[...], sin_ref[...]
        first, second = dqr_ref[:, :half], dqr_ref[:, half:]
        at = heads * NOPE
        dq_ref[:, :, :, at : at + half] = (first * cosine + second * sine).astype(BF16).reshape(shape + (half,))
        dq_ref[:, :, :, at + half :] = (second * cosine - first * sine).astype(BF16).reshape(shape + (half,))

    @pl.when((seq == pl.num_programs(0) - 1) & (step == last))
    def _():
        dup_ref[...] = up_acc[...].astype(BF16)


def attention_back(blk, query, lat, up, att, d_att, lse, cosine, sine, heads):
    n_head, seqs, own = query.shape[:3]
    n_blk = lat.shape[0] // n_head
    scale = (NOPE + ROPE) ** -0.5
    row = lambda width: pl.BlockSpec((n_head, 1, own, width), lambda s, b, r: (0, s, 0, 0))
    whole = lambda x: pl.BlockSpec(x.shape, lambda s, b, r: (0, 0))
    half = heads * ROPE // 2
    steps = n_blk * seqs
    return pl.pallas_call(
        functools.partial(attention_back_kernel, heads, scale),
        grid_spec=pltpu.PrefetchScalarGridSpec(
            num_scalar_prefetch=1,
            grid=(seqs, n_blk),
            in_specs=[
                row(query.shape[3]),
                pl.BlockSpec(
                    (n_head, 1, own, RANK + ROPE), lambda s, b, r: (jnp.minimum(b, r[0]), s, 0, 0)
                ),
                whole(up),
                row(heads * VALUE),
                row(heads * VALUE),
                pl.BlockSpec((1, BLOCK, 128), lambda s, b, r: (s, 0, 0)),
                whole(cosine),
                whole(sine),
            ],
            out_specs=[
                row(query.shape[3]),
                pl.BlockSpec((n_head, 1, own, RANK + ROPE), lambda s, b, r: (b, s, 0, 0)),
                whole(up),
            ],
            scratch_shapes=[
                pltpu.VMEM((heads, BLOCK, 128), F32),
                pltpu.VMEM((heads, BLOCK, NOPE), F32),
                pltpu.VMEM((BLOCK, 2 * half), F32),
                pltpu.VMEM(up.shape, F32),
            ],
        ),
        out_shape=[
            jax.ShapeDtypeStruct(query.shape, BF16),
            jax.ShapeDtypeStruct(lat.shape, BF16),
            jax.ShapeDtypeStruct(up.shape, BF16),
        ],
        cost_estimate=pl.CostEstimate(
            flops=steps * BLOCK * 2 * (3 * RANK * up.shape[1] + heads * BLOCK * 1700),
            bytes_accessed=lat.size * 4 + up.size * 4 + query.size * 8,
            transcendentals=steps * heads * BLOCK * BLOCK,
        ),
        name="attention_back",
    )(blk, query, lat, up, att, d_att, lse, cosine, sine)


def expert_gates(tail, base, local):
    lane = lax.broadcasted_iota(jnp.int32, tail.shape, 1)
    return [
        jnp.sum(jnp.where(lane == base + e, tail, 0.0), axis=1, keepdims=True) for e in range(local)
    ]


def gate_of(gates, eff, chunk):
    unit = lax.broadcasted_iota(jnp.int32, (1, 128), 1) + chunk * 128
    factor = jnp.where(unit < len(gates) * eff, gates[-1], 1.0)
    for e in range(len(gates) - 2, -1, -1):
        factor = jnp.where(unit < (e + 1) * eff, gates[e], factor)
    return factor


def experts_kernel(eff, local, base_ref, x_ref, tail_ref, win_ref, wout_ref, gu_ref, out_ref, act_ref):
    gates = expert_gates(tail_ref[...].astype(F32), base_ref[0], local)

    def step(chunk, carry):
        at = pl.multiple_of(chunk * 256, 256)
        both = dot(x_ref[...], win_ref[:, pl.ds(at, 256)])
        gu_ref[:, pl.ds(at, 256)] = both.astype(BF16)
        gate, up = both[:, :128], both[:, 128:]
        act = gate * jax.nn.sigmoid(gate) * up * gate_of(gates, eff, chunk)
        act_ref[:, pl.ds(pl.multiple_of(chunk * 128, 128), 128)] = act.astype(BF16)
        return carry

    lax.fori_loop(0, win_ref.shape[1] // 256, step, 0)

    def last(chunk, carry):
        at = pl.ds(pl.multiple_of(chunk * 512, 512), 512)
        out_ref[:, at] = dot(act_ref[...], wout_ref[:, at]).astype(BF16)
        return carry

    lax.fori_loop(0, out_ref.shape[1] // 512, last, 0)


def tile_of(rows):
    return max(t for t in range(16, 769, 16) if rows % t == 0)


def run_experts(base, rows_ext, win, wout, eff, local):
    rows, width, padded = rows_ext.shape[0], wout.shape[1], wout.shape[0]
    tile = tile_of(rows)
    whole = lambda x: pl.BlockSpec(x.shape, lambda i, r: (0, 0), pipeline_mode=pl.Buffered(1))
    return pl.pallas_call(
        functools.partial(experts_kernel, eff, local),
        grid_spec=pltpu.PrefetchScalarGridSpec(
            num_scalar_prefetch=1,
            grid=(rows // tile,),
            in_specs=[
                pl.BlockSpec((tile, width), lambda i, r: (i, 0)),
                pl.BlockSpec((tile, 128), lambda i, r: (i, width // 128)),
                whole(win),
                whole(wout),
            ],
            out_specs=[
                pl.BlockSpec((tile, 2 * padded), lambda i, r: (i, 0)),
                pl.BlockSpec((tile, width), lambda i, r: (i, 0)),
            ],
            scratch_shapes=[pltpu.VMEM((tile, padded), BF16)],
        ),
        out_shape=[
            jax.ShapeDtypeStruct((rows, 2 * padded), BF16),
            jax.ShapeDtypeStruct((rows, width), BF16),
        ],
        cost_estimate=pl.CostEstimate(
            flops=rows * width * padded * 6,
            bytes_accessed=(rows * (2 * width + 2 * padded) + 3 * width * padded) * 2,
            transcendentals=rows * padded,
        ),
        name="experts",
    )(base, rows_ext, rows_ext, win, wout)


def experts_back_kernel(
    eff, local, base_ref, grad_ref, tail_ref, gu_ref, win_ref, wout_ref, hid_ref, act_ref, out_ref, dact_ref
):
    gates = expert_gates(tail_ref[...].astype(F32), base_ref[0], local)
    padded = wout_ref.shape[0]
    for at in range(0, padded, 256):
        size = min(256, padded - at)
        dact_ref[:, at : at + size] = dot_nt(grad_ref[...], wout_ref[at : at + size, :])

    def step(chunk, sums):
        both = gu_ref[:, pl.ds(pl.multiple_of(chunk * 256, 256), 256)].astype(F32)
        gate, up = both[:, :128], both[:, 128:]
        here = pl.ds(pl.multiple_of(chunk * 128, 128), 128)
        d_act = dact_ref[:, here]
        sig = jax.nn.sigmoid(gate)
        silu = gate * sig
        act = silu * up
        factor = gate_of(gates, eff, chunk)
        prod = act * d_act
        unit = lax.broadcasted_iota(jnp.int32, (1, 128), 1) + chunk * 128
        sums = tuple(
            s + jnp.sum(jnp.where((unit >= e * eff) & (unit < (e + 1) * eff), prod, 0.0), axis=1, keepdims=True)
            for e, s in enumerate(sums)
        )
        d_act = d_act * factor
        d_gate = d_act * up * sig * (1.0 + gate * (1.0 - sig))
        hid_ref[:, pl.ds(pl.multiple_of(chunk * 256, 256), 128)] = d_gate.astype(BF16)
        hid_ref[:, pl.ds(pl.multiple_of(chunk * 256 + 128, 128), 128)] = (d_act * silu).astype(BF16)
        act_ref[:, here] = (act * factor).astype(BF16)
        return sums

    zero = jnp.zeros((gu_ref.shape[0], 1), F32)
    sums = lax.fori_loop(0, padded // 128, step, (zero,) * local)
    width = wout_ref.shape[1]

    def last(chunk, carry):
        at = pl.multiple_of(chunk * 256, 256)
        out_ref[:, pl.ds(at, 256)] = dot_nt(hid_ref[...], win_ref[pl.ds(at, 256), :]).astype(BF16)
        return carry

    lax.fori_loop(0, width // 256, last, 0)
    lane = lax.broadcasted_iota(jnp.int32, tail_ref.shape, 1)
    extra = jnp.zeros(tail_ref.shape, F32)
    for e in range(local):
        extra = jnp.where(lane == base_ref[0] + e, sums[e], extra)
    out_ref[:, width:] = extra.astype(BF16)


def run_experts_back(base, grad, rows_ext, gu, win, wout, eff, local):
    rows, width, padded = grad.shape[0], wout.shape[1], wout.shape[0]
    tile = tile_of(rows)
    whole = lambda x: pl.BlockSpec(x.shape, lambda i, r: (0, 0), pipeline_mode=pl.Buffered(1))
    row = lambda size: pl.BlockSpec((tile, size), lambda i, r: (i, 0))
    return pl.pallas_call(
        functools.partial(experts_back_kernel, eff, local),
        grid_spec=pltpu.PrefetchScalarGridSpec(
            num_scalar_prefetch=1,
            grid=(rows // tile,),
            in_specs=[
                row(width),
                pl.BlockSpec((tile, 128), lambda i, r: (i, width // 128)),
                row(2 * padded),
                whole(win),
                whole(wout),
            ],
            out_specs=[row(2 * padded), row(padded), row(width + 128)],
            scratch_shapes=[pltpu.VMEM((tile, padded), F32)],
        ),
        out_shape=[
            jax.ShapeDtypeStruct((rows, 2 * padded), BF16),
            jax.ShapeDtypeStruct((rows, padded), BF16),
            jax.ShapeDtypeStruct((rows, width + 128), BF16),
        ],
        input_output_aliases={3: 0},
        cost_estimate=pl.CostEstimate(
            flops=rows * width * padded * 6,
            bytes_accessed=(rows * (2 * width + 5 * padded) + 3 * width * padded) * 2,
            transcendentals=rows * padded,
        ),
        name="experts_back",
    )(base, grad, rows_ext, gu, win, wout)


def on_device(
    states, teacher, valid, routes, norm_in, w_query, w_down_kv, norm_kv, w_up_kv, w_out, norm_ffn,
    w_router, shared_in, shared_out, expert_in, expert_out,
):
    n_blk, n_head = lax.axis_size("blk"), lax.axis_size("head")
    blk, head = lax.axis_index("blk"), lax.axis_index("head")
    own_pos, seqs, width = states.shape
    block_pos = own_pos * n_head
    rows = own_pos * seqs
    block_rows = rows * n_head
    total_rows = block_rows * n_blk
    experts = w_router.shape[1]
    local = expert_in.shape[0]
    eff = expert_in.shape[3]
    shared = shared_in.shape[2] // n_blk
    heads = w_query.shape[1] // (NOPE + ROPE)
    scale = (NOPE + ROPE) ** (-0.5)
    assert block_pos == BLOCK
    blks, heads_ring = blk_dims(n_blk), head_dims(n_head)

    def gather_head(x):
        return gather_axis(x, heads_ring).reshape((-1,) + x.shape[1:])

    def scatter_head(x):
        return scatter_axis(x.reshape((n_head, -1) + x.shape[1:]), heads_ring)

    def take_own(x):
        own = lax.dynamic_slice_in_dim(x, head * own_pos, own_pos, 0)
        return jnp.moveaxis(own, 1, 0).reshape((rows,) + x.shape[2:])

    small = jnp.concatenate(
        [norm_in, norm_ffn, w_router.reshape(-1), norm_kv, jnp.sum(valid, axis=1).astype(BF16)]
    )
    small = gather_axis(small, blks)
    part = width // n_blk
    gain_in = small[:, :part].reshape(-1).astype(F32)
    gain_ffn = small[:, part : 2 * part].reshape(-1).astype(F32)
    at = 2 * part
    router = small[:, at : at + part * experts].reshape(width, experts)
    at += part * experts
    gain_kv = small[:, at : at + RANK // n_blk].reshape(-1).astype(F32)
    at += RANK // n_blk
    count = jnp.sum(small[:, at:].astype(F32))

    pieces = jnp.concatenate(
        [
            jnp.transpose(shared_in.reshape(part, 2, n_blk, shared), (2, 1, 3, 0)).reshape(
                n_blk, 2 * shared, part
            ),
            shared_out.reshape(n_blk, shared, part),
        ],
        axis=1,
    )
    pieces = lax.all_to_all(pieces, "blk", split_axis=0, concat_axis=0, tiled=True)
    sh_in = jnp.transpose(pieces[:, : 2 * shared], (0, 2, 1)).reshape(width, 2, shared)
    sh_out = jnp.transpose(pieces[:, 2 * shared :], (1, 0, 2)).reshape(shared, width)
    hidden = local * eff + shared
    padded = -(-hidden // 128) * 128
    pad_in = jnp.zeros((width, padded - hidden), BF16)
    win = jnp.stack(
        [
            jnp.concatenate(
                [expert_in[e, :, side] for e in range(local)] + [sh_in[:, side], pad_in], axis=1
            ).reshape(width, padded // 128, 128)
            for side in range(2)
        ],
        axis=2,
    ).reshape(width, 2 * padded)
    wout = jnp.concatenate(
        [expert_out.reshape(local * eff, width), sh_out, jnp.zeros((padded - hidden, width), BF16)],
        axis=0,
    )

    lanes = heads * ROPE // 2
    quarter = part // n_head
    down = gather_axis(lax.dynamic_slice_in_dim(w_down_kv, head * quarter, quarter, 0), blks)
    down = jnp.moveaxis(gather_axis(down, heads_ring), 0, 1).reshape(width, RANK + ROPE)
    wq = w_query.reshape(part, heads, NOPE + ROPE)
    wq = jnp.concatenate(
        [
            wq[:, :, :NOPE].reshape(part, -1),
            wq[:, :, NOPE : NOPE + ROPE // 2].reshape(part, -1),
            wq[:, :, NOPE + ROPE // 2 :].reshape(part, -1),
        ],
        axis=1,
    )
    most = part * 3 // 4
    wq = jnp.concatenate(
        [gather_axis(wq[:most], blks), gather_axis(wq[most:], blks[::-1])], axis=1
    ).reshape(width, -1)
    wup = gather_blk(w_up_kv)
    wo = gather_blk(w_out, 1)

    x_own = jnp.moveaxis(states, 1, 0).reshape(rows, width).astype(F32)
    h1_f, rstd_in = normed(x_own, gain_in)
    h1_own = h1_f.astype(BF16)
    h1_blk = gather_head(h1_own)
    pos_own = blk * block_pos + head * own_pos + jnp.arange(own_pos, dtype=jnp.int32)
    table_own = jnp.tile(angles(pos_own), (seqs, 1))
    pos_blk = blk * block_pos + jnp.arange(block_pos, dtype=jnp.int32)
    table_seq = angles(pos_blk)
    cos_seq, sin_seq = (jnp.tile(f(table_seq), (1, heads)) for f in (jnp.cos, jnp.sin))
    table_blk = jnp.broadcast_to(
        angles(pos_blk).reshape(n_head, 1, own_pos, ROPE // 2), (n_head, seqs, own_pos, ROPE // 2)
    ).reshape(block_rows, ROPE // 2)
    lat = dot(h1_own, down)
    lat_c = lat[:, :RANK]
    latn_f, rstd_kv = normed(lat_c, gain_kv)
    payload = jnp.concatenate([latn_f, rotate(lat[:, RANK:], table_own)], axis=1).astype(BF16)
    lat_all = gather_all(payload)
    query = dot(h1_blk, wq)
    cosine = jnp.tile(jnp.cos(table_blk), (1, heads))
    sine = jnp.tile(jnp.sin(table_blk), (1, heads))
    q_first, q_second = query[:, -2 * lanes : -lanes], query[:, -lanes:]
    query = jnp.concatenate(
        [query[:, : -2 * lanes], q_first * cosine - q_second * sine, q_second * cosine + q_first * sine],
        axis=1,
    ).astype(BF16)
    shape4 = (n_head, seqs, own_pos, -1)
    query = query.reshape(shape4)
    lat_all = lat_all.reshape(n_blk * n_head, seqs, own_pos, -1)
    blk_index = jnp.full((1,), blk, jnp.int32)
    att_b, lse = attention(blk_index, query, lat_all, wup, heads)
    att_rows = att_b.reshape(block_rows, heads * VALUE)
    y_own = x_own + scatter_head(dot(att_rows, wo).astype(BF16)).astype(F32)
    h2_f, rstd_ffn = normed(y_own, gain_ffn)
    h2_own = h2_f.astype(BF16)

    routes_own = take_own(routes)
    mask = jnp.any(routes_own[:, :, None] == jnp.arange(experts, dtype=jnp.int32), axis=1)
    logits = jnp.where(mask, dot(h2_own, router), -1e30)
    gates = jnp.where(mask, jnp.exp(logits - jnp.max(logits, axis=1, keepdims=True)), 0.0)
    gates = gates / jnp.sum(gates, axis=1, keepdims=True)
    assert experts <= 128
    tail = jnp.zeros((rows, 128 - experts), BF16)
    base = jnp.full((1,), blk * local, jnp.int32)
    x_ext = jnp.concatenate([h2_own, gates.astype(BF16), tail], axis=1)
    rounds = max(1, total_rows // 4096)

    def forward(x_rows):
        parts = gather_parts(x_rows, n_blk, n_head)
        both = [run_experts(base, part, win, wout, eff, local) for part in parts]
        return parts, [gu for gu, _ in both], [result for _, result in both]

    def backward(grad_rows, parts, hidden_parts):
        grad_parts = gather_parts(grad_rows, n_blk, n_head)
        d_win = d_wout = 0.0
        results = []
        for grad_part, part, gu in zip(grad_parts, parts, hidden_parts):
            d_hidden, act, result = run_experts_back(base, grad_part, part, gu, win, wout, eff, local)
            results.append(result)
            d_win = d_win + dot_tn(part[:, :width], d_hidden)
            d_wout = d_wout + dot_tn(act, grad_part)
        return scatter_parts(results, n_blk, n_head), d_win, d_wout

    def in_rounds(x):
        return x.reshape((rounds, -1) + x.shape[1:])

    if rounds == 1:
        parts, hidden_parts, results = forward(x_ext)
        mixed = scatter_parts(results, n_blk, n_head)
    else:
        mixed = lax.map(lambda x: scatter_parts(forward(x)[2], n_blk, n_head), in_rounds(x_ext))
        mixed = mixed.reshape(rows, width)
    mixed = mixed.astype(F32)
    out_own = (y_own + mixed).astype(BF16)
    diff = out_own.astype(F32) - take_own(teacher).astype(F32)
    valid_own = take_own(valid).astype(F32)[:, None]
    loss_part = jnp.sum(valid_own * diff * diff)
    grad_own = diff * valid_own * (total_rows / count)

    grad_own_b = grad_own.astype(BF16)
    if rounds == 1:
        back, d_win, d_wout = backward(grad_own_b, parts, hidden_parts)
    else:

        def round_back(sums, both):
            parts, hidden_parts, _ = forward(both[0])
            back, d_win, d_wout = backward(both[1], parts, hidden_parts)
            return (sums[0] + d_win, sums[1] + d_wout), back

        start = (jnp.zeros((width, 2 * padded), F32), jnp.zeros((padded, width), F32))
        (d_win, d_wout), back = lax.scan(round_back, start, (in_rounds(x_ext), in_rounds(grad_own_b)))
        back = back.reshape(rows, -1)
    back = back.astype(F32)
    d_win = jnp.moveaxis(d_win.reshape(width, padded // 128, 2, 128), 2, 1).reshape(width, 2 * padded)
    grad_ein = jnp.stack(
        [
            jnp.stack([d_win[:, s * padded + e * eff : s * padded + (e + 1) * eff] for s in range(2)], axis=1)
            for e in range(local)
        ]
    )
    grad_eout = d_wout[: local * eff].reshape(local, eff, width)
    d_sh = jnp.concatenate(
        [d_win[:, s * padded + local * eff : s * padded + hidden].T for s in range(2)]
        + [d_wout[local * eff : hidden]],
        axis=0,
    ).astype(BF16)
    d_sh = jnp.transpose(d_sh.reshape(3 * shared, n_blk, part), (1, 0, 2))
    d_sh = lax.all_to_all(d_sh, "blk", split_axis=0, concat_axis=0, tiled=True).astype(F32)
    grad_shin = jnp.transpose(d_sh[:, : 2 * shared].reshape(n_blk, 2, shared, part), (3, 1, 0, 2)).reshape(
        part, 2, n_blk * shared
    )
    grad_shout = d_sh[:, 2 * shared :].reshape(n_blk * shared, part)

    d_gates = back[:, width : width + experts]
    d_logits = gates * (d_gates - jnp.sum(gates * d_gates, axis=1, keepdims=True))
    d_logits = d_logits.astype(BF16)
    grad_router = dot_tn(h2_own, d_logits)
    dh2 = back[:, :width] + dot_nt(d_logits, router)
    dy_branch, grad_gain_ffn = norm_back(dh2, y_own, rstd_ffn, gain_ffn)
    dy_own = grad_own + dy_branch

    dy_blk = gather_head(dy_own.astype(BF16))
    grad_wo = scatter_blk(dot_tn(att_rows, dy_blk).astype(BF16), 1).astype(F32)
    d_att = dot_nt(dy_blk, wo).astype(BF16).reshape(shape4)
    dq, d_lat, d_up = attention_back(
        blk_index, query, lat_all, wup, att_b, d_att, lse, cos_seq, sin_seq, heads
    )
    d_lat = scatter_all(d_lat.reshape(total_rows, -1)).astype(F32)
    dq = dq.reshape(block_rows, -1)
    dh1 = scatter_head(dot_nt(dq, wq).astype(BF16)).astype(F32)
    grad_wq = dot_tn(h1_blk, dq).astype(BF16).reshape(n_blk, part, -1)
    grad_wq = jnp.concatenate(
        [scatter_axis(grad_wq[:, :most], blks), scatter_axis(grad_wq[:, most:], blks[::-1])], axis=0
    ).astype(F32)
    grad_wq = jnp.concatenate(
        [
            grad_wq[:, : heads * NOPE].reshape(part, heads, NOPE),
            grad_wq[:, heads * NOPE : -lanes].reshape(part, heads, ROPE // 2),
            grad_wq[:, -lanes:].reshape(part, heads, ROPE // 2),
        ],
        axis=2,
    ).reshape(part, -1)
    grad_up = scatter_blk(d_up).astype(F32)
    d_lat_c, grad_gain_kv = norm_back(d_lat[:, :RANK], lat_c, rstd_kv, gain_kv)
    d_lat_b = jnp.concatenate([d_lat_c, rotate(d_lat[:, RANK:], -table_own)], axis=1).astype(BF16)
    d_lat_blk = gather_head(d_lat_b)
    h1_part = lax.dynamic_slice_in_dim(
        h1_blk.reshape(block_rows, n_blk, n_head, quarter), head, 1, 2
    ).reshape(block_rows, -1)
    grad_down = dot_tn(h1_part, d_lat_blk).astype(BF16).reshape(n_blk, quarter, -1)
    grad_down = gather_head(scatter_axis(grad_down, blks)).astype(F32)
    dh1 = dh1 + dot_nt(d_lat_b, down)
    dx_branch, grad_gain_in = norm_back(dh1, x_own, rstd_in, gain_in)
    dx_own = dy_own + dx_branch

    loss_high = loss_part.astype(BF16).astype(F32)
    sums = jnp.concatenate(
        [
            grad_gain_in.reshape(n_blk, -1),
            grad_gain_ffn.reshape(n_blk, -1),
            grad_router.reshape(n_blk, -1),
            grad_gain_kv.reshape(n_blk, -1),
            jnp.full((n_blk, 1), loss_high),
            jnp.full((n_blk, 1), loss_part - loss_high),
        ],
        axis=1,
    )
    sums = scatter_axis(sums, blks)
    for dim in heads_ring:
        sums = sum(ring_gather(sums, dim))
    out_gain_in = sums[:part]
    out_gain_ffn = sums[part : 2 * part]
    at = 2 * part
    out_router = sums[at : at + part * experts].reshape(part, experts)
    at += part * experts
    out_gain_kv = sums[at : at + RANK // n_blk]
    loss = (sums[-2] + sums[-1]) / (width * count)

    def give(x):
        return jnp.moveaxis(x.reshape(seqs, own_pos, width), 0, 1)

    return (
        give(out_own), loss, give(dx_own), out_gain_in, grad_wq, grad_down, out_gain_kv, grad_up,
        grad_wo, out_gain_ffn, out_router, grad_shin, grad_shout, grad_ein, grad_eout,
    )


def solution(mesh):
    in_specs = (
        P(BOTH, None, None), P("blk", None, None), P("blk", None), P("blk", None, None), P("blk"),
        P("blk", "head"), P("blk", None), P("blk"), P("blk", "head"), P("head", "blk"), P("blk"),
        P("blk", None), P("blk", None, "head"), P("head", "blk"), P("blk", None, None, "head"),
        P("blk", "head", None),
    )
    out_specs = (
        P(BOTH, None, None), P(), P(BOTH, None, None), P("blk"), P("blk", "head"), P("blk", None),
        P("blk"), P("blk", "head"), P("head", "blk"), P("blk"), P("blk", None), P("blk", None, "head"),
        P("head", "blk"), P("blk", None, None, "head"), P("blk", "head", None),
    )
    return jax.shard_map(on_device, mesh=mesh, in_specs=in_specs, out_specs=out_specs, check_vma=False)
```

```python
import functools

import jax
import jax.numpy as jnp
from jax import lax
from jax.experimental import pallas as pl
from jax.experimental.pallas import tpu as pltpu
from jax.sharding import PartitionSpec as P

NOPE = 128
ROPE = 64
VALUE = 128
RANK = 512
BLOCK = 256
EPS = 1e-06
F32 = jnp.float32
BF16 = jnp.bfloat16
BOTH = ("blk", "head")


def angles(position):
    frequency = 10000.0 ** (-2.0 * jnp.arange(ROPE // 2, dtype=F32) / ROPE)
    return position.astype(F32)[:, None] * frequency[None, :]


def rotate(values, table):
    half = ROPE // 2
    cosine, sine = jnp.cos(table), jnp.sin(table)
    first, second = values[:, :half], values[:, half:]
    return jnp.concatenate([first * cosine - second * sine, second * cosine + first * sine], axis=1)


def normed(values, gain):
    rstd = lax.rsqrt(jnp.mean(values * values, axis=-1, keepdims=True) + EPS)
    return values * rstd * gain, rstd


def norm_back(grad, values, rstd, gain):
    scaled = grad * gain
    out = rstd * scaled - values * rstd**3 * jnp.mean(scaled * values, axis=-1, keepdims=True)
    return out, jnp.sum(grad * values * rstd, axis=0)


def dot(a, b):
    return jnp.dot(a, b, preferred_element_type=F32)


def dot_nt(a, b):
    return lax.dot_general(a, b, (((1,), (1,)), ((), ())), preferred_element_type=F32)


def dot_tn(a, b):
    return lax.dot_general(a, b, (((0,), (0,)), ((), ())), preferred_element_type=F32)


def blk_dims(n_blk):
    if n_blk == 8:
        return [("blk", 2, 4), ("blk", 1, 2)]
    if n_blk == 32:
        return [("blk", 8, 4), ("blk", 2, 4), ("blk", 1, 2)]
    return [("blk", 1, n_blk)]


def head_dims(n_head):
    return [("head", 2, n_head // 2), ("head", 1, 2)] if n_head % 2 == 0 else [("head", 1, n_head)]


def shift(x, dim, by):
    axis, stride, size = dim
    pairs = []
    for i in range(lax.axis_size(axis)):
        digit = i // stride % size
        pairs.append((i, i + ((digit + by) % size - digit) * stride))
    return lax.ppermute(x, axis, pairs)


def digit_of(dim):
    axis, stride, size = dim
    return lax.axis_index(axis) // stride % size


def ring_gather(x, dim):
    pieces = [x]
    for _ in range(dim[2] - 1):
        pieces.append(shift(pieces[-1], dim, -1))
    return pieces


def ring_scatter(pieces, dim):
    total = pieces[-1]
    for piece in pieces[-2::-1]:
        total = shift(total, dim, 1) + piece
    return total


def gather_dims(x, dims):
    for dim in dims:
        x = jnp.concatenate(ring_gather(x, dim), axis=0)
    return x


def scatter_dims(x, dims):
    for dim in reversed(dims):
        x = ring_scatter(jnp.split(x, dim[2], axis=0), dim)
    return x


def relative(dims, index):
    place, scale = 0, 1
    for dim in dims:
        place = place + (index // dim[1] % dim[2] - digit_of(dim)) % dim[2] * scale
        scale *= dim[2]
    return place


def absolute(dims, place):
    index = 0
    for dim in dims:
        index = index + (place % dim[2] + digit_of(dim)) % dim[2] * dim[1]
        place //= dim[2]
    return index


def gather_axis(x, dims):
    return in_order(gather_dims(x[None], dims), dims)


def in_order(stack, dims):
    n = stack.shape[0]
    return jnp.concatenate(
        [lax.dynamic_slice_in_dim(stack, relative(dims, i), 1, 0) for i in range(n)], axis=0
    )


def scatter_axis(x, dims):
    n = lax.axis_size(dims[0][0])
    stack = jnp.concatenate(
        [lax.dynamic_slice_in_dim(x, absolute(dims, i), 1, 0) for i in range(n)], axis=0
    )
    return scatter_dims(stack, dims)[0]


def gather_parts(x, n_blk, n_head):
    third = x.shape[0] * 5 // 16
    first = x.shape[0] - 2 * third
    blk, head = blk_dims(n_blk), head_dims(n_head)
    z, inner, y, core = blk[0], blk[1:], head[:-1], head[-1]
    pieces = ring_gather(x[first:], z)
    b = gather_dims(jnp.concatenate([p[:third] for p in pieces], axis=0), y + inner)
    c = gather_dims(jnp.concatenate([p[third:] for p in pieces], axis=0), inner + y)
    a = gather_dims(x[:first], inner + y + [z])
    return [ring_gather(part, core) for part in (b, c, a)]


def scatter_parts(pairs, n_blk, n_head):
    blk, head = blk_dims(n_blk), head_dims(n_head)
    z, inner, y, core = blk[0], blk[1:], head[:-1], head[-1]
    b, c, a = (ring_scatter(pair, core) for pair in pairs)
    b = scatter_dims(b, y + inner)
    c = scatter_dims(c, inner + y)
    a = scatter_dims(a, inner + y + [z])
    pieces = [
        jnp.concatenate(both, axis=0)
        for both in zip(jnp.split(b, z[2], axis=0), jnp.split(c, z[2], axis=0))
    ]
    return jnp.concatenate([a, ring_scatter(pieces, z)], axis=0)


def gather_all(x):
    return lax.all_gather(x, BOTH, axis=0, tiled=True)


def scatter_all(x):
    return lax.psum_scatter(x, BOTH, scatter_dimension=0, tiled=True)


def scatter_blk(x, axis=0):
    return lax.psum_scatter(x, "blk", scatter_dimension=axis, tiled=True)


def head_lanes(heads, head):
    lane = lax.broadcasted_iota(jnp.int32, (1, heads * ROPE), 1) % (heads * ROPE // 2)
    return lane // (ROPE // 2) == head


def spread(heads):
    row = lax.broadcasted_iota(jnp.int32, (ROPE, heads * ROPE), 0)
    lane = lax.broadcasted_iota(jnp.int32, (ROPE, heads * ROPE), 1)
    width = heads * ROPE // 2
    return jnp.where(row == lane // width * (ROPE // 2) + lane % (ROPE // 2), 1.0, 0.0).astype(BF16)


def attention_kernel(heads, scale, blk_ref, q_ref, lat_ref, up_ref, out_ref, lse_ref, m_ref, l_ref, acc_ref):
    step = pl.program_id(1)

    @pl.when(step == 0)
    def _():
        m_ref[...] = jnp.full_like(m_ref, -1e30)
        l_ref[...] = jnp.zeros_like(l_ref)
        acc_ref[...] = jnp.zeros_like(acc_ref)

    @pl.when(step <= blk_ref[0])
    def _():
        lat = lat_ref[...].reshape(BLOCK, RANK + ROPE)
        kv = dot(lat[:, :RANK], up_ref[...]).astype(BF16)
        rope = dot(lat[:, RANK:], spread(heads)).astype(BF16)
        query = q_ref[...].reshape(BLOCK, heads * (NOPE + ROPE))
        query_rope = query[:, heads * NOPE :]
        for h in range(heads):
            at = h * (NOPE + VALUE)
            scores = dot_nt(query[:, h * NOPE : (h + 1) * NOPE], kv[:, at : at + NOPE])
            masked = jnp.where(head_lanes(heads, h), query_rope, jnp.zeros_like(query_rope))
            scores = (scores + dot_nt(masked, rope)) * scale
            old = m_ref[h][:, :1]
            new = jnp.maximum(old, jnp.max(scores, axis=1, keepdims=True))
            expo = jnp.exp(scores - new)
            factor = jnp.exp(old - new)
            l_ref[h] = l_ref[h] * factor + jnp.sum(expo, axis=1, keepdims=True)
            acc_ref[h] = acc_ref[h] * factor + dot(expo.astype(BF16), kv[:, at + NOPE : at + NOPE + VALUE])
            m_ref[h] = jnp.broadcast_to(new, m_ref.shape[1:])

    @pl.when(step == pl.num_programs(1) - 1)
    def _():
        lane = lax.broadcasted_iota(jnp.int32, (BLOCK, 128), 1)
        lse = jnp.zeros((BLOCK, 128), F32)
        for h in range(heads):
            out = acc_ref[h] / l_ref[h]
            out_ref[:, :, :, h * VALUE : (h + 1) * VALUE] = out.astype(BF16).reshape(
                out_ref.shape[:3] + (VALUE,)
            )
            lse = jnp.where(lane == h, m_ref[h] + jnp.log(l_ref[h]), lse)
        lse_ref[0] = lse


def attention(blk, query, lat, up, heads):
    n_head, seqs, own = query.shape[:3]
    n_blk = lat.shape[0] // n_head
    scale = (NOPE + ROPE) ** -0.5
    row = lambda width: pl.BlockSpec((n_head, 1, own, width), lambda s, b, r: (0, s, 0, 0))
    steps = n_blk * seqs
    return pl.pallas_call(
        functools.partial(attention_kernel, heads, scale),
        grid_spec=pltpu.PrefetchScalarGridSpec(
            num_scalar_prefetch=1,
            grid=(seqs, n_blk),
            in_specs=[
                row(query.shape[3]),
                pl.BlockSpec(
                    (n_head, 1, own, RANK + ROPE), lambda s, b, r: (jnp.minimum(b, r[0]), s, 0, 0)
                ),
                pl.BlockSpec(up.shape, lambda s, b, r: (0, 0)),
            ],
            out_specs=[row(heads * VALUE), pl.BlockSpec((1, BLOCK, 128), lambda s, b, r: (s, 0, 0))],
            scratch_shapes=[
                pltpu.VMEM((heads, BLOCK, 128), F32),
                pltpu.VMEM((heads, BLOCK, 128), F32),
                pltpu.VMEM((heads, BLOCK, VALUE), F32),
            ],
        ),
        out_shape=[
            jax.ShapeDtypeStruct((n_head, seqs, own, heads * VALUE), BF16),
            jax.ShapeDtypeStruct((seqs, BLOCK, 128), F32),
        ],
        cost_estimate=pl.CostEstimate(
            flops=steps * BLOCK * 2 * (RANK * up.shape[1] + heads * BLOCK * 640),
            bytes_accessed=lat.size * 2 + up.size * 2 + query.size * 4,
            transcendentals=steps * heads * BLOCK * BLOCK,
        ),
        name="attention",
    )(blk, query, lat, up)


def attention_back_kernel(
    heads, scale, blk_ref, q_ref, lat_ref, up_ref, att_ref, datt_ref, lse_ref, cos_ref, sin_ref,
    dq_ref, dlat_ref, dup_ref, delta_ref, dqn_ref, dqr_ref, up_acc,
):
    seq, step = pl.program_id(0), pl.program_id(1)
    last = pl.num_programs(1) - 1

    @pl.when((seq == 0) & (step == 0))
    def _():
        up_acc[...] = jnp.zeros_like(up_acc)

    @pl.when(step == 0)
    def _():
        dqn_ref[...] = jnp.zeros_like(dqn_ref)
        dqr_ref[...] = jnp.zeros_like(dqr_ref)
        prod = att_ref[...].astype(F32) * datt_ref[...].astype(F32)
        prod = prod.reshape(BLOCK, heads * VALUE)
        for h in range(heads):
            delta_ref[h] = jnp.broadcast_to(
                jnp.sum(prod[:, h * VALUE : (h + 1) * VALUE], axis=1, keepdims=True), (BLOCK, 128)
            )

    @pl.when(step <= blk_ref[0])
    def _():
        lat = lat_ref[...].reshape(BLOCK, RANK + ROPE)
        latn = lat[:, :RANK]
        kv = dot(latn, up_ref[...]).astype(BF16)
        copies = spread(heads)
        rope = dot(lat[:, RANK:], copies).astype(BF16)
        query = q_ref[...].reshape(BLOCK, heads * (NOPE + ROPE))
        query_rope = query[:, heads * NOPE :]
        d_att = datt_ref[...].reshape(BLOCK, heads * VALUE)
        d_rope = jnp.zeros((BLOCK, heads * ROPE), F32)
        d_kv = []
        for h in range(heads):
            at = h * (NOPE + VALUE)
            lanes = head_lanes(heads, h)
            q_h = query[:, h * NOPE : (h + 1) * NOPE]
            k_h = kv[:, at : at + NOPE]
            d_h = d_att[:, h * VALUE : (h + 1) * VALUE]
            masked = jnp.where(lanes, query_rope, jnp.zeros_like(query_rope))
            scores = (dot_nt(q_h, k_h) + dot_nt(masked, rope)) * scale
            prob = jnp.exp(scores - lse_ref[0][:, h : h + 1])
            d_prob = dot_nt(d_h, kv[:, at + NOPE : at + NOPE + VALUE])
            d_score = (prob * (d_prob - delta_ref[h][:, :1]) * scale).astype(BF16)
            dqn_ref[h] = dqn_ref[h] + dot(d_score, k_h)
            dqr_ref[...] = dqr_ref[...] + jnp.where(lanes, dot(d_score, rope), 0.0)
            d_kv.append(dot_tn(d_score, q_h))
            d_kv.append(dot_tn(prob.astype(BF16), d_h))
            d_rope = d_rope + dot_tn(d_score, masked)
        d_kv = jnp.concatenate(d_kv, axis=1).astype(BF16)
        up_acc[...] += dot_tn(latn, d_kv)
        shape = dlat_ref.shape[:3]
        dlat_ref[:, :, :, :RANK] = dot_nt(d_kv, up_ref[...]).astype(BF16).reshape(shape + (RANK,))
        dlat_ref[:, :, :, RANK:] = (
            dot_nt(d_rope.astype(BF16), copies).astype(BF16).reshape(shape + (ROPE,))
        )

    @pl.when(step > blk_ref[0])
    def _():
        dlat_ref[...] = jnp.zeros_like(dlat_ref)

    @pl.when(step == last)
    def _():
        shape = dq_ref.shape[:3]
        for h in range(heads):
            dq_ref[:, :, :, h * NOPE : (h + 1) * NOPE] = dqn_ref[h].astype(BF16).reshape(shape + (NOPE,))
        half = heads * ROPE // 2
        cosine, sine = cos_ref[...], sin_ref[...]
        first, second = dqr_ref[:, :half], dqr_ref[:, half:]
        at = heads * NOPE
        dq_ref[:, :, :, at : at + half] = (first * cosine + second * sine).astype(BF16).reshape(shape + (half,))
        dq_ref[:, :, :, at + half :] = (second * cosine - first * sine).astype(BF16).reshape(shape + (half,))

    @pl.when((seq == pl.num_programs(0) - 1) & (step == last))
    def _():
        dup_ref[...] = up_acc[...].astype(BF16)


def attention_back(blk, query, lat, up, att, d_att, lse, cosine, sine, heads):
    n_head, seqs, own = query.shape[:3]
    n_blk = lat.shape[0] // n_head
    scale = (NOPE + ROPE) ** -0.5
    row = lambda width: pl.BlockSpec((n_head, 1, own, width), lambda s, b, r: (0, s, 0, 0))
    whole = lambda x: pl.BlockSpec(x.shape, lambda s, b, r: (0, 0))
    half = heads * ROPE // 2
    steps = n_blk * seqs
    return pl.pallas_call(
        functools.partial(attention_back_kernel, heads, scale),
        grid_spec=pltpu.PrefetchScalarGridSpec(
            num_scalar_prefetch=1,
            grid=(seqs, n_blk),
            in_specs=[
                row(query.shape[3]),
                pl.BlockSpec(
                    (n_head, 1, own, RANK + ROPE), lambda s, b, r: (jnp.minimum(b, r[0]), s, 0, 0)
                ),
                whole(up),
                row(heads * VALUE),
                row(heads * VALUE),
                pl.BlockSpec((1, BLOCK, 128), lambda s, b, r: (s, 0, 0)),
                whole(cosine),
                whole(sine),
            ],
            out_specs=[
                row(query.shape[3]),
                pl.BlockSpec((n_head, 1, own, RANK + ROPE), lambda s, b, r: (b, s, 0, 0)),
                whole(up),
            ],
            scratch_shapes=[
                pltpu.VMEM((heads, BLOCK, 128), F32),
                pltpu.VMEM((heads, BLOCK, NOPE), F32),
                pltpu.VMEM((BLOCK, 2 * half), F32),
                pltpu.VMEM(up.shape, F32),
            ],
        ),
        out_shape=[
            jax.ShapeDtypeStruct(query.shape, BF16),
            jax.ShapeDtypeStruct(lat.shape, BF16),
            jax.ShapeDtypeStruct(up.shape, BF16),
        ],
        cost_estimate=pl.CostEstimate(
            flops=steps * BLOCK * 2 * (3 * RANK * up.shape[1] + heads * BLOCK * 1700),
            bytes_accessed=lat.size * 4 + up.size * 4 + query.size * 8,
            transcendentals=steps * heads * BLOCK * BLOCK,
        ),
        name="attention_back",
    )(blk, query, lat, up, att, d_att, lse, cosine, sine)


def pick(own, first_ref, second_ref, out_ref):
    @pl.when(own)
    def _():
        out_ref[...] = first_ref[...]

    @pl.when(jnp.logical_not(own))
    def _():
        out_ref[...] = second_ref[...]


def put(own, value_ref, first_ref, second_ref):
    @pl.when(own)
    def _():
        first_ref[...] = value_ref[...]

    @pl.when(jnp.logical_not(own))
    def _():
        second_ref[...] = value_ref[...]


def gate_lanes(tail, base, local):
    lane = lax.broadcasted_iota(jnp.int32, tail.shape, 1)
    tail = tail.astype(F32)
    return [
        jnp.sum(jnp.where(lane == base + e, tail, 0.0), axis=1, keepdims=True) for e in range(local)
    ]


def spans(size, step):
    return [(at, min(step, size - at)) for at in range(0, size, step)]


def experts_kernel(
    units, local, base_ref, xa_ref, xb_ref, ta_ref, tb_ref, win_ref, wout_ref,
    x_ref, gu_ref, outa_ref, outb_ref, tail_ref, act_ref, sum_ref,
):
    own = pl.program_id(0) < pl.num_programs(0) // 2
    pick(own, xa_ref, xb_ref, x_ref)
    pick(own, ta_ref, tb_ref, tail_ref)
    gates = gate_lanes(tail_ref[...], base_ref[0], local)
    padded = wout_ref.shape[0]
    for at, size in spans(padded, 256):
        gate = dot(x_ref[...], win_ref[:, at : at + size])
        up = dot(x_ref[...], win_ref[:, padded + at : padded + at + size])
        gu_ref[:, at : at + size] = gate.astype(BF16)
        gu_ref[:, padded + at : padded + at + size] = up.astype(BF16)
        act = gate * jax.nn.sigmoid(gate) * up
        for here in range(0, size, 128):
            expert = (at + here) // units
            part = act[:, here : here + 128]
            part = part * gates[expert] if expert < local else part
            act_ref[:, at + here : at + here + 128] = part.astype(BF16)
    for at, size in spans(wout_ref.shape[1], 512):
        sum_ref[:, at : at + size] = dot(act_ref[...], wout_ref[:, at : at + size]).astype(BF16)
    put(own, sum_ref, outa_ref, outb_ref)


def half_specs(tile, steps, width, column=0):
    half = steps // 2
    return [
        pl.BlockSpec((tile, width), lambda i, r: (jnp.minimum(i, half - 1), column)),
        pl.BlockSpec((tile, width), lambda i, r: (jnp.maximum(i - half, 0), column)),
    ]


def tile_of(rows):
    return max(t for t in range(16, 385, 16) if rows % t == 0)


def resident(x):
    return pl.BlockSpec(x.shape, lambda i, r: (0, 0), pipeline_mode=pl.Buffered(1))


def run_experts(base, pair, win, wout, units, local):
    half, width, padded = pair[0].shape[0], wout.shape[1], wout.shape[0]
    tile = tile_of(half)
    steps = 2 * half // tile
    row = lambda size: pl.BlockSpec((tile, size), lambda i, r: (i, 0))
    rows = 2 * half
    shape = lambda count, size: jax.ShapeDtypeStruct((count, size), BF16)
    return pl.pallas_call(
        functools.partial(experts_kernel, units, local),
        grid_spec=pltpu.PrefetchScalarGridSpec(
            num_scalar_prefetch=1,
            grid=(steps,),
            in_specs=half_specs(tile, steps, width)
            + half_specs(tile, steps, 128, width // 128)
            + [resident(win), resident(wout)],
            out_specs=[row(width), row(2 * padded)] + half_specs(tile, steps, width),
            scratch_shapes=[
                pltpu.VMEM((tile, 128), BF16),
                pltpu.VMEM((tile, padded), BF16),
                pltpu.VMEM((tile, width), BF16),
            ],
        ),
        out_shape=[shape(rows, width), shape(rows, 2 * padded), shape(half, width), shape(half, width)],
        cost_estimate=pl.CostEstimate(
            flops=rows * width * padded * 6,
            bytes_accessed=(rows * (3 * width + 2 * padded) + 3 * width * padded) * 2,
            transcendentals=rows * padded,
        ),
        name="experts",
    )(base, *pair, *pair, win, wout)


def experts_back_kernel(
    units, local, base_ref, ga_ref, gb_ref, ta_ref, tb_ref, gu_ref, win_ref, wout_ref,
    hid_ref, act_ref, g_ref, outa_ref, outb_ref, tail_ref, sum_ref,
):
    own = pl.program_id(0) < pl.num_programs(0) // 2
    pick(own, ga_ref, gb_ref, g_ref)
    pick(own, ta_ref, tb_ref, tail_ref)
    gates = gate_lanes(tail_ref[...], base_ref[0], local)
    padded, width = wout_ref.shape
    prods = [jnp.zeros(tail_ref.shape, F32) for _ in range(local)]
    for at, size in spans(padded, 256):
        d_acts = dot_nt(g_ref[...], wout_ref[at : at + size, :])
        for here in range(0, size, 128):
            unit = at + here
            expert = unit // units
            d_act = d_acts[:, here : here + 128]
            gate = gu_ref[:, unit : unit + 128].astype(F32)
            up = gu_ref[:, padded + unit : padded + unit + 128].astype(F32)
            sig = jax.nn.sigmoid(gate)
            silu = gate * sig
            act = silu * up
            if expert < local:
                prods[expert] = prods[expert] + act * d_act
                d_act = d_act * gates[expert]
                act = act * gates[expert]
            hid_ref[:, unit : unit + 128] = (d_act * up * (sig + silu * (1.0 - sig))).astype(BF16)
            hid_ref[:, padded + unit : padded + unit + 128] = (d_act * silu).astype(BF16)
            act_ref[:, unit : unit + 128] = act.astype(BF16)
    for at, size in spans(width, 256):
        sum_ref[:, at : at + size] = dot_nt(hid_ref[...], win_ref[at : at + size, :]).astype(BF16)
    lane = lax.broadcasted_iota(jnp.int32, tail_ref.shape, 1)
    extra = jnp.zeros(tail_ref.shape, F32)
    for e in range(local):
        extra = jnp.where(lane == base_ref[0] + e, jnp.sum(prods[e], axis=1, keepdims=True), extra)
    sum_ref[:, width:] = extra.astype(BF16)
    put(own, sum_ref, outa_ref, outb_ref)


def run_experts_back(base, grads, pair, gu, win, wout, units, local):
    half, width, padded = grads[0].shape[0], wout.shape[1], wout.shape[0]
    tile = tile_of(half)
    steps = 2 * half // tile
    row = lambda size: pl.BlockSpec((tile, size), lambda i, r: (i, 0))
    rows = 2 * half
    shape = lambda count, size: jax.ShapeDtypeStruct((count, size), BF16)
    return pl.pallas_call(
        functools.partial(experts_back_kernel, units, local),
        grid_spec=pltpu.PrefetchScalarGridSpec(
            num_scalar_prefetch=1,
            grid=(steps,),
            in_specs=half_specs(tile, steps, width)
            + half_specs(tile, steps, 128, width // 128)
            + [row(2 * padded), resident(win), resident(wout)],
            out_specs=[row(2 * padded), row(padded), row(width)] + half_specs(tile, steps, width + 128),
            scratch_shapes=[pltpu.VMEM((tile, 128), BF16), pltpu.VMEM((tile, width + 128), BF16)],
        ),
        out_shape=[
            shape(rows, 2 * padded), shape(rows, padded), shape(rows, width),
            shape(half, width + 128), shape(half, width + 128),
        ],
        cost_estimate=pl.CostEstimate(
            flops=rows * width * padded * 6,
            bytes_accessed=(rows * (3 * width + 5 * padded) + 3 * width * padded) * 2,
            transcendentals=rows * padded,
        ),
        name="experts_back",
    )(base, *grads, *pair, gu, win, wout)


def on_device(
    states, teacher, valid, routes, norm_in, w_query, w_down_kv, norm_kv, w_up_kv, w_out, norm_ffn,
    w_router, shared_in, shared_out, expert_in, expert_out,
):
    n_blk, n_head = lax.axis_size("blk"), lax.axis_size("head")
    blk, head = lax.axis_index("blk"), lax.axis_index("head")
    own_pos, seqs, width = states.shape
    block_pos = own_pos * n_head
    rows = own_pos * seqs
    block_rows = rows * n_head
    total_rows = block_rows * n_blk
    experts = w_router.shape[1]
    local = expert_in.shape[0]
    eff = expert_in.shape[3]
    shared = shared_in.shape[2] // n_blk
    heads = w_query.shape[1] // (NOPE + ROPE)
    scale = (NOPE + ROPE) ** (-0.5)
    assert block_pos == BLOCK
    blks, heads_ring = blk_dims(n_blk), head_dims(n_head)

    def gather_head(x):
        return gather_axis(x, heads_ring).reshape((-1,) + x.shape[1:])

    def scatter_head(x):
        return scatter_axis(x.reshape((n_head, -1) + x.shape[1:]), heads_ring)

    def take_own(x):
        own = lax.dynamic_slice_in_dim(x, head * own_pos, own_pos, 0)
        return jnp.moveaxis(own, 1, 0).reshape((rows,) + x.shape[2:])

    part = width // n_blk
    quarter = part // n_head
    lat_width = RANK + ROPE
    small = jnp.concatenate(
        [norm_in, norm_ffn, w_router.reshape(-1), norm_kv, jnp.sum(valid, axis=1).astype(BF16)]
    )
    lines = -(-small.shape[0] // lat_width)
    small = jnp.pad(small, (0, lines * lat_width - small.shape[0])).reshape(lines, lat_width)
    down = lax.dynamic_slice_in_dim(w_down_kv, head * quarter, quarter, 0)
    down = gather_axis(jnp.concatenate([down, small], axis=0), blks)
    lanes = heads * ROPE // 2
    wq = w_query.reshape(part, heads, NOPE + ROPE)
    wq = jnp.concatenate(
        [
            wq[:, :, :NOPE].reshape(part, -1),
            wq[:, :, NOPE : NOPE + ROPE // 2].reshape(part, -1),
            wq[:, :, NOPE + ROPE // 2 :].reshape(part, -1),
        ],
        axis=1,
    )
    most = part * 3 // 4
    wq_most = gather_dims(wq[None, :most], blks[:1])
    wq_rest = gather_dims(wq[None, most:], blks[:0:-1])
    states_blk = gather_head(jnp.moveaxis(states, 1, 0).reshape(rows, width))
    down, wq_most, wq_rest = lax.optimization_barrier((down, wq_most, wq_rest))
    small = down[:, quarter:].reshape(n_blk, -1)
    down = jnp.moveaxis(gather_axis(down[:, :quarter], heads_ring), 0, 1).reshape(width, lat_width)
    wq_most = in_order(gather_dims(wq_most, blks[1:]), blks)
    wq_rest = in_order(gather_dims(wq_rest, blks[:1]), blks[::-1])
    wq = jnp.concatenate([wq_most, wq_rest], axis=1).reshape(width, -1)
    gain_in = small[:, :part].reshape(-1).astype(F32)
    gain_ffn = small[:, part : 2 * part].reshape(-1).astype(F32)
    at = 2 * part
    router = small[:, at : at + part * experts].reshape(width, experts)
    at += part * experts
    gain_kv = small[:, at : at + RANK // n_blk].reshape(-1).astype(F32)
    at += RANK // n_blk
    count = jnp.sum(small[:, at : at + block_pos].astype(F32))
    up_out = jnp.concatenate([w_up_kv, w_out.reshape(-1, w_up_kv.shape[1])], axis=0)
    up_out = lax.all_gather(up_out, "blk", axis=0)
    wup = up_out[:, : w_up_kv.shape[0]].reshape(RANK, -1)
    wo = jnp.moveaxis(up_out[:, w_up_kv.shape[0] :].reshape((n_blk,) + w_out.shape), 0, 1).reshape(-1, width)

    pieces = jnp.concatenate(
        [
            jnp.transpose(shared_in.reshape(part, 2, n_blk, shared), (2, 1, 3, 0)).reshape(
                n_blk, 2 * shared, part
            ),
            shared_out.reshape(n_blk, shared, part),
        ],
        axis=1,
    )
    pieces = lax.all_to_all(pieces, "blk", split_axis=0, concat_axis=0, tiled=True)
    sh_in = jnp.transpose(pieces[:, : 2 * shared], (0, 2, 1)).reshape(width, 2, shared)
    sh_out = jnp.transpose(pieces[:, 2 * shared :], (1, 0, 2)).reshape(shared, width)
    units = -(-eff // 128) * 128
    shared_units = -(-shared // 128) * 128
    padded = local * units + shared_units
    wide = lambda x, size: jnp.pad(x, ((0, 0), (0, size - x.shape[1])))
    win = jnp.concatenate(
        [
            block
            for side in range(2)
            for block in [wide(expert_in[e, :, side], units) for e in range(local)]
            + [wide(sh_in[:, side], shared_units)]
        ],
        axis=1,
    )
    wout = jnp.concatenate(
        [jnp.pad(expert_out, ((0, 0), (0, units - eff), (0, 0))).reshape(-1, width)]
        + [jnp.pad(sh_out, ((0, shared_units - shared), (0, 0)))],
        axis=0,
    )

    x_own = jnp.moveaxis(states, 1, 0).reshape(rows, width).astype(F32)
    h1_f, rstd_in = normed(x_own, gain_in)
    h1_own = h1_f.astype(BF16)
    h1_blk = normed(states_blk.astype(F32), gain_in)[0].astype(BF16)
    pos_own = blk * block_pos + head * own_pos + jnp.arange(own_pos, dtype=jnp.int32)
    table_own = jnp.tile(angles(pos_own), (seqs, 1))
    pos_blk = blk * block_pos + jnp.arange(block_pos, dtype=jnp.int32)
    table_seq = angles(pos_blk)
    cos_seq, sin_seq = (jnp.tile(f(table_seq), (1, heads)) for f in (jnp.cos, jnp.sin))
    table_blk = jnp.broadcast_to(
        angles(pos_blk).reshape(n_head, 1, own_pos, ROPE // 2), (n_head, seqs, own_pos, ROPE // 2)
    ).reshape(block_rows, ROPE // 2)
    lat = dot(h1_own, down)
    lat_c = lat[:, :RANK]
    latn_f, rstd_kv = normed(lat_c, gain_kv)
    payload = jnp.concatenate([latn_f, rotate(lat[:, RANK:], table_own)], axis=1).astype(BF16)
    lat_all = gather_all(payload)
    wq, win, wout = lax.optimization_barrier((wq, win, wout))
    query = dot(h1_blk, wq)
    cosine = jnp.tile(jnp.cos(table_blk), (1, heads))
    sine = jnp.tile(jnp.sin(table_blk), (1, heads))
    q_first, q_second = query[:, -2 * lanes : -lanes], query[:, -lanes:]
    query = jnp.concatenate(
        [query[:, : -2 * lanes], q_first * cosine - q_second * sine, q_second * cosine + q_first * sine],
        axis=1,
    ).astype(BF16)
    shape4 = (n_head, seqs, own_pos, -1)
    query = query.reshape(shape4)
    lat_all = lat_all.reshape(n_blk * n_head, seqs, own_pos, -1)
    blk_index = jnp.full((1,), blk, jnp.int32)
    att_b, lse = attention(blk_index, query, lat_all, wup, heads)
    att_rows = att_b.reshape(block_rows, heads * VALUE)
    y_own = x_own + scatter_head(dot(att_rows, wo).astype(BF16)).astype(F32)
    h2_f, rstd_ffn = normed(y_own, gain_ffn)
    h2_own = h2_f.astype(BF16)

    routes_own = take_own(routes)
    mask = jnp.any(routes_own[:, :, None] == jnp.arange(experts, dtype=jnp.int32), axis=1)
    logits = jnp.where(mask, dot(h2_own, router), -1e30)
    gates = jnp.where(mask, jnp.exp(logits - jnp.max(logits, axis=1, keepdims=True)), 0.0)
    gates = gates / jnp.sum(gates, axis=1, keepdims=True)
    assert experts <= 128
    tail = jnp.zeros((rows, 128 - experts), BF16)
    base = jnp.full((1,), blk * local, jnp.int32)
    x_ext = jnp.concatenate([h2_own, gates.astype(BF16), tail], axis=1)
    rounds = max(1, total_rows // 4096)

    def forward(x_rows):
        pairs = gather_parts(x_rows, n_blk, n_head)
        outs = [run_experts(base, pair, win, wout, units, local) for pair in pairs]
        kept = [(pair, x, gu) for pair, (x, gu, _, _) in zip(pairs, outs)]
        return kept, scatter_parts([out[2:] for out in outs], n_blk, n_head)

    def backward(grad_rows, kept):
        d_win = d_wout = 0.0
        results = []
        for grads, (pair, x, gu) in zip(gather_parts(grad_rows, n_blk, n_head), kept):
            d_hidden, act, grad, *result = run_experts_back(base, grads, pair, gu, win, wout, units, local)
            results.append(result)
            d_win = d_win + dot_tn(x, d_hidden)
            d_wout = d_wout + dot_tn(act, grad)
        return scatter_parts(results, n_blk, n_head), d_win, d_wout

    def in_rounds(x):
        return x.reshape((rounds, -1) + x.shape[1:])

    if rounds == 1:
        kept, mixed = forward(x_ext)
    else:
        mixed = lax.map(lambda x: forward(x)[1], in_rounds(x_ext)).reshape(rows, width)
    mixed = mixed.astype(F32)
    out_own = (y_own + mixed).astype(BF16)
    diff = out_own.astype(F32) - take_own(teacher).astype(F32)
    valid_own = take_own(valid).astype(F32)[:, None]
    loss_part = jnp.sum(valid_own * diff * diff)
    grad_own = diff * valid_own * (total_rows / count)

    grad_own_b = grad_own.astype(BF16)
    if rounds == 1:
        back, d_win, d_wout = backward(grad_own_b, kept)
    else:

        def round_back(sums, both):
            kept, _ = forward(both[0])
            back, d_win, d_wout = backward(both[1], kept)
            return (sums[0] + d_win, sums[1] + d_wout), back

        start = (jnp.zeros((width, 2 * padded), F32), jnp.zeros((padded, width), F32))
        (d_win, d_wout), back = lax.scan(round_back, start, (in_rounds(x_ext), in_rounds(grad_own_b)))
        back = back.reshape(rows, -1)
    d_sh = jnp.concatenate(
        [d_win[:, s * padded + local * units :][:, :shared].T for s in range(2)]
        + [d_wout[local * units :][:shared]],
        axis=0,
    ).astype(BF16)
    d_sh = jnp.transpose(d_sh.reshape(3 * shared, n_blk, part), (1, 0, 2))
    back, d_win, d_wout, d_sh = lax.optimization_barrier((back, d_win, d_wout, d_sh))
    back = back.astype(F32)
    d_sh = lax.all_to_all(d_sh, "blk", split_axis=0, concat_axis=0, tiled=True).astype(F32)
    grad_shin = jnp.transpose(d_sh[:, : 2 * shared].reshape(n_blk, 2, shared, part), (3, 1, 0, 2)).reshape(
        part, 2, n_blk * shared
    )
    grad_shout = d_sh[:, 2 * shared :].reshape(n_blk * shared, part)

    d_gates = back[:, width : width + experts]
    d_logits = gates * (d_gates - jnp.sum(gates * d_gates, axis=1, keepdims=True))
    d_logits = d_logits.astype(BF16)
    grad_router = dot_tn(h2_own, d_logits)
    dh2 = back[:, :width] + dot_nt(d_logits, router)
    dy_branch, grad_gain_ffn = norm_back(dh2, y_own, rstd_ffn, gain_ffn)
    dy_own = grad_own + dy_branch

    dy_blk = gather_head(dy_own.astype(BF16))
    grad_wo = dot_tn(att_rows, dy_blk).astype(BF16)
    d_att = dot_nt(dy_blk, wo).astype(BF16).reshape(shape4)
    grad_wo, d_att = lax.optimization_barrier((grad_wo, d_att))
    grad_wo = scatter_blk(grad_wo, 1).astype(F32)
    dq, d_lat, d_up = attention_back(
        blk_index, query, lat_all, wup, att_b, d_att, lse, cos_seq, sin_seq, heads
    )
    dq, d_win, d_wout = lax.optimization_barrier((dq, d_win, d_wout))
    grad_ein = jnp.stack(
        [
            jnp.stack([d_win[:, s * padded + e * units :][:, :eff] for s in range(2)], axis=1)
            for e in range(local)
        ]
    )
    grad_eout = d_wout[: local * units].reshape(local, units, width)[:, :eff]
    d_lat = scatter_all(d_lat.reshape(total_rows, -1)).astype(F32)
    dq = dq.reshape(block_rows, -1)
    dh1 = scatter_head(dot_nt(dq, wq).astype(BF16)).astype(F32)
    grad_wq = dot_tn(h1_blk, dq).astype(BF16).reshape(n_blk, part, -1)
    grad_wq = jnp.concatenate(
        [scatter_axis(grad_wq[:, :most], blks), scatter_axis(grad_wq[:, most:], blks[::-1])], axis=0
    ).astype(F32)
    grad_wq = jnp.concatenate(
        [
            grad_wq[:, : heads * NOPE].reshape(part, heads, NOPE),
            grad_wq[:, heads * NOPE : -lanes].reshape(part, heads, ROPE // 2),
            grad_wq[:, -lanes:].reshape(part, heads, ROPE // 2),
        ],
        axis=2,
    ).reshape(part, -1)
    grad_up = scatter_blk(d_up).astype(F32)
    d_lat_c, grad_gain_kv = norm_back(d_lat[:, :RANK], lat_c, rstd_kv, gain_kv)
    d_lat_b = jnp.concatenate([d_lat_c, rotate(d_lat[:, RANK:], -table_own)], axis=1).astype(BF16)
    d_lat_blk = gather_head(d_lat_b)
    h1_part = lax.dynamic_slice_in_dim(
        h1_blk.reshape(block_rows, n_blk, n_head, quarter), head, 1, 2
    ).reshape(block_rows, -1)
    grad_down = dot_tn(h1_part, d_lat_blk).astype(BF16).reshape(n_blk, quarter, -1)
    grad_down = gather_head(scatter_axis(grad_down, blks)).astype(F32)
    dh1 = dh1 + dot_nt(d_lat_b, down)
    dx_branch, grad_gain_in = norm_back(dh1, x_own, rstd_in, gain_in)
    dx_own = dy_own + dx_branch

    loss_high = loss_part.astype(BF16).astype(F32)
    sums = jnp.concatenate(
        [
            grad_gain_in.reshape(n_blk, -1),
            grad_gain_ffn.reshape(n_blk, -1),
            grad_router.reshape(n_blk, -1),
            grad_gain_kv.reshape(n_blk, -1),
            jnp.full((n_blk, 1), loss_high),
            jnp.full((n_blk, 1), loss_part - loss_high),
        ],
        axis=1,
    )
    sums = scatter_axis(sums, blks)
    for dim in heads_ring:
        sums = sum(ring_gather(sums, dim))
    out_gain_in = sums[:part]
    out_gain_ffn = sums[part : 2 * part]
    at = 2 * part
    out_router = sums[at : at + part * experts].reshape(part, experts)
    at += part * experts
    out_gain_kv = sums[at : at + RANK // n_blk]
    loss = (sums[-2] + sums[-1]) / (width * count)

    def give(x):
        return jnp.moveaxis(x.reshape(seqs, own_pos, width), 0, 1)

    return (
        give(out_own), loss, give(dx_own), out_gain_in, grad_wq, grad_down, out_gain_kv, grad_up,
        grad_wo, out_gain_ffn, out_router, grad_shin, grad_shout, grad_ein, grad_eout,
    )


def solution(mesh):
    in_specs = (
        P(BOTH, None, None), P("blk", None, None), P("blk", None), P("blk", None, None), P("blk"),
        P("blk", "head"), P("blk", None), P("blk"), P("blk", "head"), P("head", "blk"), P("blk"),
        P("blk", None), P("blk", None, "head"), P("head", "blk"), P("blk", None, None, "head"),
        P("blk", "head", None),
    )
    out_specs = (
        P(BOTH, None, None), P(), P(BOTH, None, None), P("blk"), P("blk", "head"), P("blk", None),
        P("blk"), P("blk", "head"), P("head", "blk"), P("blk"), P("blk", None), P("blk", None, "head"),
        P("head", "blk"), P("blk", None, None, "head"), P("blk", "head", None),
    )
    return jax.shard_map(on_device, mesh=mesh, in_specs=in_specs, out_specs=out_specs, check_vma=False)
```

```python
import functools

import jax
import jax.numpy as jnp
from jax import lax
from jax.experimental import pallas as pl
from jax.experimental.layout import Layout, with_layout_constraint
from jax.experimental.pallas import tpu as pltpu
from jax.sharding import PartitionSpec as P

NOPE = 128
ROPE = 64
VALUE = 128
RANK = 512
BLOCK = 256
EPS = 1e-06
F32 = jnp.float32
BF16 = jnp.bfloat16
BOTH = ("blk", "head")


def angles(position):
    frequency = 10000.0 ** (-2.0 * jnp.arange(ROPE // 2, dtype=F32) / ROPE)
    return position.astype(F32)[:, None] * frequency[None, :]


def rotate(values, table):
    half = ROPE // 2
    cosine, sine = jnp.cos(table), jnp.sin(table)
    first, second = values[:, :half], values[:, half:]
    return jnp.concatenate([first * cosine - second * sine, second * cosine + first * sine], axis=1)


def normed(values, gain):
    rstd = lax.rsqrt(jnp.mean(values * values, axis=-1, keepdims=True) + EPS)
    return values * rstd * gain, rstd


def norm_back(grad, values, rstd, gain):
    scaled = grad * gain
    out = rstd * scaled - values * rstd**3 * jnp.mean(scaled * values, axis=-1, keepdims=True)
    return out, jnp.sum(grad * values * rstd, axis=0)


def by_rows(x):
    return with_layout_constraint(x, Layout(tuple(range(x.ndim))))


def dot(a, b):
    return jnp.dot(a, b, preferred_element_type=F32)


def dot_nt(a, b):
    return lax.dot_general(a, b, (((1,), (1,)), ((), ())), preferred_element_type=F32)


def dot_tn(a, b):
    return lax.dot_general(a, b, (((0,), (0,)), ((), ())), preferred_element_type=F32)


def blk_dims(n_blk):
    if n_blk == 8:
        return [("blk", 2, 4), ("blk", 1, 2)]
    if n_blk == 32:
        return [("blk", 8, 4), ("blk", 2, 4), ("blk", 1, 2)]
    return [("blk", 1, n_blk)]


def head_dims(n_head):
    return [("head", 2, n_head // 2), ("head", 1, 2)] if n_head % 2 == 0 else [("head", 1, n_head)]


def shift(x, dim, by):
    axis, stride, size = dim
    pairs = []
    for i in range(lax.axis_size(axis)):
        digit = i // stride % size
        pairs.append((i, i + ((digit + by) % size - digit) * stride))
    return lax.ppermute(x, axis, pairs)


def digit_of(dim):
    axis, stride, size = dim
    return lax.axis_index(axis) // stride % size


def ring_gather(x, dim):
    pieces = [x]
    for _ in range(dim[2] - 1):
        pieces.append(shift(pieces[-1], dim, -1))
    return pieces


def ring_scatter(pieces, dim):
    total = pieces[-1]
    for piece in pieces[-2::-1]:
        total = shift(total, dim, 1) + piece
    return total


def direct_gather(x, dim):
    return [x] + [shift(x, dim, -k) for k in range(1, dim[2])]


def direct_scatter(pieces, dim):
    total = pieces[0].astype(F32)
    for k in range(1, dim[2]):
        total = total + shift(pieces[k], dim, k).astype(F32)
    return total.astype(pieces[0].dtype)


def gather_dims(x, dims, step=ring_gather):
    for dim in dims:
        x = jnp.concatenate(step(x, dim), axis=0)
    return x


def scatter_dims(x, dims, step=ring_scatter):
    for dim in reversed(dims):
        x = step(jnp.split(x, dim[2], axis=0), dim)
    return x


def relative(dims, index):
    place, scale = 0, 1
    for dim in dims:
        place = place + (index // dim[1] % dim[2] - digit_of(dim)) % dim[2] * scale
        scale *= dim[2]
    return place


def absolute(dims, place):
    index = 0
    for dim in dims:
        index = index + (place % dim[2] + digit_of(dim)) % dim[2] * dim[1]
        place //= dim[2]
    return index


def gather_axis(x, dims):
    return in_order(gather_dims(x[None], dims, direct_gather), dims)


def in_order(stack, dims):
    n = stack.shape[0]
    return jnp.concatenate(
        [lax.dynamic_slice_in_dim(stack, relative(dims, i), 1, 0) for i in range(n)], axis=0
    )


def scatter_axis(x, dims):
    n = lax.axis_size(dims[0][0])
    stack = jnp.concatenate(
        [lax.dynamic_slice_in_dim(x, absolute(dims, i), 1, 0) for i in range(n)], axis=0
    )
    return scatter_dims(stack, dims, direct_scatter)[0]


def split_dims(n_blk, n_head):
    blk, head = blk_dims(n_blk), head_dims(n_head)
    return blk[0], blk[1:], head[:-1], head[-1]


def gather_parts(x, n_blk, n_head):
    third = x.shape[0] * 5 // 16
    first = x.shape[0] - 2 * third
    z, inner, y, core = split_dims(n_blk, n_head)
    a, pieces = x[:first], [x[first:]]
    early = [inner, y] + [[]] * (z[2] - 4)
    for dims in early:
        piece, a = shift(pieces[-1], z, -1), gather_dims(a, dims)
        piece, a = lax.optimization_barrier((piece, a))
        pieces.append(piece)
    pieces.append(shift(pieces[-1], z, -1))
    b = gather_dims(jnp.concatenate([p[:third] for p in pieces], axis=0), y + inner)
    c = gather_dims(jnp.concatenate([p[third:] for p in pieces], axis=0), inner + y)
    a = gather_dims(a, [z])
    return [ring_gather(part, core) for part in (b, c, a)]


def scatter_parts(sums, fillers, n_blk, n_head):
    z, inner, y, _ = split_dims(n_blk, n_head)
    b, c, a = sums
    b, first = lax.optimization_barrier((b, fillers[0]))
    b, c = scatter_dims(b, inner), scatter_dims(c, y)
    b, second = lax.optimization_barrier((b, fillers[1]))
    b, c = scatter_dims(b, y), scatter_dims(c, inner)
    b, third = lax.optimization_barrier((b, fillers[2]))
    a = scatter_dims(a, inner + y + [z])
    pieces = [
        jnp.concatenate(both, axis=0)
        for both in zip(jnp.split(b, z[2], axis=0), jnp.split(c, z[2], axis=0))
    ]
    return jnp.concatenate([a, ring_scatter(pieces, z)], axis=0), (first, second, third)


def sum_cores(pair, n_blk, n_head):
    return ring_scatter(pair, split_dims(n_blk, n_head)[3])


def gather_two(x, n_blk, n_head):
    half = x.shape[0] // 2
    z, inner, y, core = split_dims(n_blk, n_head)
    pieces = direct_gather(x, z)
    b = gather_dims(jnp.concatenate([p[:half] for p in pieces], axis=0), y + inner)
    c = gather_dims(jnp.concatenate([p[half:] for p in pieces], axis=0), inner + y)
    return direct_gather(b, core), direct_gather(c, core)


def scatter_two(b, c, n_blk, n_head):
    z, inner, y, core = split_dims(n_blk, n_head)
    b = scatter_dims(direct_scatter(b, core), y + inner)
    c = scatter_dims(direct_scatter(c, core), inner + y)
    pieces = [
        jnp.concatenate(both, axis=0)
        for both in zip(jnp.split(b, z[2], axis=0), jnp.split(c, z[2], axis=0))
    ]
    return direct_scatter(pieces, z)


def scatter_blk(x, axis=0):
    return lax.psum_scatter(x, "blk", scatter_dimension=axis, tiled=True)


def head_lanes(heads, head):
    lane = lax.broadcasted_iota(jnp.int32, (1, heads * ROPE), 1) % (heads * ROPE // 2)
    return lane // (ROPE // 2) == head


def spread(heads):
    row = lax.broadcasted_iota(jnp.int32, (ROPE, heads * ROPE), 0)
    lane = lax.broadcasted_iota(jnp.int32, (ROPE, heads * ROPE), 1)
    width = heads * ROPE // 2
    return jnp.where(row == lane // width * (ROPE // 2) + lane % (ROPE // 2), 1.0, 0.0).astype(BF16)


def attention_kernel(
    heads, scale, at_ref, q_ref, lata_ref, latb_ref, up_ref, out_ref, lse_ref, m_ref, l_ref, acc_ref
):
    step = pl.program_id(0)

    @pl.when(step == 0)
    def _():
        m_ref[...] = jnp.full_like(m_ref, -1e30)
        l_ref[...] = jnp.zeros_like(l_ref)
        acc_ref[...] = jnp.zeros_like(acc_ref)

    @pl.when(step <= at_ref[0])
    def _():
        lat = both_cores(lata_ref, latb_ref)
        kv = dot(lat[:, :RANK], up_ref[...]).astype(BF16)
        rope = dot(lat[:, RANK : RANK + ROPE], spread(heads)).astype(BF16)
        query = q_ref[...].reshape(BLOCK, heads * (NOPE + ROPE))
        query_rope = query[:, heads * NOPE :]
        for h in range(heads):
            at = h * (NOPE + VALUE)
            scores = dot_nt(query[:, h * NOPE : (h + 1) * NOPE], kv[:, at : at + NOPE])
            masked = jnp.where(head_lanes(heads, h), query_rope, jnp.zeros_like(query_rope))
            scores = (scores + dot_nt(masked, rope)) * scale
            old = m_ref[h][:, :1]
            new = jnp.maximum(old, jnp.max(scores, axis=1, keepdims=True))
            expo = jnp.exp(scores - new)
            factor = jnp.exp(old - new)
            l_ref[h] = l_ref[h] * factor + jnp.sum(expo, axis=1, keepdims=True)
            acc_ref[h] = acc_ref[h] * factor + dot(expo.astype(BF16), kv[:, at + NOPE : at + NOPE + VALUE])
            m_ref[h] = jnp.broadcast_to(new, m_ref.shape[1:])

    @pl.when(step == pl.num_programs(0) - 1)
    def _():
        lane = lax.broadcasted_iota(jnp.int32, (BLOCK, 128), 1)
        lse = jnp.zeros((BLOCK, 128), F32)
        for h in range(heads):
            out = acc_ref[h] / l_ref[h]
            out_ref[:, :, :, h * VALUE : (h + 1) * VALUE] = out.astype(BF16).reshape(
                out_ref.shape[:3] + (VALUE,)
            )
            lse = jnp.where(lane == h, m_ref[h] + jnp.log(l_ref[h]), lse)
        lse_ref[...] = lse


def both_cores(first_ref, second_ref):
    flat = [ref[...].reshape(BLOCK // 2, ref.shape[-1]) for ref in (first_ref, second_ref)]
    return jnp.concatenate(flat, axis=0)


def key_specs(view, y_axis, clamp):
    n_blk = view[0] * view[1] * view[2] // view[y_axis]
    shape = tuple(n if i == y_axis else 1 if i < 3 else n for i, n in enumerate(view))

    def index(step, at):
        step = jnp.minimum(step, at[0]) if clamp else step
        inner, z = at[1 + step], at[1 + n_blk + step]
        return (0, inner, z, 0, 0) if y_axis == 0 else (inner, 0, z, 0, 0)

    return [pl.BlockSpec(shape, index)] * 2


def attention(at, seq, query, lats, up, y_axis, heads):
    n_head, own = query.shape[0], query.shape[2]
    n_blk = (at.shape[0] - 1) // 2
    scale = (NOPE + ROPE) ** -0.5
    row = lambda width, s: pl.BlockSpec((n_head, 1, own, width), lambda b, r: (0, s, 0, 0))
    return pl.pallas_call(
        functools.partial(attention_kernel, heads, scale),
        grid_spec=pltpu.PrefetchScalarGridSpec(
            num_scalar_prefetch=1,
            grid=(n_blk,),
            in_specs=[row(query.shape[3], seq)]
            + key_specs(lats[0].shape, y_axis, True)
            + [pl.BlockSpec(up.shape, lambda b, r: (0, 0))],
            out_specs=[row(heads * VALUE, 0), pl.BlockSpec((BLOCK, 128), lambda b, r: (0, 0))],
            scratch_shapes=[
                pltpu.VMEM((heads, BLOCK, 128), F32),
                pltpu.VMEM((heads, BLOCK, 128), F32),
                pltpu.VMEM((heads, BLOCK, VALUE), F32),
            ],
        ),
        out_shape=[
            jax.ShapeDtypeStruct((n_head, 1, own, heads * VALUE), BF16),
            jax.ShapeDtypeStruct((BLOCK, 128), F32),
        ],
        cost_estimate=pl.CostEstimate(
            flops=n_blk * BLOCK * 2 * (RANK * up.shape[1] + heads * BLOCK * 640),
            bytes_accessed=lats[0].size * 4 + up.size * 2 + query.size * 2,
            transcendentals=n_blk * heads * BLOCK * BLOCK,
        ),
        name="attention",
    )(at, query, *lats, up)


def attention_back_kernel(
    heads, scale, at_ref, q_ref, lata_ref, latb_ref, up_ref, att_ref, datt_ref, lse_ref, cos_ref, sin_ref,
    dq_ref, dlata_ref, dlatb_ref, dup_ref, delta_ref, dqn_ref, dqr_ref, up_acc,
):
    step = pl.program_id(0)
    last = pl.num_programs(0) - 1

    @pl.when(step == 0)
    def _():
        up_acc[...] = jnp.zeros_like(up_acc)

    @pl.when(step == 0)
    def _():
        dqn_ref[...] = jnp.zeros_like(dqn_ref)
        dqr_ref[...] = jnp.zeros_like(dqr_ref)
        prod = att_ref[...].astype(F32) * datt_ref[...].astype(F32)
        prod = prod.reshape(BLOCK, heads * VALUE)
        for h in range(heads):
            delta_ref[h] = jnp.broadcast_to(
                jnp.sum(prod[:, h * VALUE : (h + 1) * VALUE], axis=1, keepdims=True), (BLOCK, 128)
            )

    @pl.when(step <= at_ref[0])
    def _():
        lat = both_cores(lata_ref, latb_ref)
        latn = lat[:, :RANK]
        kv = dot(latn, up_ref[...]).astype(BF16)
        copies = spread(heads)
        rope = dot(lat[:, RANK : RANK + ROPE], copies).astype(BF16)
        query = q_ref[...].reshape(BLOCK, heads * (NOPE + ROPE))
        query_rope = query[:, heads * NOPE :]
        d_att = datt_ref[...].reshape(BLOCK, heads * VALUE)
        d_rope = jnp.zeros((BLOCK, heads * ROPE), F32)
        d_kv = []
        for h in range(heads):
            at = h * (NOPE + VALUE)
            lanes = head_lanes(heads, h)
            q_h = query[:, h * NOPE : (h + 1) * NOPE]
            k_h = kv[:, at : at + NOPE]
            d_h = d_att[:, h * VALUE : (h + 1) * VALUE]
            masked = jnp.where(lanes, query_rope, jnp.zeros_like(query_rope))
            scores = (dot_nt(q_h, k_h) + dot_nt(masked, rope)) * scale
            prob = jnp.exp(scores - lse_ref[:, h : h + 1])
            d_prob = dot_nt(d_h, kv[:, at + NOPE : at + NOPE + VALUE])
            d_score = (prob * (d_prob - delta_ref[h][:, :1]) * scale).astype(BF16)
            dqn_ref[h] = dqn_ref[h] + dot(d_score, k_h)
            dqr_ref[...] = dqr_ref[...] + jnp.where(lanes, dot(d_score, rope), 0.0)
            d_kv.append(dot_tn(d_score, q_h))
            d_kv.append(dot_tn(prob.astype(BF16), d_h))
            d_rope = d_rope + dot_tn(d_score, masked)
        d_kv = jnp.concatenate(d_kv, axis=1).astype(BF16)
        up_acc[...] += dot_tn(latn, d_kv)
        d_lat = dot_nt(d_kv, up_ref[...]).astype(BF16)
        d_key = dot_nt(d_rope.astype(BF16), copies).astype(BF16)
        for i, ref in enumerate((dlata_ref, dlatb_ref)):
            here = slice(i * (BLOCK // 2), (i + 1) * (BLOCK // 2))
            shape = ref.shape[:4]
            ref[:, :, :, :, :RANK] = d_lat[here].reshape(shape + (RANK,))
            ref[:, :, :, :, RANK : RANK + ROPE] = d_key[here].reshape(shape + (ROPE,))
            ref[:, :, :, :, RANK + ROPE :] = jnp.zeros(shape + (ref.shape[4] - RANK - ROPE,), BF16)

    @pl.when(step > at_ref[0])
    def _():
        dlata_ref[...] = jnp.zeros_like(dlata_ref)
        dlatb_ref[...] = jnp.zeros_like(dlatb_ref)

    @pl.when(step == last)
    def _():
        shape = dq_ref.shape[:3]
        for h in range(heads):
            dq_ref[:, :, :, h * NOPE : (h + 1) * NOPE] = dqn_ref[h].astype(BF16).reshape(shape + (NOPE,))
        half = heads * ROPE // 2
        cosine, sine = cos_ref[...], sin_ref[...]
        first, second = dqr_ref[:, :half], dqr_ref[:, half:]
        at = heads * NOPE
        dq_ref[:, :, :, at : at + half] = (first * cosine + second * sine).astype(BF16).reshape(shape + (half,))
        dq_ref[:, :, :, at + half :] = (second * cosine - first * sine).astype(BF16).reshape(shape + (half,))

    @pl.when(step == last)
    def _():
        dup_ref[...] = up_acc[...]


def attention_back(at, seq, query, lats, up, att, d_att, lse, cosine, sine, y_axis, heads):
    n_head, own = query.shape[0], query.shape[2]
    n_blk = (at.shape[0] - 1) // 2
    scale = (NOPE + ROPE) ** -0.5
    row = lambda width, s: pl.BlockSpec((n_head, 1, own, width), lambda b, r: (0, s, 0, 0))
    whole = lambda x: pl.BlockSpec(x.shape, lambda b, r: (0, 0))
    half = heads * ROPE // 2
    return pl.pallas_call(
        functools.partial(attention_back_kernel, heads, scale),
        grid_spec=pltpu.PrefetchScalarGridSpec(
            num_scalar_prefetch=1,
            grid=(n_blk,),
            in_specs=[row(query.shape[3], seq)]
            + key_specs(lats[0].shape, y_axis, True)
            + [whole(up), row(heads * VALUE, 0), row(heads * VALUE, seq)]
            + [whole(lse), whole(cosine), whole(sine)],
            out_specs=[row(query.shape[3], 0)] + key_specs(lats[0].shape, y_axis, False) + [whole(up)],
            scratch_shapes=[
                pltpu.VMEM((heads, BLOCK, 128), F32),
                pltpu.VMEM((heads, BLOCK, NOPE), F32),
                pltpu.VMEM((BLOCK, 2 * half), F32),
                pltpu.VMEM(up.shape, F32),
            ],
        ),
        out_shape=[
            jax.ShapeDtypeStruct((n_head, 1, own, query.shape[3]), BF16),
            jax.ShapeDtypeStruct(lats[0].shape, BF16),
            jax.ShapeDtypeStruct(lats[0].shape, BF16),
            jax.ShapeDtypeStruct(up.shape, F32),
        ],
        cost_estimate=pl.CostEstimate(
            flops=n_blk * BLOCK * 2 * (3 * RANK * up.shape[1] + heads * BLOCK * 1700),
            bytes_accessed=lats[0].size * 8 + up.size * 6 + query.size * 4,
            transcendentals=n_blk * heads * BLOCK * BLOCK,
        ),
        name="attention_back",
    )(at, query, *lats, up, att, d_att, lse, cosine, sine)


def pick(own, first_ref, second_ref, out_ref):
    @pl.when(own)
    def _():
        out_ref[...] = first_ref[...]

    @pl.when(jnp.logical_not(own))
    def _():
        out_ref[...] = second_ref[...]


def put(own, value_ref, first_ref, second_ref):
    @pl.when(own)
    def _():
        first_ref[...] = value_ref[...]

    @pl.when(jnp.logical_not(own))
    def _():
        second_ref[...] = value_ref[...]


def gate_lanes(tail, base, local):
    lane = lax.broadcasted_iota(jnp.int32, tail.shape, 1)
    tail = tail.astype(F32)
    return [
        jnp.sum(jnp.where(lane == base + e, tail, 0.0), axis=1, keepdims=True) for e in range(local)
    ]


def spans(size, step):
    return [(at, min(step, size - at)) for at in range(0, size, step)]


def experts_kernel(
    units, local, base_ref, xa_ref, xb_ref, ta_ref, tb_ref, win_ref, wout_ref,
    x_ref, gu_ref, outa_ref, outb_ref, tail_ref, act_ref, sum_ref,
):
    own = pl.program_id(0) < pl.num_programs(0) // 2
    pick(own, xa_ref, xb_ref, x_ref)
    pick(own, ta_ref, tb_ref, tail_ref)
    gates = gate_lanes(tail_ref[...], base_ref[0], local)
    padded = wout_ref.shape[0]
    for at, size in spans(padded, 256):
        gate = dot(x_ref[...], win_ref[:, at : at + size])
        up = dot(x_ref[...], win_ref[:, padded + at : padded + at + size])
        gu_ref[:, at : at + size] = gate.astype(BF16)
        gu_ref[:, padded + at : padded + at + size] = up.astype(BF16)
        act = gate * jax.nn.sigmoid(gate) * up
        for here in range(0, size, 128):
            expert = (at + here) // units
            part = act[:, here : here + 128]
            part = part * gates[expert] if expert < local else part
            act_ref[:, at + here : at + here + 128] = part.astype(BF16)
    for at, size in spans(wout_ref.shape[1], 512):
        sum_ref[:, at : at + size] = dot(act_ref[...], wout_ref[:, at : at + size]).astype(BF16)
    put(own, sum_ref, outa_ref, outb_ref)


def half_specs(tile, steps, width, column=0):
    half = steps // 2
    return [
        pl.BlockSpec((tile, width), lambda i, r: (jnp.minimum(i, half - 1), column)),
        pl.BlockSpec((tile, width), lambda i, r: (jnp.maximum(i - half, 0), column)),
    ]


def tile_of(rows):
    return max(t for t in range(16, 385, 16) if rows % t == 0)


def resident(x):
    return pl.BlockSpec(x.shape, lambda i, r: (0, 0), pipeline_mode=pl.Buffered(1))


def run_experts(base, pair, win, wout, units, local):
    half, width, padded = pair[0].shape[0], wout.shape[1], wout.shape[0]
    tile = tile_of(half)
    steps = 2 * half // tile
    row = lambda size: pl.BlockSpec((tile, size), lambda i, r: (i, 0))
    rows = 2 * half
    shape = lambda count, size: jax.ShapeDtypeStruct((count, size), BF16)
    return pl.pallas_call(
        functools.partial(experts_kernel, units, local),
        grid_spec=pltpu.PrefetchScalarGridSpec(
            num_scalar_prefetch=1,
            grid=(steps,),
            in_specs=half_specs(tile, steps, width)
            + half_specs(tile, steps, 128, width // 128)
            + [resident(win), resident(wout)],
            out_specs=[row(width), row(2 * padded)] + half_specs(tile, steps, width),
            scratch_shapes=[
                pltpu.VMEM((tile, 128), BF16),
                pltpu.VMEM((tile, padded), BF16),
                pltpu.VMEM((tile, width), BF16),
            ],
        ),
        out_shape=[shape(rows, width), shape(rows, 2 * padded), shape(half, width), shape(half, width)],
        cost_estimate=pl.CostEstimate(
            flops=rows * width * padded * 6,
            bytes_accessed=(rows * (3 * width + 2 * padded) + 3 * width * padded) * 2,
            transcendentals=rows * padded,
        ),
        name="experts",
    )(base, *pair, *pair, win, wout)


def experts_back_kernel(
    units, local, base_ref, ga_ref, gb_ref, ta_ref, tb_ref, gu_ref, win_ref, wout_ref,
    hid_ref, act_ref, g_ref, outa_ref, outb_ref, tail_ref, sum_ref,
):
    own = pl.program_id(0) < pl.num_programs(0) // 2
    pick(own, ga_ref, gb_ref, g_ref)
    pick(own, ta_ref, tb_ref, tail_ref)
    gates = gate_lanes(tail_ref[...], base_ref[0], local)
    padded, width = wout_ref.shape
    prods = [jnp.zeros(tail_ref.shape, F32) for _ in range(local)]
    for at, size in spans(padded, 256):
        d_acts = dot_nt(g_ref[...], wout_ref[at : at + size, :])
        for here in range(0, size, 128):
            unit = at + here
            expert = unit // units
            d_act = d_acts[:, here : here + 128]
            gate = gu_ref[:, unit : unit + 128].astype(F32)
            up = gu_ref[:, padded + unit : padded + unit + 128].astype(F32)
            sig = jax.nn.sigmoid(gate)
            silu = gate * sig
            act = silu * up
            if expert < local:
                prods[expert] = prods[expert] + act * d_act
                d_act = d_act * gates[expert]
                act = act * gates[expert]
            hid_ref[:, unit : unit + 128] = (d_act * up * (sig + silu * (1.0 - sig))).astype(BF16)
            hid_ref[:, padded + unit : padded + unit + 128] = (d_act * silu).astype(BF16)
            act_ref[:, unit : unit + 128] = act.astype(BF16)
    for at, size in spans(width, 256):
        sum_ref[:, at : at + size] = dot_nt(hid_ref[...], win_ref[at : at + size, :]).astype(BF16)
    lane = lax.broadcasted_iota(jnp.int32, tail_ref.shape, 1)
    extra = jnp.zeros(tail_ref.shape, F32)
    for e in range(local):
        extra = jnp.where(lane == base_ref[0] + e, jnp.sum(prods[e], axis=1, keepdims=True), extra)
    sum_ref[:, width:] = extra.astype(BF16)
    put(own, sum_ref, outa_ref, outb_ref)


def run_experts_back(base, grads, pair, gu, win, wout, units, local):
    half, width, padded = grads[0].shape[0], wout.shape[1], wout.shape[0]
    tile = tile_of(half)
    steps = 2 * half // tile
    row = lambda size: pl.BlockSpec((tile, size), lambda i, r: (i, 0))
    rows = 2 * half
    shape = lambda count, size: jax.ShapeDtypeStruct((count, size), BF16)
    return pl.pallas_call(
        functools.partial(experts_back_kernel, units, local),
        grid_spec=pltpu.PrefetchScalarGridSpec(
            num_scalar_prefetch=1,
            grid=(steps,),
            in_specs=half_specs(tile, steps, width)
            + half_specs(tile, steps, 128, width // 128)
            + [row(2 * padded), resident(win), resident(wout)],
            out_specs=[row(2 * padded), row(padded), row(width)] + half_specs(tile, steps, width + 128),
            scratch_shapes=[pltpu.VMEM((tile, 128), BF16), pltpu.VMEM((tile, width + 128), BF16)],
        ),
        out_shape=[
            shape(rows, 2 * padded), shape(rows, padded), shape(rows, width),
            shape(half, width + 128), shape(half, width + 128),
        ],
        cost_estimate=pl.CostEstimate(
            flops=rows * width * padded * 6,
            bytes_accessed=(rows * (3 * width + 5 * padded) + 3 * width * padded) * 2,
            transcendentals=rows * padded,
        ),
        name="experts_back",
    )(base, *grads, *pair, gu, win, wout)


def on_device(
    states, teacher, valid, routes, norm_in, w_query, w_down_kv, norm_kv, w_up_kv, w_out, norm_ffn,
    w_router, shared_in, shared_out, expert_in, expert_out,
):
    n_blk, n_head = lax.axis_size("blk"), lax.axis_size("head")
    blk, head = lax.axis_index("blk"), lax.axis_index("head")
    own_pos, seqs, width = states.shape
    block_pos = own_pos * n_head
    rows = own_pos * seqs
    block_rows = rows * n_head
    total_rows = block_rows * n_blk
    experts = w_router.shape[1]
    local = expert_in.shape[0]
    eff = expert_in.shape[3]
    shared = shared_in.shape[2] // n_blk
    heads = w_query.shape[1] // (NOPE + ROPE)
    scale = (NOPE + ROPE) ** (-0.5)
    assert block_pos == BLOCK and seqs == 2
    blks, heads_ring = blk_dims(n_blk), head_dims(n_head)

    def gather_head(x):
        return gather_axis(x, heads_ring).reshape((-1,) + x.shape[1:])

    def scatter_head(x):
        return scatter_axis(x.reshape((n_head, -1) + x.shape[1:]), heads_ring)

    def take_own(x):
        own = lax.dynamic_slice_in_dim(x, head * own_pos, own_pos, 0)
        return jnp.moveaxis(own, 1, 0).reshape((rows,) + x.shape[2:])

    part = width // n_blk
    quarter = part // n_head
    lat_width = RANK + ROPE
    small = jnp.concatenate(
        [norm_in, norm_ffn, w_router.reshape(-1), norm_kv, jnp.sum(valid, axis=1).astype(BF16)]
    )
    lines = -(-small.shape[0] // lat_width // 16) * 16
    small = jnp.pad(small, (0, lines * lat_width - small.shape[0])).reshape(lines, lat_width)
    down = lax.dynamic_slice_in_dim(w_down_kv, head * quarter, quarter, 0)
    down = gather_axis(jnp.concatenate([down, small], axis=0), blks)
    small = down[:, quarter:].reshape(n_blk, -1)
    down = jnp.moveaxis(gather_axis(down[:, :quarter], heads_ring), 0, 1).reshape(width, lat_width)
    lanes = heads * ROPE // 2
    wq = w_query.reshape(part, heads, NOPE + ROPE)
    wq = jnp.concatenate(
        [
            wq[:, :, :NOPE].reshape(part, -1),
            wq[:, :, NOPE : NOPE + ROPE // 2].reshape(part, -1),
            wq[:, :, NOPE + ROPE // 2 :].reshape(part, -1),
        ],
        axis=1,
    )
    most = part * 3 // 4
    wq_most = gather_dims(wq[None, :most], blks[:1])
    wq_rest = gather_dims(wq[None, most:], blks[:0:-1])
    states_blk = gather_head(jnp.moveaxis(states, 1, 0).reshape(rows, width))
    down, wq_most, wq_rest = lax.optimization_barrier((down, wq_most, wq_rest))
    wq_most = in_order(gather_dims(wq_most, blks[1:]), blks)
    wq_rest = in_order(gather_dims(wq_rest, blks[:1]), blks[::-1])
    wq = jnp.concatenate([wq_most, wq_rest], axis=1).reshape(width, -1)
    gain_in = small[:, :part].reshape(-1).astype(F32)
    gain_ffn = small[:, part : 2 * part].reshape(-1).astype(F32)
    at = 2 * part
    router = small[:, at : at + part * experts].reshape(width, experts)
    at += part * experts
    gain_kv = small[:, at : at + RANK // n_blk].reshape(-1).astype(F32)
    at += RANK // n_blk
    count = jnp.sum(small[:, at : at + block_pos].astype(F32))
    up_out = jnp.concatenate([w_up_kv, w_out.reshape(-1, w_up_kv.shape[1])], axis=0)
    up_out = lax.all_gather(up_out, "blk", axis=0)
    wup = up_out[:, : w_up_kv.shape[0]].reshape(RANK, -1)
    wo = jnp.moveaxis(up_out[:, w_up_kv.shape[0] :].reshape((n_blk,) + w_out.shape), 0, 1).reshape(-1, width)

    pieces = jnp.concatenate(
        [
            jnp.transpose(shared_in.reshape(part, 2, n_blk, shared), (2, 1, 3, 0)).reshape(
                n_blk, 2 * shared, part
            ),
            shared_out.reshape(n_blk, shared, part),
        ],
        axis=1,
    )
    pieces = lax.all_to_all(pieces, "blk", split_axis=0, concat_axis=0, tiled=True)
    sh_in = jnp.transpose(pieces[:, : 2 * shared], (0, 2, 1)).reshape(width, 2, shared)
    sh_out = jnp.transpose(pieces[:, 2 * shared :], (1, 0, 2)).reshape(shared, width)
    units = -(-eff // 128) * 128
    shared_units = -(-shared // 128) * 128
    padded = local * units + shared_units
    wide = lambda x, size: jnp.pad(x, ((0, 0), (0, size - x.shape[1])))
    win = jnp.concatenate(
        [
            block
            for side in range(2)
            for block in [wide(expert_in[e, :, side], units) for e in range(local)]
            + [wide(sh_in[:, side], shared_units)]
        ],
        axis=1,
    )
    wout = jnp.concatenate(
        [jnp.pad(expert_out, ((0, 0), (0, units - eff), (0, 0))).reshape(-1, width)]
        + [jnp.pad(sh_out, ((0, shared_units - shared), (0, 0)))],
        axis=0,
    )

    x_own = jnp.moveaxis(states, 1, 0).reshape(rows, width).astype(F32)
    h1_f, rstd_in = normed(x_own, gain_in)
    h1_own = h1_f.astype(BF16)
    h1_blk = normed(states_blk.astype(F32), gain_in)[0].astype(BF16)
    pos_own = blk * block_pos + head * own_pos + jnp.arange(own_pos, dtype=jnp.int32)
    table_own = jnp.tile(angles(pos_own), (seqs, 1))
    pos_blk = blk * block_pos + jnp.arange(block_pos, dtype=jnp.int32)
    table_seq = angles(pos_blk)
    cos_seq, sin_seq = (jnp.tile(f(table_seq), (1, heads)) for f in (jnp.cos, jnp.sin))
    table_blk = jnp.broadcast_to(
        angles(pos_blk).reshape(n_head, 1, own_pos, ROPE // 2), (n_head, seqs, own_pos, ROPE // 2)
    ).reshape(block_rows, ROPE // 2)
    lat = dot(h1_own, down)
    lat_c = lat[:, :RANK]
    latn_f, rstd_kv = normed(lat_c, gain_kv)
    payload = jnp.concatenate(
        [latn_f, rotate(lat[:, RANK:], table_own), jnp.zeros((rows, 128 - ROPE), F32)], axis=1
    ).astype(BF16)
    z, inner, y, _ = split_dims(n_blk, n_head)
    order = [z[2], y[0][2], n_blk // z[2]]
    lats = gather_two(by_rows(payload), n_blk, n_head)
    lats = [
        [x.reshape(tuple(shape) + (own_pos, -1)) for x in pair]
        for pair, shape in zip(lats, ([order[2], order[1], order[0]], [order[1], order[2], order[0]]))
    ]
    key_blocks = jnp.arange(n_blk, dtype=jnp.int32)
    key_at = jnp.concatenate(
        [jnp.full((1,), blk, jnp.int32), relative(inner, key_blocks) + 0 * key_blocks, relative([z], key_blocks)]
    ).astype(jnp.int32)
    wq, win, wout = lax.optimization_barrier((wq, win, wout))
    query = dot(h1_blk, wq)
    cosine = jnp.tile(jnp.cos(table_blk), (1, heads))
    sine = jnp.tile(jnp.sin(table_blk), (1, heads))
    q_first, q_second = query[:, -2 * lanes : -lanes], query[:, -lanes:]
    query = jnp.concatenate(
        [query[:, : -2 * lanes], q_first * cosine - q_second * sine, q_second * cosine + q_first * sine],
        axis=1,
    ).astype(BF16)
    shape4 = (n_head, seqs, own_pos, -1)
    query = query.reshape(shape4)
    seq_axes = list(zip(range(seqs), lats, (1, 0)))
    att_seqs, lses = zip(*(attention(key_at, s, query, pair, wup, axis, heads) for s, pair, axis in seq_axes))
    att_rows = jnp.concatenate(att_seqs, axis=1).reshape(block_rows, heads * VALUE)
    y_own = x_own + scatter_head(dot(att_rows, wo).astype(BF16)).astype(F32)
    h2_f, rstd_ffn = normed(y_own, gain_ffn)
    h2_own = h2_f.astype(BF16)

    routes_own = take_own(routes)
    mask = jnp.any(routes_own[:, :, None] == jnp.arange(experts, dtype=jnp.int32), axis=1)
    logits = jnp.where(mask, dot(h2_own, router), -1e30)
    gates = jnp.where(mask, jnp.exp(logits - jnp.max(logits, axis=1, keepdims=True)), 0.0)
    gates = gates / jnp.sum(gates, axis=1, keepdims=True)
    assert experts <= 128
    tail = jnp.zeros((rows, 128 - experts), BF16)
    base = jnp.full((1,), blk * local, jnp.int32)
    x_ext = jnp.concatenate([h2_own, gates.astype(BF16), tail], axis=1)
    rounds = max(1, total_rows // 4096)

    def in_turn(run, parts):
        outs, sums = [], []
        for i, part in enumerate(parts):
            if i == 2:
                sums[0], part = lax.optimization_barrier((sums[0], part))
            outs.append(run(*part))
            sums.append(sum_cores(outs[-1][-2:], n_blk, n_head))
        return outs, sums

    def forward(x_rows):
        pairs = gather_parts(x_rows, n_blk, n_head)
        outs, sums = in_turn(
            lambda pair: run_experts(base, pair, win, wout, units, local), [(pair,) for pair in pairs]
        )
        kept = [(pair, x, gu) for pair, (x, gu, _, _) in zip(pairs, outs)]
        return kept, scatter_parts(sums, ((), (), ()), n_blk, n_head)[0]

    def backward(grad_rows, kept):
        outs, sums = in_turn(
            lambda grads, pair, gu: run_experts_back(base, grads, pair, gu, win, wout, units, local),
            [(grads, pair, gu) for grads, (pair, _, gu) in zip(gather_parts(grad_rows, n_blk, n_head), kept)],
        )
        (x_b, x_c, x_a) = (x for _, x, _ in kept)
        (hid_b, act_b, grad_b, hid_c, act_c, grad_c, hid_a, act_a, grad_a) = (v for out in outs for v in out[:3])
        back, (first, second, third) = scatter_parts(
            sums,
            ((x_b, hid_b, act_b, grad_b), (x_c, hid_c), (act_c, grad_c, x_a, hid_a, act_a, grad_a)),
            n_blk, n_head,
        )
        x_b, hid_b, act_b, grad_b = first
        x_c, hid_c = second
        act_c, grad_c, x_a, hid_a, act_a, grad_a = third
        d_win = dot_tn(x_b, hid_b) + dot_tn(x_c, hid_c) + dot_tn(x_a, hid_a)
        d_wout = dot_tn(act_b, grad_b) + dot_tn(act_c, grad_c) + dot_tn(act_a, grad_a)
        return back, d_win, d_wout

    def in_rounds(x):
        return x.reshape((rounds, -1) + x.shape[1:])

    if rounds == 1:
        kept, mixed = forward(x_ext)
    else:
        mixed = lax.map(lambda x: forward(x)[1], in_rounds(x_ext)).reshape(rows, width)
    mixed = mixed.astype(F32)
    out_own = (y_own + mixed).astype(BF16)
    diff = out_own.astype(F32) - take_own(teacher).astype(F32)
    valid_own = take_own(valid).astype(F32)[:, None]
    loss_part = jnp.sum(valid_own * diff * diff)
    grad_own = diff * valid_own * (total_rows / count)

    grad_own_b = grad_own.astype(BF16)
    if rounds == 1:
        back, d_win, d_wout = backward(grad_own_b, kept)
    else:

        def round_back(sums, both):
            kept, _ = forward(both[0])
            back, d_win, d_wout = backward(both[1], kept)
            return (sums[0] + d_win, sums[1] + d_wout), back

        start = (jnp.zeros((width, 2 * padded), F32), jnp.zeros((padded, width), F32))
        (d_win, d_wout), back = lax.scan(round_back, start, (in_rounds(x_ext), in_rounds(grad_own_b)))
        back = back.reshape(rows, -1)
    d_sh = jnp.concatenate(
        [d_win[:, s * padded + local * units :][:, :shared].T for s in range(2)]
        + [d_wout[local * units :][:shared]],
        axis=0,
    ).astype(BF16)
    d_sh = jnp.transpose(d_sh.reshape(3 * shared, n_blk, part), (1, 0, 2))
    back, d_win, d_wout, d_sh = lax.optimization_barrier((back, d_win, d_wout, d_sh))
    back = back.astype(F32)
    d_sh = lax.all_to_all(d_sh, "blk", split_axis=0, concat_axis=0, tiled=True).astype(F32)
    grad_shin = jnp.transpose(d_sh[:, : 2 * shared].reshape(n_blk, 2, shared, part), (3, 1, 0, 2)).reshape(
        part, 2, n_blk * shared
    )
    grad_shout = d_sh[:, 2 * shared :].reshape(n_blk * shared, part)

    d_gates = back[:, width : width + experts]
    d_logits = gates * (d_gates - jnp.sum(gates * d_gates, axis=1, keepdims=True))
    d_logits = d_logits.astype(BF16)
    grad_router = dot_tn(h2_own, d_logits)
    dh2 = back[:, :width] + dot_nt(d_logits, router)
    dy_branch, grad_gain_ffn = norm_back(dh2, y_own, rstd_ffn, gain_ffn)
    dy_own = grad_own + dy_branch

    dy_blk = gather_head(dy_own.astype(BF16))
    grad_wo = dot_tn(att_rows, dy_blk).astype(BF16)
    d_att = dot_nt(dy_blk, wo).astype(BF16).reshape(shape4)
    grad_wo, d_att = lax.optimization_barrier((grad_wo, d_att))
    grad_wo = scatter_blk(grad_wo, 1).astype(F32)
    dqs, d_lats, d_ups = [], [], []
    for (s, pair, axis), att, lse in zip(seq_axes, att_seqs, lses):
        dq, first, second, d_up = attention_back(
            key_at, s, query, pair, wup, att, d_att, lse, cos_seq, sin_seq, axis, heads
        )
        dqs.append(dq)
        d_lats.append([x.reshape(total_rows // 4, -1) for x in (first, second)])
        d_ups.append(d_up)
    dq = jnp.concatenate(dqs, axis=1)
    d_up = sum(d_ups).astype(BF16)
    dq, d_win, d_wout = lax.optimization_barrier((dq, d_win, d_wout))
    grad_ein = jnp.stack(
        [
            jnp.stack([d_win[:, s * padded + e * units :][:, :eff] for s in range(2)], axis=1)
            for e in range(local)
        ]
    )
    grad_eout = d_wout[: local * units].reshape(local, units, width)[:, :eff]
    d_lat = by_rows(scatter_two(*d_lats, n_blk, n_head))[:, : RANK + ROPE].astype(F32)
    dq = dq.reshape(block_rows, -1)
    dh1 = scatter_head(dot_nt(dq, wq).astype(BF16)).astype(F32)
    grad_wq = dot_tn(h1_blk, dq).astype(BF16).reshape(n_blk, -1, d_up.shape[1])
    joined = jnp.concatenate([grad_wq, d_up.reshape(n_blk, -1, d_up.shape[1])], axis=1)
    joined, grad_wo = lax.optimization_barrier((joined, grad_wo))
    joined = lax.psum_scatter(joined, "blk", scatter_dimension=0, tiled=False).astype(F32)
    grad_wq = joined[: grad_wq.shape[1]].reshape(part, -1)
    grad_up = joined[joined.shape[0] - w_up_kv.shape[0] :]
    grad_wq = jnp.concatenate(
        [
            grad_wq[:, : heads * NOPE].reshape(part, heads, NOPE),
            grad_wq[:, heads * NOPE : -lanes].reshape(part, heads, ROPE // 2),
            grad_wq[:, -lanes:].reshape(part, heads, ROPE // 2),
        ],
        axis=2,
    ).reshape(part, -1)
    d_lat_c, grad_gain_kv = norm_back(d_lat[:, :RANK], lat_c, rstd_kv, gain_kv)
    d_lat_b = jnp.concatenate([d_lat_c, rotate(d_lat[:, RANK : RANK + ROPE], -table_own)], axis=1).astype(BF16)
    d_lat_b = by_rows(d_lat_b)
    d_lat_blk = gather_head(d_lat_b)
    h1_part = lax.dynamic_slice_in_dim(
        h1_blk.reshape(block_rows, n_blk, n_head, quarter), head, 1, 2
    ).reshape(block_rows, -1)
    grad_down = dot_tn(h1_part, d_lat_blk).astype(BF16).reshape(n_blk, quarter, -1)
    grad_down = gather_head(scatter_axis(grad_down, blks)).astype(F32)
    dh1 = dh1 + dot_nt(d_lat_b, down)
    dx_branch, grad_gain_in = norm_back(dh1, x_own, rstd_in, gain_in)
    dx_own = dy_own + dx_branch

    loss_high = loss_part.astype(BF16).astype(F32)
    sums = jnp.concatenate(
        [
            grad_gain_in.reshape(n_blk, -1),
            grad_gain_ffn.reshape(n_blk, -1),
            grad_router.reshape(n_blk, -1),
            grad_gain_kv.reshape(n_blk, -1),
            jnp.full((n_blk, 1), loss_high),
            jnp.full((n_blk, 1), loss_part - loss_high),
        ],
        axis=1,
    )
    sums = scatter_axis(sums, blks)
    for dim in heads_ring:
        sums = sum(ring_gather(sums, dim))
    out_gain_in = sums[:part]
    out_gain_ffn = sums[part : 2 * part]
    at = 2 * part
    out_router = sums[at : at + part * experts].reshape(part, experts)
    at += part * experts
    out_gain_kv = sums[at : at + RANK // n_blk]
    loss = (sums[-2] + sums[-1]) / (width * count)

    def give(x):
        return jnp.moveaxis(x.reshape(seqs, own_pos, width), 0, 1)

    return (
        give(out_own), loss, give(dx_own), out_gain_in, grad_wq, grad_down, out_gain_kv, grad_up,
        grad_wo, out_gain_ffn, out_router, grad_shin, grad_shout, grad_ein, grad_eout,
    )


def solution(mesh):
    in_specs = (
        P(BOTH, None, None), P("blk", None, None), P("blk", None), P("blk", None, None), P("blk"),
        P("blk", "head"), P("blk", None), P("blk"), P("blk", "head"), P("head", "blk"), P("blk"),
        P("blk", None), P("blk", None, "head"), P("head", "blk"), P("blk", None, None, "head"),
        P("blk", "head", None),
    )
    out_specs = (
        P(BOTH, None, None), P(), P(BOTH, None, None), P("blk"), P("blk", "head"), P("blk", None),
        P("blk"), P("blk", "head"), P("head", "blk"), P("blk"), P("blk", None), P("blk", None, "head"),
        P("head", "blk"), P("blk", None, None, "head"), P("blk", "head", None),
    )
    return jax.shard_map(on_device, mesh=mesh, in_specs=in_specs, out_specs=out_specs, check_vma=False)
```

```python
import functools

import jax
import jax.numpy as jnp
from jax import lax
from jax.experimental import pallas as pl
from jax.experimental.layout import Layout, with_layout_constraint
from jax.experimental.pallas import tpu as pltpu
from jax.sharding import PartitionSpec as P

NOPE = 128
ROPE = 64
VALUE = 128
RANK = 512
BLOCK = 256
EPS = 1e-06
F32 = jnp.float32
BF16 = jnp.bfloat16
BOTH = ("blk", "head")


def angles(position):
    frequency = 10000.0 ** (-2.0 * jnp.arange(ROPE // 2, dtype=F32) / ROPE)
    return position.astype(F32)[:, None] * frequency[None, :]


def rotate(values, table):
    half = ROPE // 2
    cosine, sine = jnp.cos(table), jnp.sin(table)
    first, second = values[:, :half], values[:, half:]
    return jnp.concatenate([first * cosine - second * sine, second * cosine + first * sine], axis=1)


def normed(values, gain):
    rstd = lax.rsqrt(jnp.mean(values * values, axis=-1, keepdims=True) + EPS)
    return values * rstd * gain, rstd


def norm_back(grad, values, rstd, gain):
    scaled = grad * gain
    out = rstd * scaled - values * rstd**3 * jnp.mean(scaled * values, axis=-1, keepdims=True)
    return out, jnp.sum(grad * values * rstd, axis=0)


def by_rows(x):
    return with_layout_constraint(x, Layout(tuple(range(x.ndim))))


def dot(a, b):
    return jnp.dot(a, b, preferred_element_type=F32)


def dot_nt(a, b):
    return lax.dot_general(a, b, (((1,), (1,)), ((), ())), preferred_element_type=F32)


def dot_tn(a, b):
    return lax.dot_general(a, b, (((0,), (0,)), ((), ())), preferred_element_type=F32)


def blk_dims(n_blk):
    if n_blk == 8:
        return [("blk", 2, 4), ("blk", 1, 2)]
    if n_blk == 32:
        return [("blk", 8, 4), ("blk", 2, 4), ("blk", 1, 2)]
    return [("blk", 1, n_blk)]


def head_dims(n_head):
    return [("head", 2, n_head // 2), ("head", 1, 2)] if n_head % 2 == 0 else [("head", 1, n_head)]


def shift(x, dim, by):
    axis, stride, size = dim
    pairs = []
    for i in range(lax.axis_size(axis)):
        digit = i // stride % size
        pairs.append((i, i + ((digit + by) % size - digit) * stride))
    return lax.ppermute(x, axis, pairs)


def digit_of(dim):
    axis, stride, size = dim
    return lax.axis_index(axis) // stride % size


def ring_gather(x, dim):
    pieces = [x]
    for _ in range(dim[2] - 1):
        pieces.append(shift(pieces[-1], dim, -1))
    return pieces


def ring_scatter(pieces, dim):
    total = pieces[-1]
    for piece in pieces[-2::-1]:
        total = shift(total, dim, 1) + piece
    return total


def direct_gather(x, dim):
    return [x] + [shift(x, dim, -k) for k in range(1, dim[2])]


def direct_scatter(pieces, dim):
    total = pieces[0].astype(F32)
    for k in range(1, dim[2]):
        total = total + shift(pieces[k], dim, k).astype(F32)
    return total.astype(pieces[0].dtype)


def gather_dims(x, dims, step=ring_gather):
    for dim in dims:
        x = jnp.concatenate(step(x, dim), axis=0)
    return x


def scatter_dims(x, dims, step=ring_scatter):
    for dim in reversed(dims):
        x = step(jnp.split(x, dim[2], axis=0), dim)
    return x


def relative(dims, index):
    place, scale = 0, 1
    for dim in dims:
        place = place + (index // dim[1] % dim[2] - digit_of(dim)) % dim[2] * scale
        scale *= dim[2]
    return place


def absolute(dims, place):
    index = 0
    for dim in dims:
        index = index + (place % dim[2] + digit_of(dim)) % dim[2] * dim[1]
        place //= dim[2]
    return index


def gather_axis(x, dims):
    return in_order(gather_dims(x[None], dims, direct_gather), dims)


def in_order(stack, dims):
    n = stack.shape[0]
    return jnp.concatenate(
        [lax.dynamic_slice_in_dim(stack, relative(dims, i), 1, 0) for i in range(n)], axis=0
    )


def scatter_axis(x, dims):
    n = lax.axis_size(dims[0][0])
    stack = jnp.concatenate(
        [lax.dynamic_slice_in_dim(x, absolute(dims, i), 1, 0) for i in range(n)], axis=0
    )
    return scatter_dims(stack, dims, direct_scatter)[0]


def split_dims(n_blk, n_head):
    blk, head = blk_dims(n_blk), head_dims(n_head)
    return blk[0], blk[1:], head[:-1], head[-1]


phase = lax.optimization_barrier


def no_fill(values):
    return values


def gather_parts(x, n_blk, n_head, fill=no_fill, fill_in=()):
    third = x.shape[0] * 5 // 16
    first = x.shape[0] - 2 * third
    z, inner, y, core = split_dims(n_blk, n_head)
    a, pieces = x[:first], [x[first:]]
    for dims in [inner, y] + [[]] * (z[2] - 4):
        piece, a = phase((shift(pieces[-1], z, -1), gather_dims(a, dims)))
        pieces.append(piece)
    pieces.append(shift(pieces[-1], z, -1))
    b = jnp.concatenate([p[:third] for p in pieces], axis=0)
    c = jnp.concatenate([p[third:] for p in pieces], axis=0)
    b, c, a = phase((b, c, a))
    b, c, last, fill_in = phase((gather_dims(b, y), gather_dims(c, inner), shift(a, z, -1), fill_in))
    pieces = [a, last]
    for _ in range(z[2] - 2):
        pieces.append(shift(pieces[-1], z, -1))
    b, c, pieces, filled = phase((gather_dims(b, inner), gather_dims(c, y), pieces, fill(fill_in)))
    return [ring_gather(part, core) for part in (b, c, jnp.concatenate(pieces, axis=0))], filled


def scatter_parts(sums, n_blk, n_head, fills=(no_fill,) * 3, fill_ins=((),) * 3):
    z, inner, y, _ = split_dims(n_blk, n_head)
    b, c, a, filled = phase((*sums, fill_ins[0]))
    pieces = jnp.split(a, z[2], axis=0)
    a = ring_scatter(pieces[1:], z)
    b, c, a, filled, fill_in = phase(
        (scatter_dims(b, inner), scatter_dims(c, y), a, fills[0](filled), fill_ins[1])
    )
    outs = [filled]
    a = shift(a, z, 1) + pieces[0]
    b, c, a, filled, fill_in = phase(
        (scatter_dims(b, y), scatter_dims(c, inner), a, fills[1](fill_in), fill_ins[2])
    )
    outs.append(filled)
    outs.append(fills[2](fill_in))
    pieces = [
        jnp.concatenate(both, axis=0)
        for both in zip(jnp.split(b, z[2], axis=0), jnp.split(c, z[2], axis=0))
    ]
    total = pieces[-1]
    for piece, dims in zip(pieces[-2::-1], [y, inner] + [[]] * z[2]):
        total, a = phase((shift(total, z, 1) + piece, scatter_dims(a, dims)))
    return jnp.concatenate([a, total], axis=0), outs


def scatter_columns(x, n_blk):
    blk = blk_dims(n_blk)
    sizes = tuple(dim[2] for dim in blk)
    x = x.reshape((x.shape[0],) + sizes + (-1,))
    for axis in range(len(blk), 0, -1):
        dim = blk[axis - 1]
        x = direct_scatter(
            [
                lax.dynamic_index_in_dim(x, (digit_of(dim) + k) % dim[2], axis, keepdims=False)
                for k in range(dim[2])
            ],
            dim,
        )
        yield x


def sum_cores(pair, n_blk, n_head):
    return ring_scatter(pair, split_dims(n_blk, n_head)[3])


def gather_two(x, n_blk, n_head, beside):
    half = x.shape[0] // 2
    z, inner, y, core = split_dims(n_blk, n_head)
    pieces = direct_gather(x, z)
    b = jnp.concatenate([p[:half] for p in pieces], axis=0)
    c = jnp.concatenate([p[half:] for p in pieces], axis=0)
    b, c = phase((gather_dims(b, y), gather_dims(c, inner)))
    b, c, beside = phase((gather_dims(b, inner), gather_dims(c, y), beside))
    return direct_gather(b, core), direct_gather(c, core), beside


def scatter_two(b, c, n_blk, n_head):
    z, inner, y, core = split_dims(n_blk, n_head)
    b = scatter_dims(direct_scatter(b, core), y + inner)
    c = scatter_dims(direct_scatter(c, core), inner + y)
    pieces = [
        jnp.concatenate(both, axis=0)
        for both in zip(jnp.split(b, z[2], axis=0), jnp.split(c, z[2], axis=0))
    ]
    return direct_scatter(pieces, z)


def scatter_blk(x, axis=0):
    return lax.psum_scatter(x, "blk", scatter_dimension=axis, tiled=True)


def head_lanes(heads, head):
    lane = lax.broadcasted_iota(jnp.int32, (1, heads * ROPE), 1) % (heads * ROPE // 2)
    return lane // (ROPE // 2) == head


def spread(heads):
    row = lax.broadcasted_iota(jnp.int32, (ROPE, heads * ROPE), 0)
    lane = lax.broadcasted_iota(jnp.int32, (ROPE, heads * ROPE), 1)
    width = heads * ROPE // 2
    return jnp.where(row == lane // width * (ROPE // 2) + lane % (ROPE // 2), 1.0, 0.0).astype(BF16)


def attention_kernel(
    heads, scale, at_ref, q_ref, lata_ref, latb_ref, up_ref, out_ref, lse_ref, m_ref, l_ref, acc_ref
):
    step = pl.program_id(0)

    @pl.when(step == 0)
    def _():
        m_ref[...] = jnp.full_like(m_ref, -1e30)
        l_ref[...] = jnp.zeros_like(l_ref)
        acc_ref[...] = jnp.zeros_like(acc_ref)

    @pl.when(step <= at_ref[0])
    def _():
        lat = both_cores(lata_ref, latb_ref)
        kv = dot(lat[:, :RANK], up_ref[...]).astype(BF16)
        rope = dot(lat[:, RANK : RANK + ROPE], spread(heads)).astype(BF16)
        query = q_ref[...].reshape(BLOCK, heads * (NOPE + ROPE))
        query_rope = query[:, heads * NOPE :]
        for h in range(heads):
            at = h * (NOPE + VALUE)
            scores = dot_nt(query[:, h * NOPE : (h + 1) * NOPE], kv[:, at : at + NOPE])
            masked = jnp.where(head_lanes(heads, h), query_rope, jnp.zeros_like(query_rope))
            scores = (scores + dot_nt(masked, rope)) * scale
            old = m_ref[h][:, :1]
            new = jnp.maximum(old, jnp.max(scores, axis=1, keepdims=True))
            expo = jnp.exp(scores - new)
            factor = jnp.exp(old - new)
            l_ref[h] = l_ref[h] * factor + jnp.sum(expo, axis=1, keepdims=True)
            acc_ref[h] = acc_ref[h] * factor + dot(expo.astype(BF16), kv[:, at + NOPE : at + NOPE + VALUE])
            m_ref[h] = jnp.broadcast_to(new, m_ref.shape[1:])

    @pl.when(step == pl.num_programs(0) - 1)
    def _():
        lane = lax.broadcasted_iota(jnp.int32, (BLOCK, 128), 1)
        lse = jnp.zeros((BLOCK, 128), F32)
        for h in range(heads):
            out = acc_ref[h] / l_ref[h]
            out_ref[:, :, :, h * VALUE : (h + 1) * VALUE] = out.astype(BF16).reshape(
                out_ref.shape[:3] + (VALUE,)
            )
            lse = jnp.where(lane == h, m_ref[h] + jnp.log(l_ref[h]), lse)
        lse_ref[...] = lse


def both_cores(first_ref, second_ref):
    flat = [ref[...].reshape(BLOCK // 2, ref.shape[-1]) for ref in (first_ref, second_ref)]
    return jnp.concatenate(flat, axis=0)


def key_specs(view, y_axis, clamp):
    n_blk = view[0] * view[1] * view[2] // view[y_axis]
    shape = tuple(n if i == y_axis else 1 if i < 3 else n for i, n in enumerate(view))

    def index(step, at):
        step = jnp.minimum(step, at[0]) if clamp else step
        inner, z = at[1 + step], at[1 + n_blk + step]
        return (0, inner, z, 0, 0) if y_axis == 0 else (inner, 0, z, 0, 0)

    return [pl.BlockSpec(shape, index)] * 2


def attention(at, seq, query, lats, up, y_axis, heads):
    n_head, own = query.shape[0], query.shape[2]
    n_blk = (at.shape[0] - 1) // 2
    scale = (NOPE + ROPE) ** -0.5
    row = lambda width, s: pl.BlockSpec((n_head, 1, own, width), lambda b, r: (0, s, 0, 0))
    return pl.pallas_call(
        functools.partial(attention_kernel, heads, scale),
        grid_spec=pltpu.PrefetchScalarGridSpec(
            num_scalar_prefetch=1,
            grid=(n_blk,),
            in_specs=[row(query.shape[3], seq)]
            + key_specs(lats[0].shape, y_axis, True)
            + [pl.BlockSpec(up.shape, lambda b, r: (0, 0))],
            out_specs=[row(heads * VALUE, 0), pl.BlockSpec((BLOCK, 128), lambda b, r: (0, 0))],
            scratch_shapes=[
                pltpu.VMEM((heads, BLOCK, 128), F32),
                pltpu.VMEM((heads, BLOCK, 128), F32),
                pltpu.VMEM((heads, BLOCK, VALUE), F32),
            ],
        ),
        out_shape=[
            jax.ShapeDtypeStruct((n_head, 1, own, heads * VALUE), BF16),
            jax.ShapeDtypeStruct((BLOCK, 128), F32),
        ],
        cost_estimate=pl.CostEstimate(
            flops=n_blk * BLOCK * 2 * (RANK * up.shape[1] + heads * BLOCK * 640),
            bytes_accessed=lats[0].size * 4 + up.size * 2 + query.size * 2,
            transcendentals=n_blk * heads * BLOCK * BLOCK,
        ),
        name="attention",
    )(at, query, *lats, up)


def attention_back_kernel(
    heads, scale, at_ref, q_ref, lata_ref, latb_ref, up_ref, att_ref, datt_ref, lse_ref, cos_ref, sin_ref,
    dq_ref, dlata_ref, dlatb_ref, dup_ref, delta_ref, dqn_ref, dqr_ref, up_acc,
):
    step = pl.program_id(0)
    last = pl.num_programs(0) - 1

    @pl.when(step == 0)
    def _():
        up_acc[...] = jnp.zeros_like(up_acc)

    @pl.when(step == 0)
    def _():
        dqn_ref[...] = jnp.zeros_like(dqn_ref)
        dqr_ref[...] = jnp.zeros_like(dqr_ref)
        prod = att_ref[...].astype(F32) * datt_ref[...].astype(F32)
        prod = prod.reshape(BLOCK, heads * VALUE)
        for h in range(heads):
            delta_ref[h] = jnp.broadcast_to(
                jnp.sum(prod[:, h * VALUE : (h + 1) * VALUE], axis=1, keepdims=True), (BLOCK, 128)
            )

    @pl.when(step <= at_ref[0])
    def _():
        lat = both_cores(lata_ref, latb_ref)
        latn = lat[:, :RANK]
        kv = dot(latn, up_ref[...]).astype(BF16)
        copies = spread(heads)
        rope = dot(lat[:, RANK : RANK + ROPE], copies).astype(BF16)
        query = q_ref[...].reshape(BLOCK, heads * (NOPE + ROPE))
        query_rope = query[:, heads * NOPE :]
        d_att = datt_ref[...].reshape(BLOCK, heads * VALUE)
        d_rope = jnp.zeros((BLOCK, heads * ROPE), F32)
        d_kv = []
        for h in range(heads):
            at = h * (NOPE + VALUE)
            lanes = head_lanes(heads, h)
            q_h = query[:, h * NOPE : (h + 1) * NOPE]
            k_h = kv[:, at : at + NOPE]
            d_h = d_att[:, h * VALUE : (h + 1) * VALUE]
            masked = jnp.where(lanes, query_rope, jnp.zeros_like(query_rope))
            scores = (dot_nt(q_h, k_h) + dot_nt(masked, rope)) * scale
            prob = jnp.exp(scores - lse_ref[:, h : h + 1])
            d_prob = dot_nt(d_h, kv[:, at + NOPE : at + NOPE + VALUE])
            d_score = (prob * (d_prob - delta_ref[h][:, :1]) * scale).astype(BF16)
            dqn_ref[h] = dqn_ref[h] + dot(d_score, k_h)
            dqr_ref[...] = dqr_ref[...] + jnp.where(lanes, dot(d_score, rope), 0.0)
            d_kv.append(dot_tn(d_score, q_h))
            d_kv.append(dot_tn(prob.astype(BF16), d_h))
            d_rope = d_rope + dot_tn(d_score, masked)
        d_kv = jnp.concatenate(d_kv, axis=1).astype(BF16)
        up_acc[...] += dot_tn(latn, d_kv)
        d_lat = dot_nt(d_kv, up_ref[...]).astype(BF16)
        d_key = dot_nt(d_rope.astype(BF16), copies).astype(BF16)
        for i, ref in enumerate((dlata_ref, dlatb_ref)):
            here = slice(i * (BLOCK // 2), (i + 1) * (BLOCK // 2))
            shape = ref.shape[:4]
            ref[:, :, :, :, :RANK] = d_lat[here].reshape(shape + (RANK,))
            ref[:, :, :, :, RANK : RANK + ROPE] = d_key[here].reshape(shape + (ROPE,))
            ref[:, :, :, :, RANK + ROPE :] = jnp.zeros(shape + (ref.shape[4] - RANK - ROPE,), BF16)

    @pl.when(step > at_ref[0])
    def _():
        dlata_ref[...] = jnp.zeros_like(dlata_ref)
        dlatb_ref[...] = jnp.zeros_like(dlatb_ref)

    @pl.when(step == last)
    def _():
        shape = dq_ref.shape[:3]
        for h in range(heads):
            dq_ref[:, :, :, h * NOPE : (h + 1) * NOPE] = dqn_ref[h].astype(BF16).reshape(shape + (NOPE,))
        half = heads * ROPE // 2
        cosine, sine = cos_ref[...], sin_ref[...]
        first, second = dqr_ref[:, :half], dqr_ref[:, half:]
        at = heads * NOPE
        dq_ref[:, :, :, at : at + half] = (first * cosine + second * sine).astype(BF16).reshape(shape + (half,))
        dq_ref[:, :, :, at + half :] = (second * cosine - first * sine).astype(BF16).reshape(shape + (half,))

    @pl.when(step == last)
    def _():
        dup_ref[...] = up_acc[...]


def attention_back(at, seq, query, lats, up, att, d_att, lse, cosine, sine, y_axis, heads):
    n_head, own = query.shape[0], query.shape[2]
    n_blk = (at.shape[0] - 1) // 2
    scale = (NOPE + ROPE) ** -0.5
    row = lambda width, s: pl.BlockSpec((n_head, 1, own, width), lambda b, r: (0, s, 0, 0))
    whole = lambda x: pl.BlockSpec(x.shape, lambda b, r: (0, 0))
    half = heads * ROPE // 2
    return pl.pallas_call(
        functools.partial(attention_back_kernel, heads, scale),
        grid_spec=pltpu.PrefetchScalarGridSpec(
            num_scalar_prefetch=1,
            grid=(n_blk,),
            in_specs=[row(query.shape[3], seq)]
            + key_specs(lats[0].shape, y_axis, True)
            + [whole(up), row(heads * VALUE, 0), row(heads * VALUE, seq)]
            + [whole(lse), whole(cosine), whole(sine)],
            out_specs=[row(query.shape[3], 0)] + key_specs(lats[0].shape, y_axis, False) + [whole(up)],
            scratch_shapes=[
                pltpu.VMEM((heads, BLOCK, 128), F32),
                pltpu.VMEM((heads, BLOCK, NOPE), F32),
                pltpu.VMEM((BLOCK, 2 * half), F32),
                pltpu.VMEM(up.shape, F32),
            ],
        ),
        out_shape=[
            jax.ShapeDtypeStruct((n_head, 1, own, query.shape[3]), BF16),
            jax.ShapeDtypeStruct(lats[0].shape, BF16),
            jax.ShapeDtypeStruct(lats[0].shape, BF16),
            jax.ShapeDtypeStruct(up.shape, F32),
        ],
        cost_estimate=pl.CostEstimate(
            flops=n_blk * BLOCK * 2 * (3 * RANK * up.shape[1] + heads * BLOCK * 1700),
            bytes_accessed=lats[0].size * 8 + up.size * 6 + query.size * 4,
            transcendentals=n_blk * heads * BLOCK * BLOCK,
        ),
        name="attention_back",
    )(at, query, *lats, up, att, d_att, lse, cosine, sine)


def pick(own, first_ref, second_ref, out_ref):
    @pl.when(own)
    def _():
        out_ref[...] = first_ref[...]

    @pl.when(jnp.logical_not(own))
    def _():
        out_ref[...] = second_ref[...]


def put(own, value_ref, first_ref, second_ref):
    @pl.when(own)
    def _():
        first_ref[...] = value_ref[...]

    @pl.when(jnp.logical_not(own))
    def _():
        second_ref[...] = value_ref[...]


def gate_lanes(tail, base, local):
    lane = lax.broadcasted_iota(jnp.int32, tail.shape, 1)
    tail = tail.astype(F32)
    return [
        jnp.sum(jnp.where(lane == base + e, tail, 0.0), axis=1, keepdims=True) for e in range(local)
    ]


def spans(size, step):
    return [(at, min(step, size - at)) for at in range(0, size, step)]


def experts_kernel(
    units, local, base_ref, xa_ref, xb_ref, ta_ref, tb_ref, win_ref, wout_ref,
    x_ref, gu_ref, outa_ref, outb_ref, tail_ref, act_ref, sum_ref,
):
    own = pl.program_id(0) < pl.num_programs(0) // 2
    pick(own, xa_ref, xb_ref, x_ref)
    pick(own, ta_ref, tb_ref, tail_ref)
    gates = gate_lanes(tail_ref[...], base_ref[0], local)
    padded = wout_ref.shape[0]
    for at, size in spans(padded, 256):
        gate = dot_nt(x_ref[...], win_ref[at : at + size, :])
        up = dot_nt(x_ref[...], win_ref[padded + at : padded + at + size, :])
        gu_ref[:, at : at + size] = gate.astype(BF16)
        gu_ref[:, padded + at : padded + at + size] = up.astype(BF16)
        act = gate * jax.nn.sigmoid(gate) * up
        for here in range(0, size, 128):
            expert = (at + here) // units
            part = act[:, here : here + 128]
            part = part * gates[expert] if expert < local else part
            act_ref[:, at + here : at + here + 128] = part.astype(BF16)
    for at, size in spans(wout_ref.shape[1], 512):
        sum_ref[:, at : at + size] = dot(act_ref[...], wout_ref[:, at : at + size]).astype(BF16)
    put(own, sum_ref, outa_ref, outb_ref)


def half_specs(tile, steps, width, column=0):
    half = steps // 2
    return [
        pl.BlockSpec((tile, width), lambda i, r: (jnp.minimum(i, half - 1), column)),
        pl.BlockSpec((tile, width), lambda i, r: (jnp.maximum(i - half, 0), column)),
    ]


def tile_of(rows):
    return max(t for t in range(16, 385, 16) if rows % t == 0)


def resident(x):
    return pl.BlockSpec(x.shape, lambda i, r: (0, 0), pipeline_mode=pl.Buffered(1))


def run_experts(base, pair, win, wout, units, local):
    half, width, padded = pair[0].shape[0], wout.shape[1], wout.shape[0]
    tile = tile_of(half)
    steps = 2 * half // tile
    row = lambda size: pl.BlockSpec((tile, size), lambda i, r: (i, 0))
    rows = 2 * half
    shape = lambda count, size: jax.ShapeDtypeStruct((count, size), BF16)
    return pl.pallas_call(
        functools.partial(experts_kernel, units, local),
        grid_spec=pltpu.PrefetchScalarGridSpec(
            num_scalar_prefetch=1,
            grid=(steps,),
            in_specs=half_specs(tile, steps, width)
            + half_specs(tile, steps, 128, width // 128)
            + [resident(win), resident(wout)],
            out_specs=[row(width), row(2 * padded)] + half_specs(tile, steps, width),
            scratch_shapes=[
                pltpu.VMEM((tile, 128), BF16),
                pltpu.VMEM((tile, padded), BF16),
                pltpu.VMEM((tile, width), BF16),
            ],
        ),
        out_shape=[shape(rows, width), shape(rows, 2 * padded), shape(half, width), shape(half, width)],
        cost_estimate=pl.CostEstimate(
            flops=rows * width * padded * 6,
            bytes_accessed=(rows * (3 * width + 2 * padded) + 3 * width * padded) * 2,
            transcendentals=rows * padded,
        ),
        name="experts",
    )(base, *pair, *pair, win, wout)


def experts_back_kernel(
    units, local, base_ref, ga_ref, gb_ref, ta_ref, tb_ref, gu_ref, win_ref, wout_ref,
    hid_ref, act_ref, g_ref, outa_ref, outb_ref, tail_ref, sum_ref,
):
    own = pl.program_id(0) < pl.num_programs(0) // 2
    pick(own, ga_ref, gb_ref, g_ref)
    pick(own, ta_ref, tb_ref, tail_ref)
    gates = gate_lanes(tail_ref[...], base_ref[0], local)
    padded, width = wout_ref.shape
    prods = [jnp.zeros(tail_ref.shape, F32) for _ in range(local)]
    for at, size in spans(padded, 256):
        d_acts = dot_nt(g_ref[...], wout_ref[at : at + size, :])
        for here in range(0, size, 128):
            unit = at + here
            expert = unit // units
            d_act = d_acts[:, here : here + 128]
            gate = gu_ref[:, unit : unit + 128].astype(F32)
            up = gu_ref[:, padded + unit : padded + unit + 128].astype(F32)
            sig = jax.nn.sigmoid(gate)
            silu = gate * sig
            act = silu * up
            if expert < local:
                prods[expert] = prods[expert] + act * d_act
                d_act = d_act * gates[expert]
                act = act * gates[expert]
            hid_ref[:, unit : unit + 128] = (d_act * up * (sig + silu * (1.0 - sig))).astype(BF16)
            hid_ref[:, padded + unit : padded + unit + 128] = (d_act * silu).astype(BF16)
            act_ref[:, unit : unit + 128] = act.astype(BF16)
    for at, size in spans(width, 512):
        sum_ref[:, at : at + size] = dot(hid_ref[...], win_ref[:, at : at + size]).astype(BF16)
    lane = lax.broadcasted_iota(jnp.int32, tail_ref.shape, 1)
    extra = jnp.zeros(tail_ref.shape, F32)
    for e in range(local):
        extra = jnp.where(lane == base_ref[0] + e, jnp.sum(prods[e], axis=1, keepdims=True), extra)
    sum_ref[:, width:] = extra.astype(BF16)
    put(own, sum_ref, outa_ref, outb_ref)


def run_experts_back(base, grads, pair, gu, win, wout, units, local):
    half, width, padded = grads[0].shape[0], wout.shape[1], wout.shape[0]
    tile = tile_of(half)
    steps = 2 * half // tile
    row = lambda size: pl.BlockSpec((tile, size), lambda i, r: (i, 0))
    rows = 2 * half
    shape = lambda count, size: jax.ShapeDtypeStruct((count, size), BF16)
    return pl.pallas_call(
        functools.partial(experts_back_kernel, units, local),
        grid_spec=pltpu.PrefetchScalarGridSpec(
            num_scalar_prefetch=1,
            grid=(steps,),
            in_specs=half_specs(tile, steps, width)
            + half_specs(tile, steps, 128, width // 128)
            + [row(2 * padded), resident(win), resident(wout)],
            out_specs=[row(2 * padded), row(padded), row(width)] + half_specs(tile, steps, width + 128),
            scratch_shapes=[pltpu.VMEM((tile, 128), BF16), pltpu.VMEM((tile, width + 128), BF16)],
        ),
        out_shape=[
            shape(rows, 2 * padded), shape(rows, padded), shape(rows, width),
            shape(half, width + 128), shape(half, width + 128),
        ],
        cost_estimate=pl.CostEstimate(
            flops=rows * width * padded * 6,
            bytes_accessed=(rows * (3 * width + 5 * padded) + 3 * width * padded) * 2,
            transcendentals=rows * padded,
        ),
        name="experts_back",
    )(base, *grads, *pair, gu, win, wout)


def on_device(
    states, teacher, valid, routes, norm_in, w_query, w_down_kv, norm_kv, w_up_kv, w_out, norm_ffn,
    w_router, shared_in, shared_out, expert_in, expert_out,
):
    n_blk, n_head = lax.axis_size("blk"), lax.axis_size("head")
    blk, head = lax.axis_index("blk"), lax.axis_index("head")
    own_pos, seqs, width = states.shape
    block_pos = own_pos * n_head
    rows = own_pos * seqs
    block_rows = rows * n_head
    total_rows = block_rows * n_blk
    experts = w_router.shape[1]
    local = expert_in.shape[0]
    eff = expert_in.shape[3]
    shared = shared_in.shape[2] // n_blk
    heads = w_query.shape[1] // (NOPE + ROPE)
    scale = (NOPE + ROPE) ** (-0.5)
    assert block_pos == BLOCK and seqs == 2
    blks, heads_ring = blk_dims(n_blk), head_dims(n_head)

    def gather_head(x):
        return gather_axis(x, heads_ring).reshape((-1,) + x.shape[1:])

    def scatter_head(x):
        return scatter_axis(x.reshape((n_head, -1) + x.shape[1:]), heads_ring)

    def take_own(x):
        own = lax.dynamic_slice_in_dim(x, head * own_pos, own_pos, 0)
        return jnp.moveaxis(own, 1, 0).reshape((rows,) + x.shape[2:])

    part = width // n_blk
    quarter = part // n_head
    lat_width = RANK + ROPE
    small = jnp.concatenate(
        [norm_in, norm_ffn, w_router.reshape(-1), norm_kv, jnp.sum(valid, axis=1).astype(BF16)]
    )
    lines = -(-small.shape[0] // lat_width // 16) * 16
    small = jnp.pad(small, (0, lines * lat_width - small.shape[0])).reshape(lines, lat_width)
    down = lax.dynamic_slice_in_dim(w_down_kv, head * quarter, quarter, 0)
    down = gather_axis(jnp.concatenate([down, small], axis=0), blks)
    small = down[:, quarter:].reshape(n_blk, -1)
    down = jnp.moveaxis(gather_axis(down[:, :quarter], heads_ring), 0, 1).reshape(width, lat_width)
    lanes = heads * ROPE // 2
    wq = w_query.reshape(part, heads, NOPE + ROPE)
    wq = jnp.concatenate(
        [
            wq[:, :, :NOPE].reshape(part, -1),
            wq[:, :, NOPE : NOPE + ROPE // 2].reshape(part, -1),
            wq[:, :, NOPE + ROPE // 2 :].reshape(part, -1),
        ],
        axis=1,
    )
    most = part * 3 // 4
    wq_most = gather_dims(wq[None, :most], blks[:1])
    wq_rest = gather_dims(wq[None, most:], blks[:0:-1])
    states_blk = gather_head(jnp.moveaxis(states, 1, 0).reshape(rows, width))
    down, wq_most, wq_rest = lax.optimization_barrier((down, wq_most, wq_rest))
    wq_most = in_order(gather_dims(wq_most, blks[1:]), blks)
    wq_rest = in_order(gather_dims(wq_rest, blks[:1]), blks[::-1])
    wq = jnp.concatenate([wq_most, wq_rest], axis=1).reshape(width, -1)
    gain_in = small[:, :part].reshape(-1).astype(F32)
    gain_ffn = small[:, part : 2 * part].reshape(-1).astype(F32)
    at = 2 * part
    router = small[:, at : at + part * experts].reshape(width, experts)
    at += part * experts
    gain_kv = small[:, at : at + RANK // n_blk].reshape(-1).astype(F32)
    at += RANK // n_blk
    count = jnp.sum(small[:, at : at + block_pos].astype(F32))
    wup = lax.all_gather(w_up_kv, "blk", axis=0, tiled=True)
    wo, wup = phase((w_out, wup))
    wo = lax.all_gather(wo, "blk", axis=1, tiled=True)

    pieces = jnp.concatenate(
        [
            jnp.transpose(shared_in.reshape(part, 2, n_blk, shared), (2, 1, 3, 0)).reshape(
                n_blk, 2 * shared, part
            ),
            shared_out.reshape(n_blk, shared, part),
        ],
        axis=1,
    )
    units = -(-eff // 128) * 128
    shared_units = -(-shared // 128) * 128
    padded = local * units + shared_units
    tall = lambda x, size: jnp.pad(x, ((0, size - x.shape[0]), (0, 0)))

    def expert_weights(values):
        expert_in, expert_out, pieces = values
        mine = jnp.transpose(pieces, (1, 0, 2)).reshape(3, shared, width)
        rows_in = jnp.transpose(expert_in, (0, 2, 3, 1))
        win = [
            block
            for side in range(2)
            for block in [tall(rows_in[e, side], units) for e in range(local)]
            + [tall(mine[side], shared_units)]
        ]
        wout = [tall(expert_out[e], units) for e in range(local)] + [tall(mine[2], shared_units)]
        return jnp.concatenate(win, axis=0), jnp.concatenate(wout, axis=0)

    x_own = jnp.moveaxis(states, 1, 0).reshape(rows, width).astype(F32)
    h1_f, rstd_in = normed(x_own, gain_in)
    h1_own = h1_f.astype(BF16)
    h1_blk = normed(states_blk.astype(F32), gain_in)[0].astype(BF16)
    pos_own = blk * block_pos + head * own_pos + jnp.arange(own_pos, dtype=jnp.int32)
    table_own = jnp.tile(angles(pos_own), (seqs, 1))
    pos_blk = blk * block_pos + jnp.arange(block_pos, dtype=jnp.int32)
    table_seq = angles(pos_blk)
    cos_seq, sin_seq = (jnp.tile(f(table_seq), (1, heads)) for f in (jnp.cos, jnp.sin))
    table_blk = jnp.broadcast_to(
        angles(pos_blk).reshape(n_head, 1, own_pos, ROPE // 2), (n_head, seqs, own_pos, ROPE // 2)
    ).reshape(block_rows, ROPE // 2)
    lat = dot(h1_own, down)
    lat_c = lat[:, :RANK]
    latn_f, rstd_kv = normed(lat_c, gain_kv)
    payload = jnp.concatenate(
        [latn_f, rotate(lat[:, RANK:], table_own), jnp.zeros((rows, 128 - ROPE), F32)], axis=1
    ).astype(BF16)
    z, inner, y, _ = split_dims(n_blk, n_head)
    order = [z[2], y[0][2], n_blk // z[2]]
    payload, pieces = phase((by_rows(payload), pieces))
    pieces = lax.all_to_all(pieces, "blk", split_axis=0, concat_axis=0, tiled=True)
    *lats, (wup, wo) = gather_two(payload, n_blk, n_head, (wup, wo))
    lats = [
        [x.reshape(tuple(shape) + (own_pos, -1)) for x in pair]
        for pair, shape in zip(lats, ([order[2], order[1], order[0]], [order[1], order[2], order[0]]))
    ]
    key_blocks = jnp.arange(n_blk, dtype=jnp.int32)
    key_at = jnp.concatenate(
        [jnp.full((1,), blk, jnp.int32), relative(inner, key_blocks) + 0 * key_blocks, relative([z], key_blocks)]
    ).astype(jnp.int32)
    query = dot(h1_blk, wq)
    cosine = jnp.tile(jnp.cos(table_blk), (1, heads))
    sine = jnp.tile(jnp.sin(table_blk), (1, heads))
    q_first, q_second = query[:, -2 * lanes : -lanes], query[:, -lanes:]
    query = jnp.concatenate(
        [query[:, : -2 * lanes], q_first * cosine - q_second * sine, q_second * cosine + q_first * sine],
        axis=1,
    ).astype(BF16)
    shape4 = (n_head, seqs, own_pos, -1)
    query = query.reshape(shape4)
    seq_axes = list(zip(range(seqs), lats, (1, 0)))
    att_seqs, lses = zip(*(attention(key_at, s, query, pair, wup, axis, heads) for s, pair, axis in seq_axes))
    att_rows = jnp.concatenate(att_seqs, axis=1).reshape(block_rows, heads * VALUE)
    y_own = x_own + scatter_head(dot(att_rows, wo).astype(BF16)).astype(F32)
    h2_f, rstd_ffn = normed(y_own, gain_ffn)
    h2_own = h2_f.astype(BF16)

    routes_own = take_own(routes)
    mask = jnp.any(routes_own[:, :, None] == jnp.arange(experts, dtype=jnp.int32), axis=1)
    logits = jnp.where(mask, dot(h2_own, router), -1e30)
    gates = jnp.where(mask, jnp.exp(logits - jnp.max(logits, axis=1, keepdims=True)), 0.0)
    gates = gates / jnp.sum(gates, axis=1, keepdims=True)
    assert experts <= 128
    tail = jnp.zeros((rows, 128 - experts), BF16)
    base = jnp.full((1,), blk * local, jnp.int32)
    x_ext = jnp.concatenate([h2_own, gates.astype(BF16), tail], axis=1)
    rounds = max(1, total_rows // 4096)

    def in_turn(run, parts):
        outs, sums = [], []
        for i, part in enumerate(parts):
            if i == 2:
                sums[0], part = lax.optimization_barrier((sums[0], part))
            outs.append(run(*part))
            sums.append(sum_cores(outs[-1][-2:], n_blk, n_head))
        return outs, sums

    def forward(x_rows, weights=None):
        if weights is None:
            pairs, (win, wout) = gather_parts(
                x_rows, n_blk, n_head, expert_weights, (expert_in, expert_out, pieces)
            )
        else:
            pairs, (win, wout) = gather_parts(x_rows, n_blk, n_head)[0], weights
        outs, sums = in_turn(
            lambda pair: run_experts(base, pair, win, wout, units, local), [(pair,) for pair in pairs]
        )
        kept = [(pair, x, gu) for pair, (x, gu, _, _) in zip(pairs, outs)]
        return kept, (win, wout), scatter_parts(sums, n_blk, n_head)[0]

    def products(values):
        return tuple(dot_tn(values[i], values[i + 1]) for i in range(0, len(values), 2))

    def backward(grad_rows, kept, weights):
        win, wout = weights
        outs, sums = in_turn(
            lambda grads, pair, gu: run_experts_back(base, grads, pair, gu, win, wout, units, local),
            [
                (grads, pair, gu)
                for grads, (pair, _, gu) in zip(gather_parts(grad_rows, n_blk, n_head)[0], kept)
            ],
        )
        (x_b, x_c, x_a) = (x for _, x, _ in kept)
        (hid_b, act_b, grad_b, hid_c, act_c, grad_c, hid_a, act_a, grad_a) = (v for out in outs for v in out[:3])
        back, ((win_b, wout_b, win_c), (wout_c, wout_a), (win_a,)) = scatter_parts(
            sums,
            n_blk,
            n_head,
            (products,) * 3,
            (
                (hid_b, x_b, act_b, grad_b, hid_c, x_c),
                (act_c, grad_c, act_a, grad_a),
                (hid_a, x_a),
            ),
        )
        return back, win_b + win_c + win_a, wout_b + wout_c + wout_a

    def in_rounds(x):
        return x.reshape((rounds, -1) + x.shape[1:])

    if rounds == 1:
        kept, weights, mixed = forward(x_ext)
    else:
        weights = expert_weights((expert_in, expert_out, pieces))
        mixed = lax.map(lambda x: forward(x, weights)[2], in_rounds(x_ext)).reshape(rows, width)
    mixed = mixed.astype(F32)
    out_own = (y_own + mixed).astype(BF16)
    diff = out_own.astype(F32) - take_own(teacher).astype(F32)
    valid_own = take_own(valid).astype(F32)[:, None]
    loss_part = jnp.sum(valid_own * diff * diff)
    grad_own = diff * valid_own * (total_rows / count)

    grad_own_b = grad_own.astype(BF16)
    if rounds == 1:
        back, d_win, d_wout = backward(grad_own_b, kept, weights)
    else:

        def round_back(sums, both):
            kept, _, _ = forward(both[0], weights)
            back, d_win, d_wout = backward(both[1], kept, weights)
            return (sums[0] + d_win, sums[1] + d_wout), back

        start = (jnp.zeros((2 * padded, width), F32), jnp.zeros((padded, width), F32))
        (d_win, d_wout), back = lax.scan(round_back, start, (in_rounds(x_ext), in_rounds(grad_own_b)))
        back = back.reshape(rows, -1)
    d_sh = jnp.concatenate(
        [d_win[s * padded + local * units :][:shared] for s in range(2)]
        + [d_wout[local * units :][:shared]],
        axis=0,
    ).astype(BF16)
    d_sh = jnp.transpose(d_sh.reshape(3 * shared, n_blk, part), (1, 0, 2))
    back, d_win, d_wout, d_sh = lax.optimization_barrier((back, d_win, d_wout, d_sh))
    back = back.astype(F32)
    d_sh = lax.all_to_all(d_sh, "blk", split_axis=0, concat_axis=0, tiled=True).astype(F32)
    grad_shin = jnp.transpose(d_sh[:, : 2 * shared].reshape(n_blk, 2, shared, part), (3, 1, 0, 2)).reshape(
        part, 2, n_blk * shared
    )
    grad_shout = d_sh[:, 2 * shared :].reshape(n_blk * shared, part)

    d_gates = back[:, width : width + experts]
    d_logits = gates * (d_gates - jnp.sum(gates * d_gates, axis=1, keepdims=True))
    d_logits = d_logits.astype(BF16)
    grad_router = dot_tn(h2_own, d_logits)
    dh2 = back[:, :width] + dot_nt(d_logits, router)
    dy_branch, grad_gain_ffn = norm_back(dh2, y_own, rstd_ffn, gain_ffn)
    dy_own = grad_own + dy_branch

    dy_blk = gather_head(dy_own.astype(BF16))
    grad_wo = dot_tn(att_rows, dy_blk).astype(BF16)
    d_att = dot_nt(dy_blk, wo).astype(BF16).reshape(shape4)
    grad_wo, d_att = phase((grad_wo, d_att))
    wo_steps = scatter_columns(grad_wo, n_blk)
    dqs, d_lats, d_ups = [], [], []
    for (s, pair, axis), att, lse in zip(seq_axes, att_seqs, lses):
        dq, first, second, d_up = attention_back(
            key_at, s, query, pair, wup, att, d_att, lse, cos_seq, sin_seq, axis, heads
        )
        if s == 0:
            grad_wo, d_att = phase((next(wo_steps), d_att))
        dqs.append(dq)
        d_lats.append([x.reshape(total_rows // 4, -1) for x in (first, second)])
        d_ups.append(d_up)
    for grad_wo in wo_steps:
        pass
    grad_wo = grad_wo.astype(F32)
    dq = jnp.concatenate(dqs, axis=1)
    d_up = sum(d_ups).astype(BF16)
    d_lat = by_rows(scatter_two(*d_lats, n_blk, n_head))[:, : RANK + ROPE].astype(F32)
    dq = dq.reshape(block_rows, -1)
    dh1 = scatter_head(dot_nt(dq, wq).astype(BF16)).astype(F32)
    up_rows = w_up_kv.shape[0]
    wide = up_rows * w_up_kv.shape[1] // part
    grad_wq = by_rows(dot_tn(h1_blk, dq).astype(BF16)).reshape(n_blk, part, -1)
    d_up = jnp.moveaxis(d_up.reshape(n_blk, up_rows, -1, wide), 2, 1).reshape(n_blk, part, wide)
    joined = jnp.concatenate([grad_wq, d_up], axis=2)
    joined, d_win, d_wout = phase((by_rows(joined), d_win, d_wout))
    joined = by_rows(lax.psum_scatter(joined, "blk", scatter_dimension=0, tiled=False)).astype(F32)
    grad_wq = joined[:, :-wide]
    grad_up = jnp.moveaxis(joined[:, -wide:].reshape(-1, up_rows, wide), 0, 1).reshape(up_rows, -1)
    grad_ein = jnp.stack(
        [jnp.stack([d_win[s * padded + e * units :][:eff] for s in range(2)]) for e in range(local)]
    )
    grad_ein = jnp.transpose(grad_ein, (0, 3, 1, 2))
    grad_eout = jnp.stack([d_wout[e * units :][:eff] for e in range(local)])
    grad_wq = jnp.concatenate(
        [
            grad_wq[:, : heads * NOPE].reshape(part, heads, NOPE),
            grad_wq[:, heads * NOPE : -lanes].reshape(part, heads, ROPE // 2),
            grad_wq[:, -lanes:].reshape(part, heads, ROPE // 2),
        ],
        axis=2,
    ).reshape(part, -1)
    d_lat_c, grad_gain_kv = norm_back(d_lat[:, :RANK], lat_c, rstd_kv, gain_kv)
    d_lat_b = jnp.concatenate([d_lat_c, rotate(d_lat[:, RANK : RANK + ROPE], -table_own)], axis=1).astype(BF16)
    d_lat_b = by_rows(d_lat_b)
    d_lat_blk = gather_head(d_lat_b)
    grad_down = by_rows(dot_tn(h1_blk, d_lat_blk).astype(BF16)).reshape(n_blk, n_head, quarter, -1)
    grad_down = lax.dynamic_index_in_dim(grad_down, head, 1, keepdims=False)
    grad_down = gather_head(by_rows(scatter_axis(grad_down, blks))).astype(F32)
    dh1 = dh1 + dot_nt(d_lat_b, down)
    dx_branch, grad_gain_in = norm_back(dh1, x_own, rstd_in, gain_in)
    dx_own = dy_own + dx_branch

    loss_high = loss_part.astype(BF16).astype(F32)
    sums = jnp.concatenate(
        [
            grad_gain_in.reshape(n_blk, -1),
            grad_gain_ffn.reshape(n_blk, -1),
            grad_router.reshape(n_blk, -1),
            grad_gain_kv.reshape(n_blk, -1),
            jnp.full((n_blk, 1), loss_high),
            jnp.full((n_blk, 1), loss_part - loss_high),
        ],
        axis=1,
    )
    sums = scatter_axis(sums, blks)
    for dim in heads_ring:
        sums = sum(ring_gather(sums, dim))
    out_gain_in = sums[:part]
    out_gain_ffn = sums[part : 2 * part]
    at = 2 * part
    out_router = sums[at : at + part * experts].reshape(part, experts)
    at += part * experts
    out_gain_kv = sums[at : at + RANK // n_blk]
    loss = (sums[-2] + sums[-1]) / (width * count)

    def give(x):
        return jnp.moveaxis(x.reshape(seqs, own_pos, width), 0, 1)

    return (
        give(out_own), loss, give(dx_own), out_gain_in, grad_wq, grad_down, out_gain_kv, grad_up,
        grad_wo, out_gain_ffn, out_router, grad_shin, grad_shout, grad_ein, grad_eout,
    )


def solution(mesh):
    in_specs = (
        P(BOTH, None, None), P("blk", None, None), P("blk", None), P("blk", None, None), P("blk"),
        P("blk", "head"), P("blk", None), P("blk"), P("blk", "head"), P("head", "blk"), P("blk"),
        P("blk", None), P("blk", None, "head"), P("head", "blk"), P("blk", None, None, "head"),
        P("blk", "head", None),
    )
    out_specs = (
        P(BOTH, None, None), P(), P(BOTH, None, None), P("blk"), P("blk", "head"), P("blk", None),
        P("blk"), P("blk", "head"), P("head", "blk"), P("blk"), P("blk", None), P("blk", None, "head"),
        P("head", "blk"), P("blk", None, None, "head"), P("blk", "head", None),
    )
    return jax.shard_map(on_device, mesh=mesh, in_specs=in_specs, out_specs=out_specs, check_vma=False)
```

```python
import functools

import jax
import jax.numpy as jnp
from jax import lax
from jax.experimental import pallas as pl
from jax.experimental.layout import Layout, with_layout_constraint
from jax.experimental.pallas import tpu as pltpu
from jax.sharding import PartitionSpec as P

NOPE = 128
ROPE = 64
VALUE = 128
RANK = 512
BLOCK = 256
EPS = 1e-06
F32 = jnp.float32
BF16 = jnp.bfloat16
BOTH = ("blk", "head")


def angles(position):
    frequency = 10000.0 ** (-2.0 * jnp.arange(ROPE // 2, dtype=F32) / ROPE)
    return position.astype(F32)[:, None] * frequency[None, :]


def rotate(values, table):
    half = ROPE // 2
    cosine, sine = jnp.cos(table), jnp.sin(table)
    first, second = values[:, :half], values[:, half:]
    return jnp.concatenate([first * cosine - second * sine, second * cosine + first * sine], axis=1)


def normed(values, gain):
    rstd = lax.rsqrt(jnp.mean(values * values, axis=-1, keepdims=True) + EPS)
    return values * rstd * gain, rstd


def norm_back(grad, values, rstd, gain):
    scaled = grad * gain
    out = rstd * scaled - values * rstd**3 * jnp.mean(scaled * values, axis=-1, keepdims=True)
    return out, jnp.sum(grad * values * rstd, axis=0)


def by_rows(x):
    return with_layout_constraint(x, Layout(tuple(range(x.ndim))))


def dot(a, b):
    return jnp.dot(a, b, preferred_element_type=F32)


def dot_nt(a, b):
    return lax.dot_general(a, b, (((1,), (1,)), ((), ())), preferred_element_type=F32)


def dot_tn(a, b):
    return lax.dot_general(a, b, (((0,), (0,)), ((), ())), preferred_element_type=F32)


def blk_dims(n_blk):
    if n_blk == 8:
        return [("blk", 2, 4), ("blk", 1, 2)]
    if n_blk == 32:
        return [("blk", 8, 4), ("blk", 2, 4), ("blk", 1, 2)]
    return [("blk", 1, n_blk)]


def head_dims(n_head):
    return [("head", 2, n_head // 2), ("head", 1, 2)] if n_head % 2 == 0 else [("head", 1, n_head)]


def shift(x, dim, by):
    axis, stride, size = dim
    pairs = []
    for i in range(lax.axis_size(axis)):
        digit = i // stride % size
        pairs.append((i, i + ((digit + by) % size - digit) * stride))
    return lax.ppermute(x, axis, pairs)


def digit_of(dim):
    axis, stride, size = dim
    return lax.axis_index(axis) // stride % size


def ring_gather(x, dim):
    pieces = [x]
    for _ in range(dim[2] - 1):
        pieces.append(shift(pieces[-1], dim, -1))
    return pieces


def ring_scatter(pieces, dim):
    total = pieces[-1]
    for piece in pieces[-2::-1]:
        total = shift(total, dim, 1) + piece
    return total


def direct_gather(x, dim):
    return [x] + [shift(x, dim, -k) for k in range(1, dim[2])]


def direct_scatter(pieces, dim):
    total = pieces[0].astype(F32)
    for k in range(1, dim[2]):
        total = total + shift(pieces[k], dim, k).astype(F32)
    return total.astype(pieces[0].dtype)


def gather_dims(x, dims, step=ring_gather):
    for dim in dims:
        x = jnp.concatenate(step(x, dim), axis=0)
    return x


def scatter_dims(x, dims, step=ring_scatter):
    for dim in reversed(dims):
        x = step(jnp.split(x, dim[2], axis=0), dim)
    return x


def relative(dims, index):
    place, scale = 0, 1
    for dim in dims:
        place = place + (index // dim[1] % dim[2] - digit_of(dim)) % dim[2] * scale
        scale *= dim[2]
    return place


def absolute(dims, place):
    index = 0
    for dim in dims:
        index = index + (place % dim[2] + digit_of(dim)) % dim[2] * dim[1]
        place //= dim[2]
    return index


def gather_axis(x, dims):
    return in_order(gather_dims(x[None], dims, direct_gather), dims)


def in_order(stack, dims):
    n = stack.shape[0]
    return jnp.concatenate(
        [lax.dynamic_slice_in_dim(stack, relative(dims, i), 1, 0) for i in range(n)], axis=0
    )


def scatter_axis(x, dims):
    n = lax.axis_size(dims[0][0])
    stack = jnp.concatenate(
        [lax.dynamic_slice_in_dim(x, absolute(dims, i), 1, 0) for i in range(n)], axis=0
    )
    return scatter_dims(stack, dims, direct_scatter)[0]


def split_dims(n_blk, n_head):
    blk, head = blk_dims(n_blk), head_dims(n_head)
    return blk[0], blk[1:], head[:-1], head[-1]


phase = lax.optimization_barrier


def no_fill(values):
    return values


def gather_parts(x, n_blk, n_head, fill=no_fill, fill_in=()):
    third = x.shape[0] * 5 // 16
    first = x.shape[0] - 2 * third
    z, inner, y, core = split_dims(n_blk, n_head)
    a, pieces = x[:first], [x[first:]]
    for dims in [inner, y] + [[]] * (z[2] - 4):
        piece, a = phase((shift(pieces[-1], z, -1), gather_dims(a, dims)))
        pieces.append(piece)
    pieces.append(shift(pieces[-1], z, -1))
    b = jnp.concatenate([p[:third] for p in pieces], axis=0)
    c = jnp.concatenate([p[third:] for p in pieces], axis=0)
    b, c, a = phase((b, c, a))
    b, c, last, fill_in = phase((gather_dims(b, y), gather_dims(c, inner), shift(a, z, -1), fill_in))
    pieces = [a, last]
    for _ in range(z[2] - 2):
        pieces.append(shift(pieces[-1], z, -1))
    b, c, pieces, filled = phase((gather_dims(b, inner), gather_dims(c, y), pieces, fill(fill_in)))
    return [ring_gather(part, core) for part in (b, c, jnp.concatenate(pieces, axis=0))], filled


def scatter_parts(sums, n_blk, n_head, fills=(no_fill,) * 3, fill_ins=((),) * 3):
    z, inner, y, _ = split_dims(n_blk, n_head)
    b, c, a, filled = phase((*sums, fill_ins[0]))
    pieces = jnp.split(a, z[2], axis=0)
    a = ring_scatter(pieces[1:], z)
    b, c, a, filled, fill_in = phase(
        (scatter_dims(b, inner), scatter_dims(c, y), a, fills[0](filled), fill_ins[1])
    )
    outs = [filled]
    a = shift(a, z, 1) + pieces[0]
    b, c, a, filled, fill_in = phase(
        (scatter_dims(b, y), scatter_dims(c, inner), a, fills[1](fill_in), fill_ins[2])
    )
    outs.append(filled)
    outs.append(fills[2](fill_in))
    pieces = [
        jnp.concatenate(both, axis=0)
        for both in zip(jnp.split(b, z[2], axis=0), jnp.split(c, z[2], axis=0))
    ]
    total = pieces[-1]
    for piece, dims in zip(pieces[-2::-1], [y, inner] + [[]] * z[2]):
        total, a = phase((shift(total, z, 1) + piece, scatter_dims(a, dims)))
    return jnp.concatenate([a, total], axis=0), outs


def scatter_columns(x, n_blk):
    blk = blk_dims(n_blk)
    sizes = tuple(dim[2] for dim in blk)
    x = x.reshape((x.shape[0],) + sizes + (-1,))
    for axis in range(len(blk), 0, -1):
        dim = blk[axis - 1]
        x = direct_scatter(
            [
                lax.dynamic_index_in_dim(x, (digit_of(dim) + k) % dim[2], axis, keepdims=False)
                for k in range(dim[2])
            ],
            dim,
        )
        yield x


def sum_cores(pair, n_blk, n_head):
    return ring_scatter(pair, split_dims(n_blk, n_head)[3])


def gather_two(x, n_blk, n_head, beside):
    half = x.shape[0] // 2
    z, inner, y, core = split_dims(n_blk, n_head)
    pieces = direct_gather(x, z)
    b = jnp.concatenate([p[:half] for p in pieces], axis=0)
    c = jnp.concatenate([p[half:] for p in pieces], axis=0)
    b, c = phase((gather_dims(b, y), gather_dims(c, inner)))
    b, c, beside = phase((gather_dims(b, inner), gather_dims(c, y), beside))
    return direct_gather(b, core), direct_gather(c, core), beside


def scatter_two(b, c, n_blk, n_head, beside):
    z, inner, y, core = split_dims(n_blk, n_head)
    b, c, beside = phase((direct_scatter(b, core), direct_scatter(c, core), beside))
    b = scatter_dims(b, y + inner)
    c = scatter_dims(c, inner + y)
    pieces = [
        jnp.concatenate(both, axis=0)
        for both in zip(jnp.split(b, z[2], axis=0), jnp.split(c, z[2], axis=0))
    ]
    return direct_scatter(pieces, z), beside


def scatter_blk(x, axis=0):
    return lax.psum_scatter(x, "blk", scatter_dimension=axis, tiled=True)


HEAD = 256


def attention_kernel(
    heads, scale, at_ref, q_ref, lata_ref, latb_ref, up_ref, out_ref, lse_ref, m_ref, acc_ref
):
    step = pl.program_id(0)

    @pl.when(step == 0)
    def _():
        m_ref[...] = jnp.full_like(m_ref, -1e30)
        acc_ref[...] = jnp.zeros_like(acc_ref)

    @pl.when(step <= at_ref[0])
    def _():
        lat = both_cores(lata_ref, latb_ref)
        kv = dot(lat[:, :RANK], up_ref[...]).astype(BF16)
        query = q_ref[...].reshape(BLOCK, heads * HEAD)
        ones = jnp.ones((BLOCK, HEAD - VALUE), BF16)
        for h in range(heads):
            at = h * (NOPE + VALUE)
            keys = jnp.concatenate([kv[:, at : at + NOPE], lat[:, RANK:]], axis=1)
            values = jnp.concatenate([kv[:, at + NOPE : at + NOPE + VALUE], ones], axis=1)
            scores = dot_nt(query[:, h * HEAD : (h + 1) * HEAD], keys) * scale
            old = m_ref[h][:, :1]
            new = jnp.maximum(old, jnp.max(scores, axis=1, keepdims=True))
            expo = jnp.exp(scores - new)
            acc_ref[h] = acc_ref[h] * jnp.exp(old - new) + dot(expo.astype(BF16), values)
            m_ref[h] = jnp.broadcast_to(new, m_ref.shape[1:])

    @pl.when(step == pl.num_programs(0) - 1)
    def _():
        lane = lax.broadcasted_iota(jnp.int32, (BLOCK, 128), 1)
        lse = jnp.zeros((BLOCK, 128), F32)
        for h in range(heads):
            total = acc_ref[h][:, VALUE:]
            out = acc_ref[h][:, :VALUE] / total
            out_ref[:, :, :, h * VALUE : (h + 1) * VALUE] = out.astype(BF16).reshape(
                out_ref.shape[:3] + (VALUE,)
            )
            lse = jnp.where(lane == h, m_ref[h] + jnp.log(total), lse)
        lse_ref[...] = lse


def both_cores(first_ref, second_ref):
    flat = [ref[...].reshape(BLOCK // 2, ref.shape[-1]) for ref in (first_ref, second_ref)]
    return jnp.concatenate(flat, axis=0)


def key_specs(view, y_axis, clamp):
    n_blk = view[0] * view[1] * view[2] // view[y_axis]
    shape = tuple(n if i == y_axis else 1 if i < 3 else n for i, n in enumerate(view))

    def index(step, at):
        step = jnp.minimum(step, at[0]) if clamp else step
        inner, z = at[1 + step], at[1 + n_blk + step]
        return (0, inner, z, 0, 0) if y_axis == 0 else (inner, 0, z, 0, 0)

    return [pl.BlockSpec(shape, index)] * 2


def attention(at, seq, query, lats, up, y_axis, heads):
    n_head, own = query.shape[0], query.shape[2]
    n_blk = (at.shape[0] - 1) // 2
    scale = (NOPE + ROPE) ** -0.5
    row = lambda width, s: pl.BlockSpec((n_head, 1, own, width), lambda b, r: (0, s, 0, 0))
    return pl.pallas_call(
        functools.partial(attention_kernel, heads, scale),
        grid_spec=pltpu.PrefetchScalarGridSpec(
            num_scalar_prefetch=1,
            grid=(n_blk,),
            in_specs=[row(query.shape[3], seq)]
            + key_specs(lats[0].shape, y_axis, True)
            + [pl.BlockSpec(up.shape, lambda b, r: (0, 0))],
            out_specs=[row(heads * VALUE, 0), pl.BlockSpec((BLOCK, 128), lambda b, r: (0, 0))],
            scratch_shapes=[
                pltpu.VMEM((heads, BLOCK, 128), F32),
                pltpu.VMEM((heads, BLOCK, HEAD), F32),
            ],
        ),
        out_shape=[
            jax.ShapeDtypeStruct((n_head, 1, own, heads * VALUE), BF16),
            jax.ShapeDtypeStruct((BLOCK, 128), F32),
        ],
        cost_estimate=pl.CostEstimate(
            flops=n_blk * BLOCK * 2 * (RANK * up.shape[1] + heads * BLOCK * 640),
            bytes_accessed=lats[0].size * 4 + up.size * 2 + query.size * 2,
            transcendentals=n_blk * heads * BLOCK * BLOCK,
        ),
        name="attention",
    )(at, query, *lats, up)


def attention_back_kernel(
    heads, scale, at_ref, q_ref, lata_ref, latb_ref, up_ref, att_ref, datt_ref, lse_ref,
    dq_ref, dlata_ref, dlatb_ref, dup_ref, delta_ref, dq_acc, up_acc,
):
    step = pl.program_id(0)
    last = pl.num_programs(0) - 1

    @pl.when(step == 0)
    def _():
        up_acc[...] = jnp.zeros_like(up_acc)

    @pl.when(step == 0)
    def _():
        dq_acc[...] = jnp.zeros_like(dq_acc)
        prod = att_ref[...].astype(F32) * datt_ref[...].astype(F32)
        prod = prod.reshape(BLOCK, heads * VALUE)
        for h in range(heads):
            delta_ref[h] = jnp.broadcast_to(
                jnp.sum(prod[:, h * VALUE : (h + 1) * VALUE], axis=1, keepdims=True), (BLOCK, 128)
            )

    @pl.when(step <= at_ref[0])
    def _():
        lat = both_cores(lata_ref, latb_ref)
        latn = lat[:, :RANK]
        kv = dot(latn, up_ref[...]).astype(BF16)
        query = q_ref[...].reshape(BLOCK, heads * HEAD)
        d_att = datt_ref[...].reshape(BLOCK, heads * VALUE)
        d_key = jnp.zeros((BLOCK, HEAD - NOPE), F32)
        d_kv = []
        for h in range(heads):
            at = h * (NOPE + VALUE)
            q_h = query[:, h * HEAD : (h + 1) * HEAD]
            d_h = d_att[:, h * VALUE : (h + 1) * VALUE]
            keys = jnp.concatenate([kv[:, at : at + NOPE], lat[:, RANK:]], axis=1)
            prob = jnp.exp(dot_nt(q_h, keys) * scale - lse_ref[:, h : h + 1])
            d_prob = dot_nt(d_h, kv[:, at + NOPE : at + NOPE + VALUE])
            d_score = (prob * (d_prob - delta_ref[h][:, :1]) * scale).astype(BF16)
            dq_acc[h] = dq_acc[h] + dot(d_score, keys)
            d_both = dot_tn(d_score, q_h)
            d_kv.append(d_both[:, :NOPE])
            d_kv.append(dot_tn(prob.astype(BF16), d_h))
            d_key = d_key + d_both[:, NOPE:]
        d_kv = jnp.concatenate(d_kv, axis=1).astype(BF16)
        up_acc[...] += dot_tn(latn, d_kv)
        d_lat = dot_nt(d_kv, up_ref[...]).astype(BF16)
        d_key = d_key.astype(BF16)
        for i, ref in enumerate((dlata_ref, dlatb_ref)):
            here = slice(i * (BLOCK // 2), (i + 1) * (BLOCK // 2))
            shape = ref.shape[:4]
            ref[:, :, :, :, :RANK] = d_lat[here].reshape(shape + (RANK,))
            ref[:, :, :, :, RANK:] = d_key[here].reshape(shape + (-1,))

    @pl.when(step > at_ref[0])
    def _():
        dlata_ref[...] = jnp.zeros_like(dlata_ref)
        dlatb_ref[...] = jnp.zeros_like(dlatb_ref)

    @pl.when(step == last)
    def _():
        for h in range(heads):
            dq_ref[:, :, :, h * HEAD : (h + 1) * HEAD] = (
                dq_acc[h].astype(BF16).reshape(dq_ref.shape[:3] + (HEAD,))
            )

    @pl.when(step == last)
    def _():
        dup_ref[...] = up_acc[...]


def attention_back(at, seq, query, lats, up, att, d_att, lse, y_axis, heads):
    n_head, own = query.shape[0], query.shape[2]
    n_blk = (at.shape[0] - 1) // 2
    scale = (NOPE + ROPE) ** -0.5
    row = lambda width, s: pl.BlockSpec((n_head, 1, own, width), lambda b, r: (0, s, 0, 0))
    whole = lambda x: pl.BlockSpec(x.shape, lambda b, r: (0, 0))
    return pl.pallas_call(
        functools.partial(attention_back_kernel, heads, scale),
        grid_spec=pltpu.PrefetchScalarGridSpec(
            num_scalar_prefetch=1,
            grid=(n_blk,),
            in_specs=[row(query.shape[3], seq)]
            + key_specs(lats[0].shape, y_axis, True)
            + [whole(up), row(heads * VALUE, 0), row(heads * VALUE, seq)]
            + [whole(lse)],
            out_specs=[row(query.shape[3], 0)] + key_specs(lats[0].shape, y_axis, False) + [whole(up)],
            scratch_shapes=[
                pltpu.VMEM((heads, BLOCK, 128), F32),
                pltpu.VMEM((heads, BLOCK, HEAD), F32),
                pltpu.VMEM(up.shape, F32),
            ],
        ),
        out_shape=[
            jax.ShapeDtypeStruct((n_head, 1, own, query.shape[3]), BF16),
            jax.ShapeDtypeStruct(lats[0].shape, BF16),
            jax.ShapeDtypeStruct(lats[0].shape, BF16),
            jax.ShapeDtypeStruct(up.shape, F32),
        ],
        cost_estimate=pl.CostEstimate(
            flops=n_blk * BLOCK * 2 * (3 * RANK * up.shape[1] + heads * BLOCK * 1700),
            bytes_accessed=lats[0].size * 8 + up.size * 6 + query.size * 4,
            transcendentals=n_blk * heads * BLOCK * BLOCK,
        ),
        name="attention_back",
    )(at, query, *lats, up, att, d_att, lse)


def pick(own, first_ref, second_ref, out_ref):
    @pl.when(own)
    def _():
        out_ref[...] = first_ref[...]

    @pl.when(jnp.logical_not(own))
    def _():
        out_ref[...] = second_ref[...]


def put(own, value_ref, first_ref, second_ref):
    @pl.when(own)
    def _():
        first_ref[...] = value_ref[...]

    @pl.when(jnp.logical_not(own))
    def _():
        second_ref[...] = value_ref[...]


def gate_lanes(tail, base, local):
    lane = lax.broadcasted_iota(jnp.int32, tail.shape, 1)
    tail = tail.astype(F32)
    return [
        jnp.sum(jnp.where(lane == base + e, tail, 0.0), axis=1, keepdims=True) for e in range(local)
    ]


def spans(size, step):
    return [(at, min(step, size - at)) for at in range(0, size, step)]


def experts_kernel(
    units, local, base_ref, xa_ref, xb_ref, ta_ref, tb_ref, win_ref, wout_ref,
    *refs,
):
    x_ref, gu_ref, outa_ref, outb_ref, tail_ref, act_ref, sum_ref = refs[-7:]
    own = pl.program_id(0) < pl.num_programs(0) // 2
    pick(own, xa_ref, xb_ref, x_ref)
    pick(own, ta_ref, tb_ref, tail_ref)
    gates = gate_lanes(tail_ref[...], base_ref[0], local)
    padded = wout_ref.shape[0]
    for at, size in spans(padded, 256):
        gate = dot_nt(x_ref[...], win_ref[at : at + size, :])
        up = dot_nt(x_ref[...], win_ref[padded + at : padded + at + size, :])
        gu_ref[:, at : at + size] = gate.astype(BF16)
        gu_ref[:, padded + at : padded + at + size] = up.astype(BF16)
        act = gate * jax.nn.sigmoid(gate) * up
        for here in range(0, size, 128):
            expert = (at + here) // units
            part = act[:, here : here + 128]
            part = part * gates[expert] if expert < local else part
            act_ref[:, at + here : at + here + 128] = part.astype(BF16)
    for at, size in spans(wout_ref.shape[1], 512):
        sum_ref[:, at : at + size] = dot(act_ref[...], wout_ref[:, at : at + size]).astype(BF16)
    put(own, sum_ref, outa_ref, outb_ref)


def half_specs(tile, steps, width, column=0):
    half = steps // 2
    return [
        pl.BlockSpec((tile, width), lambda i, r: (jnp.minimum(i, half - 1), column)),
        pl.BlockSpec((tile, width), lambda i, r: (jnp.maximum(i - half, 0), column)),
    ]


def tile_of(half, start):
    return max(t for t in range(16, 385, 16) if half % t == 0 and start % t == 0)


def resident(x):
    return pl.BlockSpec(x.shape, lambda i, r: (0, 0), pipeline_mode=pl.Buffered(1))


def stored(total, sizes, tile, start, stores, first_in):
    at = start // tile
    specs = [pl.BlockSpec((tile, size), lambda i, r: (i + at, 0)) for size in sizes]
    shapes = [jax.ShapeDtypeStruct((total, size), BF16) for size in sizes]
    aliases = {first_in + i: i for i in range(len(stores))}
    return specs, shapes, [pl.BlockSpec(memory_space=pl.ANY) for _ in stores], aliases


def run_experts(base, pair, win, wout, units, local, total, start, stores):
    half, width, padded = pair[0].shape[0], wout.shape[1], wout.shape[0]
    tile = tile_of(half, start)
    steps = 2 * half // tile
    row = lambda size: pl.BlockSpec((tile, size), lambda i, r: (i, 0))
    rows = 2 * half
    shape = lambda count, size: jax.ShapeDtypeStruct((count, size), BF16)
    store_out, store_shapes, store_in, aliases = stored(total, (width,), tile, start, stores, 7)
    return pl.pallas_call(
        functools.partial(experts_kernel, units, local),
        grid_spec=pltpu.PrefetchScalarGridSpec(
            num_scalar_prefetch=1,
            grid=(steps,),
            in_specs=half_specs(tile, steps, width)
            + half_specs(tile, steps, 128, width // 128)
            + [resident(win), resident(wout)]
            + store_in,
            out_specs=store_out + [row(2 * padded)] + half_specs(tile, steps, width),
            scratch_shapes=[
                pltpu.VMEM((tile, 128), BF16),
                pltpu.VMEM((tile, padded), BF16),
                pltpu.VMEM((tile, width), BF16),
            ],
        ),
        out_shape=store_shapes + [shape(rows, 2 * padded), shape(half, width), shape(half, width)],
        input_output_aliases=aliases,
        cost_estimate=pl.CostEstimate(
            flops=rows * width * padded * 6,
            bytes_accessed=(rows * (3 * width + 2 * padded) + 3 * width * padded) * 2,
            transcendentals=rows * padded,
        ),
        name="experts",
    )(base, *pair, *pair, win, wout, *stores)


def experts_back_kernel(
    units, local, base_ref, ga_ref, gb_ref, ta_ref, tb_ref, gu_ref, win_ref, wout_ref,
    *refs,
):
    hid_ref, act_ref, g_ref, outa_ref, outb_ref, tail_ref, sum_ref = refs[-7:]
    own = pl.program_id(0) < pl.num_programs(0) // 2
    pick(own, ga_ref, gb_ref, g_ref)
    pick(own, ta_ref, tb_ref, tail_ref)
    gates = gate_lanes(tail_ref[...], base_ref[0], local)
    padded, width = wout_ref.shape
    prods = [jnp.zeros(tail_ref.shape, F32) for _ in range(local)]
    for at, size in spans(padded, 256):
        d_acts = dot_nt(g_ref[...], wout_ref[at : at + size, :])
        for here in range(0, size, 128):
            unit = at + here
            expert = unit // units
            d_act = d_acts[:, here : here + 128]
            gate = gu_ref[:, unit : unit + 128].astype(F32)
            up = gu_ref[:, padded + unit : padded + unit + 128].astype(F32)
            sig = jax.nn.sigmoid(gate)
            silu = gate * sig
            act = silu * up
            if expert < local:
                prods[expert] = prods[expert] + act * d_act
                d_act = d_act * gates[expert]
                act = act * gates[expert]
            hid_ref[:, unit : unit + 128] = (d_act * up * (sig + silu * (1.0 - sig))).astype(BF16)
            hid_ref[:, padded + unit : padded + unit + 128] = (d_act * silu).astype(BF16)
            act_ref[:, unit : unit + 128] = act.astype(BF16)
    for at, size in spans(width, 512):
        sum_ref[:, at : at + size] = dot(hid_ref[...], win_ref[:, at : at + size]).astype(BF16)
    lane = lax.broadcasted_iota(jnp.int32, tail_ref.shape, 1)
    extra = jnp.zeros(tail_ref.shape, F32)
    for e in range(local):
        extra = jnp.where(lane == base_ref[0] + e, jnp.sum(prods[e], axis=1, keepdims=True), extra)
    sum_ref[:, width:] = extra.astype(BF16)
    put(own, sum_ref, outa_ref, outb_ref)


def run_experts_back(base, grads, pair, gu, win, wout, units, local, total, start, stores):
    half, width, padded = grads[0].shape[0], wout.shape[1], wout.shape[0]
    tile = tile_of(half, start)
    steps = 2 * half // tile
    row = lambda size: pl.BlockSpec((tile, size), lambda i, r: (i, 0))
    rows = 2 * half
    shape = lambda count, size: jax.ShapeDtypeStruct((count, size), BF16)
    store_out, store_shapes, store_in, aliases = stored(
        total, (2 * padded, padded, width), tile, start, stores, 8
    )
    return pl.pallas_call(
        functools.partial(experts_back_kernel, units, local),
        grid_spec=pltpu.PrefetchScalarGridSpec(
            num_scalar_prefetch=1,
            grid=(steps,),
            in_specs=half_specs(tile, steps, width)
            + half_specs(tile, steps, 128, width // 128)
            + [row(2 * padded), resident(win), resident(wout)]
            + store_in,
            out_specs=store_out + half_specs(tile, steps, width + 128),
            scratch_shapes=[pltpu.VMEM((tile, 128), BF16), pltpu.VMEM((tile, width + 128), BF16)],
        ),
        out_shape=store_shapes + [shape(half, width + 128), shape(half, width + 128)],
        input_output_aliases=aliases,
        cost_estimate=pl.CostEstimate(
            flops=rows * width * padded * 6,
            bytes_accessed=(rows * (3 * width + 5 * padded) + 3 * width * padded) * 2,
            transcendentals=rows * padded,
        ),
        name="experts_back",
    )(base, *grads, *pair, gu, win, wout, *stores)


def on_device(
    states, teacher, valid, routes, norm_in, w_query, w_down_kv, norm_kv, w_up_kv, w_out, norm_ffn,
    w_router, shared_in, shared_out, expert_in, expert_out,
):
    n_blk, n_head = lax.axis_size("blk"), lax.axis_size("head")
    blk, head = lax.axis_index("blk"), lax.axis_index("head")
    own_pos, seqs, width = states.shape
    block_pos = own_pos * n_head
    rows = own_pos * seqs
    block_rows = rows * n_head
    total_rows = block_rows * n_blk
    experts = w_router.shape[1]
    local = expert_in.shape[0]
    eff = expert_in.shape[3]
    shared = shared_in.shape[2] // n_blk
    heads = w_query.shape[1] // (NOPE + ROPE)
    scale = (NOPE + ROPE) ** (-0.5)
    assert block_pos == BLOCK and seqs == 2
    blks, heads_ring = blk_dims(n_blk), head_dims(n_head)

    def gather_head(x):
        return gather_axis(x, heads_ring).reshape((-1,) + x.shape[1:])

    def scatter_head(x):
        return scatter_axis(x.reshape((n_head, -1) + x.shape[1:]), heads_ring)

    def take_own(x):
        own = lax.dynamic_slice_in_dim(x, head * own_pos, own_pos, 0)
        return jnp.moveaxis(own, 1, 0).reshape((rows,) + x.shape[2:])

    part = width // n_blk
    quarter = part // n_head
    lat_width = RANK + ROPE
    small = jnp.concatenate(
        [norm_in, norm_ffn, w_router.reshape(-1), norm_kv, jnp.sum(valid, axis=1).astype(BF16)]
    )
    lines = -(-small.shape[0] // lat_width // 16) * 16
    small = jnp.pad(small, (0, lines * lat_width - small.shape[0])).reshape(lines, lat_width)
    down = lax.dynamic_slice_in_dim(w_down_kv, head * quarter, quarter, 0)
    down = gather_axis(jnp.concatenate([down, small], axis=0), blks)
    small = down[:, quarter:].reshape(n_blk, -1)
    down = jnp.moveaxis(gather_axis(down[:, :quarter], heads_ring), 0, 1).reshape(width, lat_width)
    lanes = heads * ROPE // 2
    wq = w_query.reshape(part, heads, NOPE + ROPE)
    wq = jnp.concatenate(
        [
            wq[:, :, :NOPE].reshape(part, -1),
            wq[:, :, NOPE : NOPE + ROPE // 2].reshape(part, -1),
            wq[:, :, NOPE + ROPE // 2 :].reshape(part, -1),
        ],
        axis=1,
    )
    most = part * 3 // 4
    wq_most = gather_dims(wq[None, :most], blks[:1])
    wq_rest = gather_dims(wq[None, most:], blks[:0:-1])
    states_blk = gather_head(jnp.moveaxis(states, 1, 0).reshape(rows, width))
    down, wq_most, wq_rest = lax.optimization_barrier((down, wq_most, wq_rest))
    wq_most = in_order(gather_dims(wq_most, blks[1:]), blks)
    wq_rest = in_order(gather_dims(wq_rest, blks[:1]), blks[::-1])
    wq = jnp.concatenate([wq_most, wq_rest], axis=1).reshape(width, -1)
    gain_in = small[:, :part].reshape(-1).astype(F32)
    gain_ffn = small[:, part : 2 * part].reshape(-1).astype(F32)
    at = 2 * part
    router = small[:, at : at + part * experts].reshape(width, experts)
    at += part * experts
    gain_kv = small[:, at : at + RANK // n_blk].reshape(-1).astype(F32)
    at += RANK // n_blk
    count = jnp.sum(small[:, at : at + block_pos].astype(F32))
    wup = lax.all_gather(w_up_kv, "blk", axis=0, tiled=True)
    wo, wup = phase((w_out, wup))
    wo = lax.all_gather(wo, "blk", axis=1, tiled=True)

    pieces = jnp.concatenate(
        [
            jnp.transpose(shared_in.reshape(part, 2, n_blk, shared), (2, 1, 3, 0)).reshape(
                n_blk, 2 * shared, part
            ),
            shared_out.reshape(n_blk, shared, part),
        ],
        axis=1,
    )
    units = -(-eff // 128) * 128
    shared_units = -(-shared // 128) * 128
    padded = local * units + shared_units
    tall = lambda x, size: jnp.pad(x, ((0, size - x.shape[0]), (0, 0)))

    def expert_weights(values):
        expert_in, expert_out, pieces = values
        mine = jnp.transpose(pieces, (1, 0, 2)).reshape(3, shared, width)
        rows_in = jnp.transpose(expert_in, (0, 2, 3, 1))
        win = [
            block
            for side in range(2)
            for block in [tall(rows_in[e, side], units) for e in range(local)]
            + [tall(mine[side], shared_units)]
        ]
        wout = [tall(expert_out[e], units) for e in range(local)] + [tall(mine[2], shared_units)]
        return jnp.concatenate(win, axis=0), jnp.concatenate(wout, axis=0)

    x_own = jnp.moveaxis(states, 1, 0).reshape(rows, width).astype(F32)
    h1_f, rstd_in = normed(x_own, gain_in)
    h1_own = h1_f.astype(BF16)
    h1_blk = normed(states_blk.astype(F32), gain_in)[0].astype(BF16)
    pos_own = blk * block_pos + head * own_pos + jnp.arange(own_pos, dtype=jnp.int32)
    table_own = jnp.tile(angles(pos_own), (seqs, 1))
    pos_blk = blk * block_pos + jnp.arange(block_pos, dtype=jnp.int32)
    table_blk = jnp.broadcast_to(
        angles(pos_blk).reshape(n_head, 1, own_pos, ROPE // 2), (n_head, seqs, own_pos, ROPE // 2)
    ).reshape(block_rows, ROPE // 2)
    lat = dot(h1_own, down)
    lat_c = lat[:, :RANK]
    latn_f, rstd_kv = normed(lat_c, gain_kv)
    payload = jnp.concatenate(
        [latn_f, rotate(lat[:, RANK:], table_own), jnp.zeros((rows, 128 - ROPE), F32)], axis=1
    ).astype(BF16)
    z, inner, y, _ = split_dims(n_blk, n_head)
    order = [z[2], y[0][2], n_blk // z[2]]
    payload, pieces = phase((by_rows(payload), pieces))
    pieces = lax.all_to_all(pieces, "blk", split_axis=0, concat_axis=0, tiled=True)
    *lats, (wup, wo) = gather_two(payload, n_blk, n_head, (wup, wo))
    lats = [
        [x.reshape(tuple(shape) + (own_pos, -1)) for x in pair]
        for pair, shape in zip(lats, ([order[2], order[1], order[0]], [order[1], order[2], order[0]]))
    ]
    key_blocks = jnp.arange(n_blk, dtype=jnp.int32)
    key_at = jnp.concatenate(
        [jnp.full((1,), blk, jnp.int32), relative(inner, key_blocks) + 0 * key_blocks, relative([z], key_blocks)]
    ).astype(jnp.int32)
    query = dot(h1_blk, wq)
    cosine = jnp.tile(jnp.cos(table_blk), (1, heads))
    sine = jnp.tile(jnp.sin(table_blk), (1, heads))
    q_first, q_second = query[:, -2 * lanes : -lanes], query[:, -lanes:]
    turned = (q_first * cosine - q_second * sine, q_second * cosine + q_first * sine)
    step = ROPE // 2
    query = jnp.concatenate(
        [
            block
            for h in range(heads)
            for block in (
                query[:, h * NOPE : (h + 1) * NOPE],
                *(half[:, h * step : (h + 1) * step] for half in turned),
                jnp.zeros((block_rows, HEAD - NOPE - ROPE), F32),
            )
        ],
        axis=1,
    ).astype(BF16)
    shape4 = (n_head, seqs, own_pos, -1)
    query = query.reshape(shape4)
    seq_axes = list(zip(range(seqs), lats, (1, 0)))
    att_seqs, lses = zip(*(attention(key_at, s, query, pair, wup, axis, heads) for s, pair, axis in seq_axes))
    att_rows = jnp.concatenate(att_seqs, axis=1).reshape(block_rows, heads * VALUE)
    y_own = x_own + scatter_head(dot(att_rows, wo).astype(BF16)).astype(F32)
    h2_f, rstd_ffn = normed(y_own, gain_ffn)
    h2_own = h2_f.astype(BF16)

    routes_own = take_own(routes)
    mask = jnp.any(routes_own[:, :, None] == jnp.arange(experts, dtype=jnp.int32), axis=1)
    logits = jnp.where(mask, dot(h2_own, router), -1e30)
    gates = jnp.where(mask, jnp.exp(logits - jnp.max(logits, axis=1, keepdims=True)), 0.0)
    gates = gates / jnp.sum(gates, axis=1, keepdims=True)
    assert experts <= 128
    tail = jnp.zeros((rows, 128 - experts), BF16)
    base = jnp.full((1,), blk * local, jnp.int32)
    x_ext = jnp.concatenate([h2_own, gates.astype(BF16), tail], axis=1)
    rounds = max(1, total_rows // 4096)

    def in_turn(run, parts, count):
        outs, sums, stores, start = [], [], (), 0
        total = sum(2 * part[0][0].shape[0] for part in parts)
        for i, part in enumerate(parts):
            if i == 2:
                sums[0], part = phase((sums[0], part))
            outs.append(run(*part, total, start, stores))
            stores = outs[-1][:count]
            start += 2 * part[0][0].shape[0]
            sums.append(sum_cores(outs[-1][-2:], n_blk, n_head))
        return outs, sums

    def forward(x_rows, weights=None):
        if weights is None:
            pairs, (win, wout) = gather_parts(
                x_rows, n_blk, n_head, expert_weights, (expert_in, expert_out, pieces)
            )
        else:
            pairs, (win, wout) = gather_parts(x_rows, n_blk, n_head)[0], weights
        outs, sums = in_turn(
            lambda pair, *rest: run_experts(base, pair, win, wout, units, local, *rest),
            [(pair,) for pair in pairs],
            1,
        )
        kept = [(pair, out[1]) for pair, out in zip(pairs, outs)], outs[-1][0]
        return kept, (win, wout), scatter_parts(sums, n_blk, n_head)[0]

    def products(values):
        return tuple(dot_tn(values[i], values[i + 1]) for i in range(0, len(values), 2))

    def backward(grad_rows, kept, weights):
        win, wout = weights
        parts, x_all = kept
        outs, sums = in_turn(
            lambda grads, pair, gu, *rest: run_experts_back(
                base, grads, pair, gu, win, wout, units, local, *rest
            ),
            [
                (grads, pair, gu)
                for grads, (pair, gu) in zip(gather_parts(grad_rows, n_blk, n_head)[0], parts)
            ],
            3,
        )
        hid_all, act_all, grad_all = outs[-1][:3]
        back, ((d_win,), (d_wout,), _) = scatter_parts(
            sums, n_blk, n_head, (products, products, no_fill), ((hid_all, x_all), (act_all, grad_all), ())
        )
        return back, d_win, d_wout

    def in_rounds(x):
        return x.reshape((rounds, -1) + x.shape[1:])

    if rounds == 1:
        kept, weights, mixed = forward(x_ext)
    else:
        weights = expert_weights((expert_in, expert_out, pieces))
        mixed = lax.map(lambda x: forward(x, weights)[2], in_rounds(x_ext)).reshape(rows, width)
    mixed = mixed.astype(F32)
    out_own = (y_own + mixed).astype(BF16)
    diff = out_own.astype(F32) - take_own(teacher).astype(F32)
    valid_own = take_own(valid).astype(F32)[:, None]
    loss_part = jnp.sum(valid_own * diff * diff)
    grad_own = diff * valid_own * (total_rows / count)

    grad_own_b = grad_own.astype(BF16)
    if rounds == 1:
        back, d_win, d_wout = backward(grad_own_b, kept, weights)
    else:

        def round_back(sums, both):
            kept, _, _ = forward(both[0], weights)
            back, d_win, d_wout = backward(both[1], kept, weights)
            return (sums[0] + d_win, sums[1] + d_wout), back

        start = (jnp.zeros((2 * padded, width), F32), jnp.zeros((padded, width), F32))
        (d_win, d_wout), back = lax.scan(round_back, start, (in_rounds(x_ext), in_rounds(grad_own_b)))
        back = back.reshape(rows, -1)
    d_sh = jnp.concatenate(
        [d_win[s * padded + local * units :][:shared] for s in range(2)]
        + [d_wout[local * units :][:shared]],
        axis=0,
    ).astype(BF16)
    d_sh = jnp.transpose(d_sh.reshape(3 * shared, n_blk, part), (1, 0, 2))
    back, d_win, d_wout, d_sh = lax.optimization_barrier((back, d_win, d_wout, d_sh))
    back = back.astype(F32)
    d_sh = lax.all_to_all(d_sh, "blk", split_axis=0, concat_axis=0, tiled=True).astype(F32)
    grad_shin = jnp.transpose(d_sh[:, : 2 * shared].reshape(n_blk, 2, shared, part), (3, 1, 0, 2)).reshape(
        part, 2, n_blk * shared
    )
    grad_shout = d_sh[:, 2 * shared :].reshape(n_blk * shared, part)

    d_gates = back[:, width : width + experts]
    d_logits = gates * (d_gates - jnp.sum(gates * d_gates, axis=1, keepdims=True))
    d_logits = d_logits.astype(BF16)
    grad_router = dot_tn(h2_own, d_logits)
    dh2 = back[:, :width] + dot_nt(d_logits, router)
    dy_branch, grad_gain_ffn = norm_back(dh2, y_own, rstd_ffn, gain_ffn)
    dy_own = grad_own + dy_branch

    dy_blk = gather_head(dy_own.astype(BF16))
    grad_wo = dot_tn(att_rows, dy_blk).astype(BF16)
    d_att = dot_nt(dy_blk, wo).astype(BF16).reshape(shape4)
    grad_wo, d_att = phase((grad_wo, d_att))
    wo_steps = scatter_columns(grad_wo, n_blk)
    dqs, d_lats, d_ups = [], [], []
    for (s, pair, axis), att, lse in zip(seq_axes, att_seqs, lses):
        dq, first, second, d_up = attention_back(
            key_at, s, query, pair, wup, att, d_att, lse, axis, heads
        )
        if s == 0:
            grad_wo, d_att = phase((next(wo_steps), d_att))
        dqs.append(dq)
        d_lats.append([x.reshape(total_rows // 4, -1) for x in (first, second)])
        d_ups.append(d_up)
    for grad_wo in wo_steps:
        pass
    grad_wo = grad_wo.astype(F32)
    dq = jnp.concatenate(dqs, axis=1)
    d_up = sum(d_ups).astype(BF16)
    dq = dq.reshape(block_rows, heads, HEAD)
    first, second = (
        dq[:, :, at : at + step].reshape(block_rows, lanes).astype(F32) for at in (NOPE, NOPE + step)
    )
    dq = jnp.concatenate(
        [
            dq[:, :, :NOPE].reshape(block_rows, heads * NOPE),
            (first * cosine + second * sine).astype(BF16),
            (second * cosine - first * sine).astype(BF16),
        ],
        axis=1,
    )
    dh1 = scatter_head(dot_nt(dq, wq).astype(BF16)).astype(F32)
    up_rows = w_up_kv.shape[0]
    wide = up_rows * w_up_kv.shape[1] // part
    grad_wq = by_rows(dot_tn(h1_blk, dq).astype(BF16)).reshape(n_blk, part, -1)
    d_up = jnp.moveaxis(d_up.reshape(n_blk, up_rows, -1, wide), 2, 1).reshape(n_blk, part, wide)
    joined = jnp.concatenate([grad_wq, d_up], axis=2)
    d_lat, (joined, d_win, d_wout) = scatter_two(*d_lats, n_blk, n_head, (by_rows(joined), d_win, d_wout))
    d_lat = by_rows(d_lat)[:, : RANK + ROPE].astype(F32)
    joined = by_rows(lax.psum_scatter(joined, "blk", scatter_dimension=0, tiled=False)).astype(F32)
    grad_wq = joined[:, :-wide]
    grad_up = jnp.moveaxis(joined[:, -wide:].reshape(-1, up_rows, wide), 0, 1).reshape(up_rows, -1)
    grad_ein = d_win.reshape(2, padded, width)[:, : local * units]
    grad_ein = grad_ein.reshape(2, local, units, width)[:, :, :eff]
    grad_ein = jnp.transpose(grad_ein, (1, 3, 0, 2))
    grad_eout = jnp.stack([d_wout[e * units :][:eff] for e in range(local)])
    grad_wq = jnp.concatenate(
        [
            grad_wq[:, : heads * NOPE].reshape(part, heads, NOPE),
            grad_wq[:, heads * NOPE : -lanes].reshape(part, heads, ROPE // 2),
            grad_wq[:, -lanes:].reshape(part, heads, ROPE // 2),
        ],
        axis=2,
    ).reshape(part, -1)
    d_lat_c, grad_gain_kv = norm_back(d_lat[:, :RANK], lat_c, rstd_kv, gain_kv)
    d_lat_b = jnp.concatenate([d_lat_c, rotate(d_lat[:, RANK : RANK + ROPE], -table_own)], axis=1).astype(BF16)
    d_lat_b = by_rows(d_lat_b)
    d_lat_blk = gather_head(d_lat_b)
    grad_down = by_rows(dot_tn(h1_blk, d_lat_blk).astype(BF16)).reshape(n_blk, n_head, quarter, -1)
    grad_down = lax.dynamic_index_in_dim(grad_down, head, 1, keepdims=False)
    grad_down = gather_head(by_rows(scatter_axis(grad_down, blks))).astype(F32)
    dh1 = dh1 + dot_nt(d_lat_b, down)
    dx_branch, grad_gain_in = norm_back(dh1, x_own, rstd_in, gain_in)
    dx_own = dy_own + dx_branch

    loss_high = loss_part.astype(BF16).astype(F32)
    sums = jnp.concatenate(
        [
            grad_gain_in.reshape(n_blk, -1),
            grad_gain_ffn.reshape(n_blk, -1),
            grad_router.reshape(n_blk, -1),
            grad_gain_kv.reshape(n_blk, -1),
            jnp.full((n_blk, 1), loss_high),
            jnp.full((n_blk, 1), loss_part - loss_high),
        ],
        axis=1,
    )
    sums = scatter_axis(sums, blks)
    for dim in heads_ring:
        sums = sum(ring_gather(sums, dim))
    out_gain_in = sums[:part]
    out_gain_ffn = sums[part : 2 * part]
    at = 2 * part
    out_router = sums[at : at + part * experts].reshape(part, experts)
    at += part * experts
    out_gain_kv = sums[at : at + RANK // n_blk]
    loss = (sums[-2] + sums[-1]) / (width * count)

    def give(x):
        return jnp.moveaxis(x.reshape(seqs, own_pos, width), 0, 1)

    return (
        give(out_own), loss, give(dx_own), out_gain_in, grad_wq, grad_down, out_gain_kv, grad_up,
        grad_wo, out_gain_ffn, out_router, grad_shin, grad_shout, grad_ein, grad_eout,
    )


def solution(mesh):
    in_specs = (
        P(BOTH, None, None), P("blk", None, None), P("blk", None), P("blk", None, None), P("blk"),
        P("blk", "head"), P("blk", None), P("blk"), P("blk", "head"), P("head", "blk"), P("blk"),
        P("blk", None), P("blk", None, "head"), P("head", "blk"), P("blk", None, None, "head"),
        P("blk", "head", None),
    )
    out_specs = (
        P(BOTH, None, None), P(), P(BOTH, None, None), P("blk"), P("blk", "head"), P("blk", None),
        P("blk"), P("blk", "head"), P("head", "blk"), P("blk"), P("blk", None), P("blk", None, "head"),
        P("head", "blk"), P("blk", None, None, "head"), P("blk", "head", None),
    )
    return jax.shard_map(on_device, mesh=mesh, in_specs=in_specs, out_specs=out_specs, check_vma=False)
```

```python
import functools

import jax
import jax.numpy as jnp
from jax import lax
from jax.experimental import pallas as pl
from jax.experimental.layout import Layout, with_layout_constraint
from jax.experimental.pallas import tpu as pltpu
from jax.sharding import PartitionSpec as P

NOPE = 128
ROPE = 64
VALUE = 128
RANK = 512
BLOCK = 256
EPS = 1e-06
F32 = jnp.float32
BF16 = jnp.bfloat16
BOTH = ("blk", "head")


def angles(position):
    frequency = 10000.0 ** (-2.0 * jnp.arange(ROPE // 2, dtype=F32) / ROPE)
    return position.astype(F32)[:, None] * frequency[None, :]


def rotate(values, table):
    half = ROPE // 2
    cosine, sine = jnp.cos(table), jnp.sin(table)
    first, second = values[:, :half], values[:, half:]
    return jnp.concatenate([first * cosine - second * sine, second * cosine + first * sine], axis=1)


def normed(values, gain):
    rstd = lax.rsqrt(jnp.mean(values * values, axis=-1, keepdims=True) + EPS)
    return values * rstd * gain, rstd


def norm_back(grad, values, rstd, gain):
    scaled = grad * gain
    out = rstd * scaled - values * rstd**3 * jnp.mean(scaled * values, axis=-1, keepdims=True)
    return out, jnp.sum(grad * values * rstd, axis=0)


def by_rows(x):
    return with_layout_constraint(x, Layout(tuple(range(x.ndim))))


def dot(a, b):
    return jnp.dot(a, b, preferred_element_type=F32)


def dot_nt(a, b):
    return lax.dot_general(a, b, (((1,), (1,)), ((), ())), preferred_element_type=F32)


def dot_tn(a, b):
    return lax.dot_general(a, b, (((0,), (0,)), ((), ())), preferred_element_type=F32)


def blk_dims(n_blk):
    if n_blk == 8:
        return [("blk", 2, 4), ("blk", 1, 2)]
    if n_blk == 32:
        return [("blk", 8, 4), ("blk", 2, 4), ("blk", 1, 2)]
    return [("blk", 1, n_blk)]


def head_dims(n_head):
    return [("head", 2, n_head // 2), ("head", 1, 2)] if n_head % 2 == 0 else [("head", 1, n_head)]


def shift(x, dim, by):
    axis, stride, size = dim
    pairs = []
    for i in range(lax.axis_size(axis)):
        digit = i // stride % size
        pairs.append((i, i + ((digit + by) % size - digit) * stride))
    return lax.ppermute(x, axis, pairs)


def digit_of(dim):
    axis, stride, size = dim
    return lax.axis_index(axis) // stride % size


def ring_gather(x, dim):
    pieces = [x]
    for _ in range(dim[2] - 1):
        pieces.append(shift(pieces[-1], dim, -1))
    return pieces


def ring_scatter(pieces, dim):
    total = pieces[-1]
    for piece in pieces[-2::-1]:
        total = shift(total, dim, 1) + piece
    return total


def direct_gather(x, dim):
    return [x] + [shift(x, dim, -k) for k in range(1, dim[2])]


def direct_scatter(pieces, dim):
    total = pieces[0].astype(F32)
    for k in range(1, dim[2]):
        total = total + shift(pieces[k], dim, k).astype(F32)
    return total.astype(pieces[0].dtype)


def gather_dims(x, dims, step=ring_gather):
    for dim in dims:
        x = jnp.concatenate(step(x, dim), axis=0)
    return x


def scatter_dims(x, dims, step=ring_scatter):
    for dim in reversed(dims):
        x = step(jnp.split(x, dim[2], axis=0), dim)
    return x


def relative(dims, index):
    place, scale = 0, 1
    for dim in dims:
        place = place + (index // dim[1] % dim[2] - digit_of(dim)) % dim[2] * scale
        scale *= dim[2]
    return place


def absolute(dims, place):
    index = 0
    for dim in dims:
        index = index + (place % dim[2] + digit_of(dim)) % dim[2] * dim[1]
        place //= dim[2]
    return index


def gather_axis(x, dims):
    return in_order(gather_dims(x[None], dims, direct_gather), dims)


def in_order(stack, dims):
    n = stack.shape[0]
    return jnp.concatenate(
        [lax.dynamic_slice_in_dim(stack, relative(dims, i), 1, 0) for i in range(n)], axis=0
    )


def scatter_axis(x, dims):
    n = lax.axis_size(dims[0][0])
    stack = jnp.concatenate(
        [lax.dynamic_slice_in_dim(x, absolute(dims, i), 1, 0) for i in range(n)], axis=0
    )
    return scatter_dims(stack, dims, direct_scatter)[0]


def split_dims(n_blk, n_head):
    blk, head = blk_dims(n_blk), head_dims(n_head)
    return blk[0], blk[1:], head[:-1], head[-1]


phase = lax.optimization_barrier


def no_fill(values):
    return values


def gather_parts(x, n_blk, n_head, fill=no_fill, fill_in=()):
    third = x.shape[0] * 5 // 16
    first = x.shape[0] - 2 * third
    z, inner, y, core = split_dims(n_blk, n_head)
    a, pieces = x[:first], [x[first:]]
    for dims in [inner, y] + [[]] * (z[2] - 4):
        piece, a = phase((shift(pieces[-1], z, -1), gather_dims(a, dims)))
        pieces.append(piece)
    pieces.append(shift(pieces[-1], z, -1))
    b = jnp.concatenate([p[:third] for p in pieces], axis=0)
    c = jnp.concatenate([p[third:] for p in pieces], axis=0)
    b, c, a = phase((b, c, a))
    b, c, last, fill_in = phase((gather_dims(b, y), gather_dims(c, inner), shift(a, z, -1), fill_in))
    pieces = [a, last]
    for _ in range(z[2] - 2):
        pieces.append(shift(pieces[-1], z, -1))
    b, c, pieces, filled = phase((gather_dims(b, inner), gather_dims(c, y), pieces, fill(fill_in)))
    return [ring_gather(part, core) for part in (b, c, jnp.concatenate(pieces, axis=0))], filled


def scatter_parts(sums, n_blk, n_head, fills=(no_fill,) * 2, fill_ins=((),) * 2):
    z, inner, y, _ = split_dims(n_blk, n_head)
    b, c, a, filled = phase((*sums, fill_ins[0]))
    pieces = jnp.split(a, z[2], axis=0)

    def advance(total, steps):
        for _ in range(steps):
            total = shift(total, z, 1) + pieces.pop()
        return total

    each = 1 if fill_ins[0] else z[2] - 2
    b, c, a, filled, fill_in = phase(
        (scatter_dims(b, inner), scatter_dims(c, y), advance(pieces.pop(), each), fills[0](filled), fill_ins[1])
    )
    outs = [filled]
    b, c, a, filled = phase((scatter_dims(b, y), scatter_dims(c, inner), advance(a, 1), fills[1](fill_in)))
    outs.append(filled)
    both = [
        jnp.concatenate(rows, axis=0)
        for rows in zip(jnp.split(b, z[2], axis=0), jnp.split(c, z[2], axis=0))
    ]
    total = both.pop()
    a = advance(a, len(pieces))
    for dims in [y, inner] + [[]] * (z[2] - 3):
        total, a = phase((shift(total, z, 1) + both.pop(), scatter_dims(a, dims)))
    return jnp.concatenate([a, total], axis=0), outs


def scatter_columns(x, n_blk):
    c = x.shape[1] // n_blk
    for dim in reversed(blk_dims(n_blk)):
        size = dim[2]
        pieces = []
        for k in range(size):
            place = (digit_of(dim) + k) % size
            pieces.append(
                jnp.concatenate(
                    [
                        lax.dynamic_slice_in_dim(x, (outer * size + place) * c, c, 1)
                        for outer in range(x.shape[1] // c // size)
                    ],
                    axis=1,
                )
            )
        x = direct_scatter(pieces, dim)
        yield x


def sum_cores(pair, n_blk, n_head):
    return ring_scatter(pair, split_dims(n_blk, n_head)[3])


def gather_two(x, n_blk, n_head, beside):
    half = x.shape[0] // 2
    z, inner, y, core = split_dims(n_blk, n_head)
    pieces = direct_gather(x, z)
    b = jnp.concatenate([p[:half] for p in pieces], axis=0)
    c = jnp.concatenate([p[half:] for p in pieces], axis=0)
    b, c = phase((gather_dims(b, y), gather_dims(c, inner)))
    b, c, beside = phase((gather_dims(b, inner), gather_dims(c, y), beside))
    return direct_gather(b, core), direct_gather(c, core), beside


def scatter_two(b, c, n_blk, n_head, beside):
    z, inner, y, core = split_dims(n_blk, n_head)
    b, c, beside = phase((direct_scatter(b, core), direct_scatter(c, core), beside))
    b = scatter_dims(b, y + inner)
    c = scatter_dims(c, inner + y)
    pieces = [
        jnp.concatenate(both, axis=0)
        for both in zip(jnp.split(b, z[2], axis=0), jnp.split(c, z[2], axis=0))
    ]
    return direct_scatter(pieces, z), beside


def scatter_blk(x, axis=0):
    return lax.psum_scatter(x, "blk", scatter_dimension=axis, tiled=True)


HEAD = 256


def attention_kernel(
    heads, scale, at_ref, q_ref, lata_ref, latb_ref, up_ref, out_ref, lse_ref, m_ref, acc_ref
):
    step = pl.program_id(0)

    @pl.when(step == 0)
    def _():
        m_ref[...] = jnp.full_like(m_ref, -1e30)
        acc_ref[...] = jnp.zeros_like(acc_ref)

    @pl.when(step <= at_ref[0])
    def _():
        lat = both_cores(lata_ref, latb_ref)
        kv = dot(lat[:, :RANK], up_ref[...]).astype(BF16)
        query = q_ref[...].reshape(BLOCK, heads * HEAD)
        ones = jnp.ones((BLOCK, HEAD - VALUE), BF16)
        for h in range(heads):
            at = h * (NOPE + VALUE)
            keys = jnp.concatenate([kv[:, at : at + NOPE], lat[:, RANK:]], axis=1)
            values = jnp.concatenate([kv[:, at + NOPE : at + NOPE + VALUE], ones], axis=1)
            scores = dot_nt(query[:, h * HEAD : (h + 1) * HEAD], keys) * scale
            old = m_ref[h][:, :1]
            new = jnp.maximum(old, jnp.max(scores, axis=1, keepdims=True))
            expo = jnp.exp(scores - new)
            acc_ref[h] = acc_ref[h] * jnp.exp(old - new) + dot(expo.astype(BF16), values)
            m_ref[h] = jnp.broadcast_to(new, m_ref.shape[1:])

    @pl.when(step == pl.num_programs(0) - 1)
    def _():
        lane = lax.broadcasted_iota(jnp.int32, (BLOCK, 128), 1)
        lse = jnp.zeros((BLOCK, 128), F32)
        for h in range(heads):
            total = acc_ref[h][:, VALUE:]
            out = acc_ref[h][:, :VALUE] / total
            out_ref[:, :, :, h * VALUE : (h + 1) * VALUE] = out.astype(BF16).reshape(
                out_ref.shape[:3] + (VALUE,)
            )
            lse = jnp.where(lane == h, m_ref[h] + jnp.log(total), lse)
        lse_ref[...] = lse


def both_cores(first_ref, second_ref):
    flat = [ref[...].reshape(BLOCK // 2, ref.shape[-1]) for ref in (first_ref, second_ref)]
    return jnp.concatenate(flat, axis=0)


def key_specs(view, y_axis, clamp):
    n_blk = view[0] * view[1] * view[2] // view[y_axis]
    shape = tuple(n if i == y_axis else 1 if i < 3 else n for i, n in enumerate(view))

    def index(step, at):
        step = jnp.minimum(step, at[0]) if clamp else step
        inner, z = at[1 + step], at[1 + n_blk + step]
        return (0, inner, z, 0, 0) if y_axis == 0 else (inner, 0, z, 0, 0)

    return [pl.BlockSpec(shape, index)] * 2


def attention(at, seq, query, lats, up, y_axis, heads):
    n_head, own = query.shape[0], query.shape[2]
    n_blk = (at.shape[0] - 1) // 2
    scale = (NOPE + ROPE) ** -0.5
    row = lambda width, s: pl.BlockSpec((n_head, 1, own, width), lambda b, r: (0, s, 0, 0))
    return pl.pallas_call(
        functools.partial(attention_kernel, heads, scale),
        grid_spec=pltpu.PrefetchScalarGridSpec(
            num_scalar_prefetch=1,
            grid=(n_blk,),
            in_specs=[row(query.shape[3], seq)]
            + key_specs(lats[0].shape, y_axis, True)
            + [pl.BlockSpec(up.shape, lambda b, r: (0, 0))],
            out_specs=[row(heads * VALUE, 0), pl.BlockSpec((BLOCK, 128), lambda b, r: (0, 0))],
            scratch_shapes=[
                pltpu.VMEM((heads, BLOCK, 128), F32),
                pltpu.VMEM((heads, BLOCK, HEAD), F32),
            ],
        ),
        out_shape=[
            jax.ShapeDtypeStruct((n_head, 1, own, heads * VALUE), BF16),
            jax.ShapeDtypeStruct((BLOCK, 128), F32),
        ],
        cost_estimate=pl.CostEstimate(
            flops=n_blk * BLOCK * 2 * (RANK * up.shape[1] + heads * BLOCK * 640),
            bytes_accessed=lats[0].size * 4 + up.size * 2 + query.size * 2,
            transcendentals=n_blk * heads * BLOCK * BLOCK,
        ),
        name="attention",
    )(at, query, *lats, up)


def attention_back_kernel(
    heads, scale, at_ref, q_ref, lata_ref, latb_ref, up_ref, att_ref, datt_ref, lse_ref,
    dq_ref, dlata_ref, dlatb_ref, dup_ref, delta_ref, dq_acc, up_acc,
):
    step = pl.program_id(0)
    last = pl.num_programs(0) - 1

    @pl.when(step == 0)
    def _():
        up_acc[...] = jnp.zeros_like(up_acc)

    @pl.when(step == 0)
    def _():
        dq_acc[...] = jnp.zeros_like(dq_acc)
        prod = att_ref[...].astype(F32) * datt_ref[...].astype(F32)
        prod = prod.reshape(BLOCK, heads * VALUE)
        for h in range(heads):
            delta_ref[h] = jnp.broadcast_to(
                jnp.sum(prod[:, h * VALUE : (h + 1) * VALUE], axis=1, keepdims=True), (BLOCK, 128)
            )

    @pl.when(step <= at_ref[0])
    def _():
        lat = both_cores(lata_ref, latb_ref)
        latn = lat[:, :RANK]
        kv = dot(latn, up_ref[...]).astype(BF16)
        query = q_ref[...].reshape(BLOCK, heads * HEAD)
        d_att = datt_ref[...].reshape(BLOCK, heads * VALUE)
        d_key = jnp.zeros((BLOCK, HEAD - NOPE), F32)
        d_kv = []
        for h in range(heads):
            at = h * (NOPE + VALUE)
            q_h = query[:, h * HEAD : (h + 1) * HEAD]
            d_h = d_att[:, h * VALUE : (h + 1) * VALUE]
            keys = jnp.concatenate([kv[:, at : at + NOPE], lat[:, RANK:]], axis=1)
            prob = jnp.exp(dot_nt(q_h, keys) * scale - lse_ref[:, h : h + 1])
            d_prob = dot_nt(d_h, kv[:, at + NOPE : at + NOPE + VALUE])
            d_score = (prob * (d_prob - delta_ref[h][:, :1]) * scale).astype(BF16)
            dq_acc[h] = dq_acc[h] + dot(d_score, keys)
            d_both = dot_tn(d_score, q_h)
            d_kv.append(d_both[:, :NOPE])
            d_kv.append(dot_tn(prob.astype(BF16), d_h))
            d_key = d_key + d_both[:, NOPE:]
        d_kv = jnp.concatenate(d_kv, axis=1).astype(BF16)
        up_acc[...] += dot_tn(latn, d_kv)
        d_lat = dot_nt(d_kv, up_ref[...]).astype(BF16)
        d_key = d_key.astype(BF16)
        for i, ref in enumerate((dlata_ref, dlatb_ref)):
            here = slice(i * (BLOCK // 2), (i + 1) * (BLOCK // 2))
            shape = ref.shape[:4]
            ref[:, :, :, :, :RANK] = d_lat[here].reshape(shape + (RANK,))
            ref[:, :, :, :, RANK:] = d_key[here].reshape(shape + (-1,))

    @pl.when(step > at_ref[0])
    def _():
        dlata_ref[...] = jnp.zeros_like(dlata_ref)
        dlatb_ref[...] = jnp.zeros_like(dlatb_ref)

    @pl.when(step == last)
    def _():
        for h in range(heads):
            dq_ref[:, :, :, h * HEAD : (h + 1) * HEAD] = (
                dq_acc[h].astype(BF16).reshape(dq_ref.shape[:3] + (HEAD,))
            )

    @pl.when(step == last)
    def _():
        dup_ref[...] = up_acc[...]


def attention_back(at, seq, query, lats, up, att, d_att, lse, y_axis, heads):
    n_head, own = query.shape[0], query.shape[2]
    n_blk = (at.shape[0] - 1) // 2
    scale = (NOPE + ROPE) ** -0.5
    row = lambda width, s: pl.BlockSpec((n_head, 1, own, width), lambda b, r: (0, s, 0, 0))
    whole = lambda x: pl.BlockSpec(x.shape, lambda b, r: (0, 0))
    return pl.pallas_call(
        functools.partial(attention_back_kernel, heads, scale),
        grid_spec=pltpu.PrefetchScalarGridSpec(
            num_scalar_prefetch=1,
            grid=(n_blk,),
            in_specs=[row(query.shape[3], seq)]
            + key_specs(lats[0].shape, y_axis, True)
            + [whole(up), row(heads * VALUE, 0), row(heads * VALUE, seq)]
            + [whole(lse)],
            out_specs=[row(query.shape[3], 0)] + key_specs(lats[0].shape, y_axis, False) + [whole(up)],
            scratch_shapes=[
                pltpu.VMEM((heads, BLOCK, 128), F32),
                pltpu.VMEM((heads, BLOCK, HEAD), F32),
                pltpu.VMEM(up.shape, F32),
            ],
        ),
        out_shape=[
            jax.ShapeDtypeStruct((n_head, 1, own, query.shape[3]), BF16),
            jax.ShapeDtypeStruct(lats[0].shape, BF16),
            jax.ShapeDtypeStruct(lats[0].shape, BF16),
            jax.ShapeDtypeStruct(up.shape, F32),
        ],
        cost_estimate=pl.CostEstimate(
            flops=n_blk * BLOCK * 2 * (3 * RANK * up.shape[1] + heads * BLOCK * 1700),
            bytes_accessed=lats[0].size * 8 + up.size * 6 + query.size * 4,
            transcendentals=n_blk * heads * BLOCK * BLOCK,
        ),
        name="attention_back",
    )(at, query, *lats, up, att, d_att, lse)


def pick(own, first_ref, second_ref, out_ref):
    @pl.when(own)
    def _():
        out_ref[...] = first_ref[...]

    @pl.when(jnp.logical_not(own))
    def _():
        out_ref[...] = second_ref[...]


def put(own, value_ref, first_ref, second_ref):
    @pl.when(own)
    def _():
        first_ref[...] = value_ref[...]

    @pl.when(jnp.logical_not(own))
    def _():
        second_ref[...] = value_ref[...]


def gate_lanes(tail, base, local):
    lane = lax.broadcasted_iota(jnp.int32, tail.shape, 1)
    tail = tail.astype(F32)
    return [
        jnp.sum(jnp.where(lane == base + e, tail, 0.0), axis=1, keepdims=True) for e in range(local)
    ]


def spans(size, step):
    return [(at, min(step, size - at)) for at in range(0, size, step)]


def experts_kernel(
    units, local, base_ref, xa_ref, xb_ref, ta_ref, tb_ref, win_ref, wout_ref,
    *refs,
):
    x_ref, gu_ref, outa_ref, outb_ref, tail_ref, act_ref, sum_ref = refs[-7:]
    own = pl.program_id(0) < pl.num_programs(0) // 2
    pick(own, xa_ref, xb_ref, x_ref)
    pick(own, ta_ref, tb_ref, tail_ref)
    gates = gate_lanes(tail_ref[...], base_ref[0], local)
    padded = wout_ref.shape[0]
    for at, size in spans(padded, 256):
        gate = dot_nt(x_ref[...], win_ref[at : at + size, :])
        up = dot_nt(x_ref[...], win_ref[padded + at : padded + at + size, :])
        gu_ref[:, at : at + size] = gate.astype(BF16)
        gu_ref[:, padded + at : padded + at + size] = up.astype(BF16)
        act = gate * jax.nn.sigmoid(gate) * up
        for here in range(0, size, 128):
            expert = (at + here) // units
            part = act[:, here : here + 128]
            part = part * gates[expert] if expert < local else part
            act_ref[:, at + here : at + here + 128] = part.astype(BF16)
    for at, size in spans(wout_ref.shape[1], 512):
        sum_ref[:, at : at + size] = dot(act_ref[...], wout_ref[:, at : at + size]).astype(BF16)
    put(own, sum_ref, outa_ref, outb_ref)


def half_specs(tile, steps, width, column=0):
    half = steps // 2
    return [
        pl.BlockSpec((tile, width), lambda i, r: (jnp.minimum(i, half - 1), column)),
        pl.BlockSpec((tile, width), lambda i, r: (jnp.maximum(i - half, 0), column)),
    ]


def tile_of(half, start):
    return max(t for t in range(16, 385, 16) if half % t == 0 and start % t == 0)


def resident(x):
    return pl.BlockSpec(x.shape, lambda i, r: (0, 0), pipeline_mode=pl.Buffered(1))


def stored(total, sizes, tile, start, stores, first_in):
    at = start // tile
    specs = [pl.BlockSpec((tile, size), lambda i, r: (i + at, 0)) for size in sizes]
    shapes = [jax.ShapeDtypeStruct((total, size), BF16) for size in sizes]
    aliases = {first_in + i: i for i in range(len(stores))}
    return specs, shapes, [pl.BlockSpec(memory_space=pl.ANY) for _ in stores], aliases


def run_experts(base, pair, win, wout, units, local, total, start, stores):
    half, width, padded = pair[0].shape[0], wout.shape[1], wout.shape[0]
    tile = tile_of(half, start)
    steps = 2 * half // tile
    row = lambda size: pl.BlockSpec((tile, size), lambda i, r: (i, 0))
    rows = 2 * half
    shape = lambda count, size: jax.ShapeDtypeStruct((count, size), BF16)
    store_out, store_shapes, store_in, aliases = stored(total, (width,), tile, start, stores, 7)
    return pl.pallas_call(
        functools.partial(experts_kernel, units, local),
        grid_spec=pltpu.PrefetchScalarGridSpec(
            num_scalar_prefetch=1,
            grid=(steps,),
            in_specs=half_specs(tile, steps, width)
            + half_specs(tile, steps, 128, width // 128)
            + [resident(win), resident(wout)]
            + store_in,
            out_specs=store_out + [row(2 * padded)] + half_specs(tile, steps, width),
            scratch_shapes=[
                pltpu.VMEM((tile, 128), BF16),
                pltpu.VMEM((tile, padded), BF16),
                pltpu.VMEM((tile, width), BF16),
            ],
        ),
        out_shape=store_shapes + [shape(rows, 2 * padded), shape(half, width), shape(half, width)],
        input_output_aliases=aliases,
        cost_estimate=pl.CostEstimate(
            flops=rows * width * padded * 6,
            bytes_accessed=(rows * (3 * width + 2 * padded) + 3 * width * padded) * 2,
            transcendentals=rows * padded,
        ),
        name="experts",
    )(base, *pair, *pair, win, wout, *stores)


def experts_back_kernel(
    units, local, base_ref, ga_ref, gb_ref, ta_ref, tb_ref, gu_ref, win_ref, wout_ref,
    *refs,
):
    hid_ref, act_ref, g_ref, outa_ref, outb_ref, tail_ref, sum_ref = refs[-7:]
    own = pl.program_id(0) < pl.num_programs(0) // 2
    pick(own, ga_ref, gb_ref, g_ref)
    pick(own, ta_ref, tb_ref, tail_ref)
    gates = gate_lanes(tail_ref[...], base_ref[0], local)
    padded, width = wout_ref.shape
    prods = [jnp.zeros(tail_ref.shape, F32) for _ in range(local)]
    for at, size in spans(padded, 256):
        d_acts = dot_nt(g_ref[...], wout_ref[at : at + size, :])
        for here in range(0, size, 128):
            unit = at + here
            expert = unit // units
            d_act = d_acts[:, here : here + 128]
            gate = gu_ref[:, unit : unit + 128].astype(F32)
            up = gu_ref[:, padded + unit : padded + unit + 128].astype(F32)
            sig = jax.nn.sigmoid(gate)
            silu = gate * sig
            act = silu * up
            if expert < local:
                prods[expert] = prods[expert] + act * d_act
                d_act = d_act * gates[expert]
                act = act * gates[expert]
            hid_ref[:, unit : unit + 128] = (d_act * up * (sig + silu * (1.0 - sig))).astype(BF16)
            hid_ref[:, padded + unit : padded + unit + 128] = (d_act * silu).astype(BF16)
            act_ref[:, unit : unit + 128] = act.astype(BF16)
    for at, size in spans(width, 512):
        sum_ref[:, at : at + size] = dot(hid_ref[...], win_ref[:, at : at + size]).astype(BF16)
    lane = lax.broadcasted_iota(jnp.int32, tail_ref.shape, 1)
    extra = jnp.zeros(tail_ref.shape, F32)
    for e in range(local):
        extra = jnp.where(lane == base_ref[0] + e, jnp.sum(prods[e], axis=1, keepdims=True), extra)
    sum_ref[:, width:] = extra.astype(BF16)
    put(own, sum_ref, outa_ref, outb_ref)


def run_experts_back(base, grads, pair, gu, win, wout, units, local, total, start, stores):
    half, width, padded = grads[0].shape[0], wout.shape[1], wout.shape[0]
    tile = tile_of(half, start)
    steps = 2 * half // tile
    row = lambda size: pl.BlockSpec((tile, size), lambda i, r: (i, 0))
    rows = 2 * half
    shape = lambda count, size: jax.ShapeDtypeStruct((count, size), BF16)
    store_out, store_shapes, store_in, aliases = stored(
        total, (2 * padded, padded, width), tile, start, stores, 8
    )
    return pl.pallas_call(
        functools.partial(experts_back_kernel, units, local),
        grid_spec=pltpu.PrefetchScalarGridSpec(
            num_scalar_prefetch=1,
            grid=(steps,),
            in_specs=half_specs(tile, steps, width)
            + half_specs(tile, steps, 128, width // 128)
            + [row(2 * padded), resident(win), resident(wout)]
            + store_in,
            out_specs=store_out + half_specs(tile, steps, width + 128),
            scratch_shapes=[pltpu.VMEM((tile, 128), BF16), pltpu.VMEM((tile, width + 128), BF16)],
        ),
        out_shape=store_shapes + [shape(half, width + 128), shape(half, width + 128)],
        input_output_aliases=aliases,
        cost_estimate=pl.CostEstimate(
            flops=rows * width * padded * 6,
            bytes_accessed=(rows * (3 * width + 5 * padded) + 3 * width * padded) * 2,
            transcendentals=rows * padded,
        ),
        name="experts_back",
    )(base, *grads, *pair, gu, win, wout, *stores)


def on_device(
    states, teacher, valid, routes, norm_in, w_query, w_down_kv, norm_kv, w_up_kv, w_out, norm_ffn,
    w_router, shared_in, shared_out, expert_in, expert_out,
):
    n_blk, n_head = lax.axis_size("blk"), lax.axis_size("head")
    blk, head = lax.axis_index("blk"), lax.axis_index("head")
    own_pos, seqs, width = states.shape
    block_pos = own_pos * n_head
    rows = own_pos * seqs
    block_rows = rows * n_head
    total_rows = block_rows * n_blk
    experts = w_router.shape[1]
    local = expert_in.shape[0]
    eff = expert_in.shape[3]
    shared = shared_in.shape[2] // n_blk
    heads = w_query.shape[1] // (NOPE + ROPE)
    scale = (NOPE + ROPE) ** (-0.5)
    assert block_pos == BLOCK and seqs == 2
    blks, heads_ring = blk_dims(n_blk), head_dims(n_head)

    def gather_head(x):
        return gather_axis(x, heads_ring).reshape((-1,) + x.shape[1:])

    def scatter_head(x):
        return scatter_axis(x.reshape((n_head, -1) + x.shape[1:]), heads_ring)

    def take_own(x):
        own = lax.dynamic_slice_in_dim(x, head * own_pos, own_pos, 0)
        return jnp.moveaxis(own, 1, 0).reshape((rows,) + x.shape[2:])

    part = width // n_blk
    quarter = part // n_head
    lat_width = RANK + ROPE
    small = jnp.concatenate(
        [norm_in, norm_ffn, w_router.reshape(-1), norm_kv, jnp.sum(valid, axis=1).astype(BF16)]
    )
    lines = -(-small.shape[0] // lat_width // 16) * 16
    small = jnp.pad(small, (0, lines * lat_width - small.shape[0])).reshape(lines, lat_width)
    down = lax.dynamic_slice_in_dim(w_down_kv, head * quarter, quarter, 0)
    down = gather_axis(jnp.concatenate([down, small], axis=0), blks)
    small = down[:, quarter:].reshape(n_blk, -1)
    down = jnp.moveaxis(gather_axis(down[:, :quarter], heads_ring), 0, 1).reshape(width, lat_width)
    lanes = heads * ROPE // 2
    wq = w_query.reshape(part, heads, NOPE + ROPE)
    wq = jnp.concatenate(
        [
            wq[:, :, :NOPE].reshape(part, -1),
            wq[:, :, NOPE : NOPE + ROPE // 2].reshape(part, -1),
            wq[:, :, NOPE + ROPE // 2 :].reshape(part, -1),
        ],
        axis=1,
    )
    most = part * 3 // 4
    wq_most = gather_dims(wq[None, :most], blks[:1])
    wq_rest = gather_dims(wq[None, most:], blks[:0:-1])
    states_blk = gather_head(jnp.moveaxis(states, 1, 0).reshape(rows, width))
    down, wq_most, wq_rest = lax.optimization_barrier((down, wq_most, wq_rest))
    wq_most = in_order(gather_dims(wq_most, blks[1:]), blks)
    wq_rest = in_order(gather_dims(wq_rest, blks[:1]), blks[::-1])
    wq = jnp.concatenate([wq_most, wq_rest], axis=1).reshape(width, -1)
    gain_in = small[:, :part].reshape(-1).astype(F32)
    gain_ffn = small[:, part : 2 * part].reshape(-1).astype(F32)
    at = 2 * part
    router = small[:, at : at + part * experts].reshape(width, experts)
    at += part * experts
    gain_kv = small[:, at : at + RANK // n_blk].reshape(-1).astype(F32)
    at += RANK // n_blk
    count = jnp.sum(small[:, at : at + block_pos].astype(F32))
    wup = lax.all_gather(w_up_kv, "blk", axis=0, tiled=True)

    pieces = jnp.concatenate(
        [
            jnp.transpose(shared_in.reshape(part, 2, n_blk, shared), (2, 1, 3, 0)).reshape(
                n_blk, 2 * shared, part
            ),
            shared_out.reshape(n_blk, shared, part),
        ],
        axis=1,
    )
    units = -(-eff // 128) * 128
    shared_units = -(-shared // 128) * 128
    padded = local * units + shared_units
    tall = lambda x, size: jnp.pad(x, ((0, size - x.shape[0]), (0, 0)))

    def expert_weights(values):
        expert_in, expert_out, pieces = values
        mine = jnp.transpose(pieces, (1, 0, 2)).reshape(3, shared, width)
        rows_in = jnp.transpose(expert_in, (0, 2, 3, 1))
        win = [
            block
            for side in range(2)
            for block in [tall(rows_in[e, side], units) for e in range(local)]
            + [tall(mine[side], shared_units)]
        ]
        wout = [tall(expert_out[e], units) for e in range(local)] + [tall(mine[2], shared_units)]
        return jnp.concatenate(win, axis=0), jnp.concatenate(wout, axis=0)

    x_own = jnp.moveaxis(states, 1, 0).reshape(rows, width).astype(F32)
    h1_f, rstd_in = normed(x_own, gain_in)
    h1_own = h1_f.astype(BF16)
    h1_blk = normed(states_blk.astype(F32), gain_in)[0].astype(BF16)
    pos_own = blk * block_pos + head * own_pos + jnp.arange(own_pos, dtype=jnp.int32)
    table_own = jnp.tile(angles(pos_own), (seqs, 1))
    pos_blk = blk * block_pos + jnp.arange(block_pos, dtype=jnp.int32)
    table_blk = jnp.broadcast_to(
        angles(pos_blk).reshape(n_head, 1, own_pos, ROPE // 2), (n_head, seqs, own_pos, ROPE // 2)
    ).reshape(block_rows, ROPE // 2)
    lat = dot(h1_own, down)
    lat_c = lat[:, :RANK]
    latn_f, rstd_kv = normed(lat_c, gain_kv)
    payload = jnp.concatenate(
        [latn_f, rotate(lat[:, RANK:], table_own), jnp.zeros((rows, 128 - ROPE), F32)], axis=1
    ).astype(BF16)
    z, inner, y, _ = split_dims(n_blk, n_head)
    order = [z[2], y[0][2], n_blk // z[2]]
    payload, pieces = phase((by_rows(payload), pieces))
    pieces = lax.all_to_all(pieces, "blk", split_axis=0, concat_axis=0, tiled=True)
    *lats, wup = gather_two(payload, n_blk, n_head, wup)
    lats, wo = phase((lats, w_out))
    wo = lax.all_gather(wo, "blk", axis=1, tiled=True)
    lats = [
        [x.reshape(tuple(shape) + (own_pos, -1)) for x in pair]
        for pair, shape in zip(lats, ([order[2], order[1], order[0]], [order[1], order[2], order[0]]))
    ]
    key_blocks = jnp.arange(n_blk, dtype=jnp.int32)
    key_at = jnp.concatenate(
        [jnp.full((1,), blk, jnp.int32), relative(inner, key_blocks) + 0 * key_blocks, relative([z], key_blocks)]
    ).astype(jnp.int32)
    query = dot(h1_blk, wq)
    cosine = jnp.tile(jnp.cos(table_blk), (1, heads))
    sine = jnp.tile(jnp.sin(table_blk), (1, heads))
    q_first, q_second = query[:, -2 * lanes : -lanes], query[:, -lanes:]
    turned = (q_first * cosine - q_second * sine, q_second * cosine + q_first * sine)
    step = ROPE // 2
    query = jnp.concatenate(
        [
            block
            for h in range(heads)
            for block in (
                query[:, h * NOPE : (h + 1) * NOPE],
                *(half[:, h * step : (h + 1) * step] for half in turned),
                jnp.zeros((block_rows, HEAD - NOPE - ROPE), F32),
            )
        ],
        axis=1,
    ).astype(BF16)
    shape4 = (n_head, seqs, own_pos, -1)
    query = query.reshape(shape4)
    seq_axes = list(zip(range(seqs), lats, (1, 0)))
    att_seqs, lses = zip(*(attention(key_at, s, query, pair, wup, axis, heads) for s, pair, axis in seq_axes))
    att_rows = jnp.concatenate(att_seqs, axis=1).reshape(block_rows, heads * VALUE)
    y_own = x_own + scatter_head(dot(att_rows, wo).astype(BF16)).astype(F32)
    h2_f, rstd_ffn = normed(y_own, gain_ffn)
    h2_own = h2_f.astype(BF16)

    routes_own = take_own(routes)
    mask = jnp.any(routes_own[:, :, None] == jnp.arange(experts, dtype=jnp.int32), axis=1)
    logits = jnp.where(mask, dot(h2_own, router), -1e30)
    gates = jnp.where(mask, jnp.exp(logits - jnp.max(logits, axis=1, keepdims=True)), 0.0)
    gates = gates / jnp.sum(gates, axis=1, keepdims=True)
    assert experts <= 128
    tail = jnp.zeros((rows, 128 - experts), BF16)
    base = jnp.full((1,), blk * local, jnp.int32)
    x_ext = jnp.concatenate([h2_own, gates.astype(BF16), tail], axis=1)
    rounds = max(1, total_rows // 4096)

    def in_turn(run, parts, count):
        outs, sums, stores, start = [], [], (), 0
        total = sum(2 * part[0][0].shape[0] for part in parts)
        for i, part in enumerate(parts):
            if i == 2:
                sums[0], part = phase((sums[0], part))
            outs.append(run(*part, total, start, stores))
            stores = outs[-1][:count]
            start += 2 * part[0][0].shape[0]
            sums.append(sum_cores(outs[-1][-2:], n_blk, n_head))
        return outs, sums

    def forward(x_rows, weights=None):
        if weights is None:
            pairs, (win, wout) = gather_parts(
                x_rows, n_blk, n_head, expert_weights, (expert_in, expert_out, pieces)
            )
        else:
            pairs, (win, wout) = gather_parts(x_rows, n_blk, n_head)[0], weights
        outs, sums = in_turn(
            lambda pair, *rest: run_experts(base, pair, win, wout, units, local, *rest),
            [(pair,) for pair in pairs],
            1,
        )
        kept = [(pair, out[1]) for pair, out in zip(pairs, outs)], outs[-1][0]
        return kept, (win, wout), scatter_parts(sums, n_blk, n_head)[0]

    def products(values):
        return tuple(dot_tn(values[i], values[i + 1]) for i in range(0, len(values), 2))

    def backward(grad_rows, kept, weights):
        win, wout = weights
        parts, x_all = kept
        outs, sums = in_turn(
            lambda grads, pair, gu, *rest: run_experts_back(
                base, grads, pair, gu, win, wout, units, local, *rest
            ),
            [
                (grads, pair, gu)
                for grads, (pair, gu) in zip(gather_parts(grad_rows, n_blk, n_head)[0], parts)
            ],
            3,
        )
        hid_all, act_all, grad_all = outs[-1][:3]
        back, ((d_win,), (d_wout,)) = scatter_parts(
            sums, n_blk, n_head, (products, products), ((hid_all, x_all), (act_all, grad_all))
        )
        return back, d_win, d_wout

    def in_rounds(x):
        return x.reshape((rounds, -1) + x.shape[1:])

    if rounds == 1:
        kept, weights, mixed = forward(x_ext)
    else:
        weights = expert_weights((expert_in, expert_out, pieces))
        mixed = lax.map(lambda x: forward(x, weights)[2], in_rounds(x_ext)).reshape(rows, width)
    mixed = mixed.astype(F32)
    out_own = (y_own + mixed).astype(BF16)
    diff = out_own.astype(F32) - take_own(teacher).astype(F32)
    valid_own = take_own(valid).astype(F32)[:, None]
    loss_part = jnp.sum(valid_own * diff * diff)
    grad_own = diff * valid_own * (total_rows / count)

    grad_own_b = grad_own.astype(BF16)
    if rounds == 1:
        back, d_win, d_wout = backward(grad_own_b, kept, weights)
    else:

        def round_back(sums, both):
            kept, _, _ = forward(both[0], weights)
            back, d_win, d_wout = backward(both[1], kept, weights)
            return (sums[0] + d_win, sums[1] + d_wout), back

        start = (jnp.zeros((2 * padded, width), F32), jnp.zeros((padded, width), F32))
        (d_win, d_wout), back = lax.scan(round_back, start, (in_rounds(x_ext), in_rounds(grad_own_b)))
        back = back.reshape(rows, -1)
    d_sh = jnp.concatenate(
        [d_win[s * padded + local * units :][:shared] for s in range(2)]
        + [d_wout[local * units :][:shared]],
        axis=0,
    )
    d_sh = phase(d_sh).astype(BF16)
    d_sh = jnp.transpose(d_sh.reshape(3 * shared, n_blk, part), (1, 0, 2))
    back, d_win, d_wout, d_sh = lax.optimization_barrier((back, d_win, d_wout, d_sh))
    back = back.astype(F32)

    d_gates = back[:, width : width + experts]
    d_logits = gates * (d_gates - jnp.sum(gates * d_gates, axis=1, keepdims=True))
    d_logits = d_logits.astype(BF16)
    grad_router = dot_tn(h2_own, d_logits)
    dh2 = back[:, :width] + dot_nt(d_logits, router)
    dy_branch, grad_gain_ffn = norm_back(dh2, y_own, rstd_ffn, gain_ffn)
    dy_own = grad_own + dy_branch

    dy_blk = gather_head(dy_own.astype(BF16))
    grad_wo = dot_tn(att_rows, dy_blk).astype(BF16)
    d_att = dot_nt(dy_blk, wo).astype(BF16).reshape(shape4)
    grad_wo, d_att = phase((grad_wo, d_att))
    wo_steps = scatter_columns(grad_wo, n_blk)
    dqs, d_lats, d_ups = [], [], []
    for (s, pair, axis), att, lse in zip(seq_axes, att_seqs, lses):
        dq, first, second, d_up = attention_back(
            key_at, s, query, pair, wup, att, d_att, lse, axis, heads
        )
        if s == 0:
            grad_wo, d_att = phase((next(wo_steps), d_att))
        dqs.append(dq)
        d_lats.append([x.reshape(total_rows // 4, -1) for x in (first, second)])
        d_ups.append(d_up)
    for grad_wo in wo_steps:
        pass
    grad_wo = grad_wo.astype(F32)
    dq = jnp.concatenate(dqs, axis=1)
    d_up = sum(d_ups).astype(BF16)
    dq = dq.reshape(block_rows, heads, HEAD)
    first, second = (
        dq[:, :, at : at + step].reshape(block_rows, lanes).astype(F32) for at in (NOPE, NOPE + step)
    )
    dq = jnp.concatenate(
        [
            dq[:, :, :NOPE].reshape(block_rows, heads * NOPE),
            (first * cosine + second * sine).astype(BF16),
            (second * cosine - first * sine).astype(BF16),
        ],
        axis=1,
    )
    dh1 = scatter_head(dot_nt(dq, wq).astype(BF16)).astype(F32)
    up_rows = w_up_kv.shape[0]
    wide = up_rows * w_up_kv.shape[1] // part
    grad_wq = by_rows(dot_tn(h1_blk, dq).astype(BF16)).reshape(n_blk, part, -1)
    d_up = jnp.moveaxis(d_up.reshape(n_blk, up_rows, -1, wide), 2, 1).reshape(n_blk, part, wide)
    joined = jnp.concatenate([grad_wq, d_up], axis=2)
    joined, d_win, d_wout, d_sh = phase((by_rows(joined), d_win, d_wout, d_sh))
    d_lat, (d_win, d_wout, d_sh) = scatter_two(*d_lats, n_blk, n_head, (d_win, d_wout, d_sh))
    d_lat = by_rows(d_lat)[:, : RANK + ROPE].astype(F32)
    joined = by_rows(lax.psum_scatter(joined, "blk", scatter_dimension=0, tiled=False)).astype(F32)
    grad_wq = joined[:, :-wide]
    grad_up = jnp.moveaxis(joined[:, -wide:].reshape(-1, up_rows, wide), 0, 1).reshape(up_rows, -1)
    grad_ein = jnp.concatenate(
        [d_win[s * padded + e * units :][:eff] for e in range(local) for s in range(2)], axis=0
    )
    grad_ein = jnp.transpose(grad_ein.reshape(local, 2, eff, width), (0, 3, 1, 2))
    grad_eout = jnp.concatenate([d_wout[e * units :][:eff] for e in range(local)], axis=0)
    grad_eout = grad_eout.reshape(local, eff, width)
    d_sh = lax.all_to_all(d_sh, "blk", split_axis=0, concat_axis=0, tiled=True).astype(F32)
    grad_shin = jnp.transpose(d_sh[:, : 2 * shared].reshape(n_blk, 2, shared, part), (3, 1, 0, 2)).reshape(
        part, 2, n_blk * shared
    )
    grad_shout = d_sh[:, 2 * shared :].reshape(n_blk * shared, part)
    grad_wq = jnp.concatenate(
        [
            grad_wq[:, : heads * NOPE].reshape(part, heads, NOPE),
            grad_wq[:, heads * NOPE : -lanes].reshape(part, heads, ROPE // 2),
            grad_wq[:, -lanes:].reshape(part, heads, ROPE // 2),
        ],
        axis=2,
    ).reshape(part, -1)
    d_lat_c, grad_gain_kv = norm_back(d_lat[:, :RANK], lat_c, rstd_kv, gain_kv)
    d_lat_b = jnp.concatenate([d_lat_c, rotate(d_lat[:, RANK : RANK + ROPE], -table_own)], axis=1).astype(BF16)
    d_lat_b = by_rows(d_lat_b)
    d_lat_blk = gather_head(d_lat_b)
    grad_down = by_rows(dot_tn(h1_blk, d_lat_blk).astype(BF16)).reshape(n_blk, n_head, quarter, -1)
    grad_down = lax.dynamic_index_in_dim(grad_down, head, 1, keepdims=False)
    grad_down = gather_head(by_rows(scatter_axis(grad_down, blks))).astype(F32)
    dh1 = dh1 + dot_nt(d_lat_b, down)
    dx_branch, grad_gain_in = norm_back(dh1, x_own, rstd_in, gain_in)
    dx_own = dy_own + dx_branch

    loss_high = loss_part.astype(BF16).astype(F32)
    sums = jnp.concatenate(
        [
            grad_gain_in.reshape(n_blk, -1),
            grad_gain_ffn.reshape(n_blk, -1),
            grad_router.reshape(n_blk, -1),
            grad_gain_kv.reshape(n_blk, -1),
            jnp.full((n_blk, 1), loss_high),
            jnp.full((n_blk, 1), loss_part - loss_high),
        ],
        axis=1,
    )
    sums = scatter_axis(sums, blks)
    for dim in heads_ring:
        sums = sum(ring_gather(sums, dim))
    out_gain_in = sums[:part]
    out_gain_ffn = sums[part : 2 * part]
    at = 2 * part
    out_router = sums[at : at + part * experts].reshape(part, experts)
    at += part * experts
    out_gain_kv = sums[at : at + RANK // n_blk]
    loss = (sums[-2] + sums[-1]) / (width * count)

    def give(x):
        return jnp.moveaxis(x.reshape(seqs, own_pos, width), 0, 1)

    return (
        give(out_own), loss, give(dx_own), out_gain_in, grad_wq, grad_down, out_gain_kv, grad_up,
        grad_wo, out_gain_ffn, out_router, grad_shin, grad_shout, grad_ein, grad_eout,
    )


def solution(mesh):
    in_specs = (
        P(BOTH, None, None), P("blk", None, None), P("blk", None), P("blk", None, None), P("blk"),
        P("blk", "head"), P("blk", None), P("blk"), P("blk", "head"), P("head", "blk"), P("blk"),
        P("blk", None), P("blk", None, "head"), P("head", "blk"), P("blk", None, None, "head"),
        P("blk", "head", None),
    )
    out_specs = (
        P(BOTH, None, None), P(), P(BOTH, None, None), P("blk"), P("blk", "head"), P("blk", None),
        P("blk"), P("blk", "head"), P("head", "blk"), P("blk"), P("blk", None), P("blk", None, "head"),
        P("head", "blk"), P("blk", None, None, "head"), P("blk", "head", None),
    )
    return jax.shard_map(on_device, mesh=mesh, in_specs=in_specs, out_specs=out_specs, check_vma=False)
```

```python
import functools

import jax
import jax.numpy as jnp
from jax import lax
from jax.experimental import pallas as pl
from jax.experimental.layout import Layout, with_layout_constraint
from jax.experimental.pallas import tpu as pltpu
from jax.sharding import PartitionSpec as P

NOPE = 128
ROPE = 64
VALUE = 128
RANK = 512
BLOCK = 256
EPS = 1e-06
F32 = jnp.float32
BF16 = jnp.bfloat16
BOTH = ("blk", "head")


def angles(position):
    frequency = 10000.0 ** (-2.0 * jnp.arange(ROPE // 2, dtype=F32) / ROPE)
    return position.astype(F32)[:, None] * frequency[None, :]


def rotate(values, table):
    half = ROPE // 2
    cosine, sine = jnp.cos(table), jnp.sin(table)
    first, second = values[:, :half], values[:, half:]
    return jnp.concatenate([first * cosine - second * sine, second * cosine + first * sine], axis=1)


def normed(values, gain):
    rstd = lax.rsqrt(jnp.mean(values * values, axis=-1, keepdims=True) + EPS)
    return values * rstd * gain, rstd


def norm_back(grad, values, rstd, gain):
    scaled = grad * gain
    out = rstd * scaled - values * rstd**3 * jnp.mean(scaled * values, axis=-1, keepdims=True)
    return out, jnp.sum(grad * values * rstd, axis=0)


def by_rows(x):
    return with_layout_constraint(x, Layout(tuple(range(x.ndim))))


def dot(a, b):
    return jnp.dot(a, b, preferred_element_type=F32)


def dot_nt(a, b):
    return lax.dot_general(a, b, (((1,), (1,)), ((), ())), preferred_element_type=F32)


def dot_tn(a, b):
    return lax.dot_general(a, b, (((0,), (0,)), ((), ())), preferred_element_type=F32)


def blk_dims(n_blk):
    if n_blk == 8:
        return [("blk", 2, 4), ("blk", 1, 2)]
    if n_blk == 32:
        return [("blk", 8, 4), ("blk", 2, 4), ("blk", 1, 2)]
    return [("blk", 1, n_blk)]


def head_dims(n_head):
    return [("head", 2, n_head // 2), ("head", 1, 2)] if n_head % 2 == 0 else [("head", 1, n_head)]


def shift(x, dim, by):
    axis, stride, size = dim
    pairs = []
    for i in range(lax.axis_size(axis)):
        digit = i // stride % size
        pairs.append((i, i + ((digit + by) % size - digit) * stride))
    return lax.ppermute(x, axis, pairs)


def digit_of(dim):
    axis, stride, size = dim
    return lax.axis_index(axis) // stride % size


def ring_gather(x, dim):
    pieces = [x]
    for _ in range(dim[2] - 1):
        pieces.append(shift(pieces[-1], dim, -1))
    return pieces


def ring_scatter(pieces, dim):
    total = pieces[-1]
    for piece in pieces[-2::-1]:
        total = shift(total, dim, 1) + piece
    return total


def direct_gather(x, dim):
    return [x] + [shift(x, dim, -k) for k in range(1, dim[2])]


def direct_scatter(pieces, dim):
    total = pieces[0].astype(F32)
    for k in range(1, dim[2]):
        total = total + shift(pieces[k], dim, k).astype(F32)
    return total.astype(pieces[0].dtype)


def gather_dims(x, dims, step=ring_gather):
    for dim in dims:
        x = jnp.concatenate(step(x, dim), axis=0)
    return x


def scatter_dims(x, dims, step=ring_scatter):
    for dim in reversed(dims):
        x = step(jnp.split(x, dim[2], axis=0), dim)
    return x


def relative(dims, index):
    place, scale = 0, 1
    for dim in dims:
        place = place + (index // dim[1] % dim[2] - digit_of(dim)) % dim[2] * scale
        scale *= dim[2]
    return place


def absolute(dims, place):
    index = 0
    for dim in dims:
        index = index + (place % dim[2] + digit_of(dim)) % dim[2] * dim[1]
        place //= dim[2]
    return index


def gather_axis(x, dims):
    return in_order(gather_dims(x[None], dims, direct_gather), dims)


def in_order(stack, dims):
    n = stack.shape[0]
    return jnp.concatenate(
        [lax.dynamic_slice_in_dim(stack, relative(dims, i), 1, 0) for i in range(n)], axis=0
    )


def scatter_axis(x, dims):
    n = lax.axis_size(dims[0][0])
    stack = jnp.concatenate(
        [lax.dynamic_slice_in_dim(x, absolute(dims, i), 1, 0) for i in range(n)], axis=0
    )
    return scatter_dims(stack, dims, direct_scatter)[0]


def split_dims(n_blk, n_head):
    blk, head = blk_dims(n_blk), head_dims(n_head)
    return blk[0], blk[1:], head[:-1], head[-1]


phase = lax.optimization_barrier


def no_fill(values):
    return values


def gather_parts(x, n_blk, n_head, fill=no_fill, fill_in=()):
    third = x.shape[0] * 5 // 16
    first = x.shape[0] - 2 * third
    z, inner, y, core = split_dims(n_blk, n_head)
    a, pieces = x[:first], [x[first:]]
    for dims in [inner, y] + [[]] * (z[2] - 4):
        piece, a = phase((shift(pieces[-1], z, -1), gather_dims(a, dims)))
        pieces.append(piece)
    pieces.append(shift(pieces[-1], z, -1))
    b = jnp.concatenate([p[:third] for p in pieces], axis=0)
    c = jnp.concatenate([p[third:] for p in pieces], axis=0)
    b, c, a = phase((b, c, a))
    b, c, last, fill_in = phase((gather_dims(b, y), gather_dims(c, inner), shift(a, z, -1), fill_in))
    pieces = [a, last]
    for _ in range(z[2] - 2):
        pieces.append(shift(pieces[-1], z, -1))
    b, c, pieces, filled = phase((gather_dims(b, inner), gather_dims(c, y), pieces, fill(fill_in)))
    return [ring_gather(part, core) for part in (b, c, jnp.concatenate(pieces, axis=0))], filled


def scatter_parts(sums, n_blk, n_head, fills=(no_fill,) * 2, fill_ins=((),) * 2):
    z, inner, y, _ = split_dims(n_blk, n_head)
    b, c, a, filled = phase((*sums, fill_ins[0]))
    pieces = jnp.split(a, z[2], axis=0)

    def advance(total, steps):
        for _ in range(steps):
            total = shift(total, z, 1) + pieces.pop()
        return total

    each = 1 if fill_ins[0] else z[2] - 2
    b, c, a, filled, fill_in = phase(
        (scatter_dims(b, inner), scatter_dims(c, y), advance(pieces.pop(), each), fills[0](filled), fill_ins[1])
    )
    outs = [filled]
    b, c, a, filled = phase((scatter_dims(b, y), scatter_dims(c, inner), advance(a, 1), fills[1](fill_in)))
    outs.append(filled)
    both = [
        jnp.concatenate(rows, axis=0)
        for rows in zip(jnp.split(b, z[2], axis=0), jnp.split(c, z[2], axis=0))
    ]
    total = both.pop()
    a = advance(a, len(pieces))
    for dims in [y, inner] + [[]] * (z[2] - 3):
        total, a = phase((shift(total, z, 1) + both.pop(), scatter_dims(a, dims)))
    return jnp.concatenate([a, total], axis=0), outs


def scatter_columns(x, n_blk):
    c = x.shape[1] // n_blk
    for dim in reversed(blk_dims(n_blk)):
        size = dim[2]
        pieces = []
        for k in range(size):
            place = (digit_of(dim) + k) % size
            pieces.append(
                jnp.concatenate(
                    [
                        lax.dynamic_slice_in_dim(x, (outer * size + place) * c, c, 1)
                        for outer in range(x.shape[1] // c // size)
                    ],
                    axis=1,
                )
            )
        x = direct_scatter(pieces, dim)
        yield x


def sum_cores(pair, n_blk, n_head):
    return ring_scatter(pair, split_dims(n_blk, n_head)[3])


def gather_two(x, n_blk, n_head, beside):
    half = x.shape[0] // 2
    z, inner, y, core = split_dims(n_blk, n_head)
    pieces = direct_gather(x, z)
    b = jnp.concatenate([p[:half] for p in pieces], axis=0)
    c = jnp.concatenate([p[half:] for p in pieces], axis=0)
    b, c = phase((gather_dims(b, y), gather_dims(c, inner)))
    b, c, beside = phase((gather_dims(b, inner), gather_dims(c, y), beside))
    return direct_gather(b, core), direct_gather(c, core), beside


def scatter_two(b, c, n_blk, n_head, beside):
    z, inner, y, core = split_dims(n_blk, n_head)
    b, c, beside = phase((direct_scatter(b, core), direct_scatter(c, core), beside))
    b = scatter_dims(b, y + inner)
    c = scatter_dims(c, inner + y)
    pieces = [
        jnp.concatenate(both, axis=0)
        for both in zip(jnp.split(b, z[2], axis=0), jnp.split(c, z[2], axis=0))
    ]
    return direct_scatter(pieces, z), beside


def scatter_blk(x, axis=0):
    return lax.psum_scatter(x, "blk", scatter_dimension=axis, tiled=True)


HEAD = 256


def attention_kernel(
    heads, scale, at_ref, q_ref, lata_ref, latb_ref, up_ref, out_ref, lse_ref, m_ref, acc_ref
):
    step = pl.program_id(0)

    @pl.when(step == 0)
    def _():
        m_ref[...] = jnp.full_like(m_ref, -1e30)
        acc_ref[...] = jnp.zeros_like(acc_ref)

    @pl.when(step <= at_ref[0])
    def _():
        lat = both_cores(lata_ref, latb_ref)
        kv = dot(lat[:, :RANK], up_ref[...]).astype(BF16)
        query = q_ref[...].reshape(BLOCK, heads * HEAD)
        ones = jnp.ones((BLOCK, HEAD - VALUE), BF16)
        for h in range(heads):
            at = h * (NOPE + VALUE)
            keys = jnp.concatenate([kv[:, at : at + NOPE], lat[:, RANK:]], axis=1)
            values = jnp.concatenate([kv[:, at + NOPE : at + NOPE + VALUE], ones], axis=1)
            scores = dot_nt(query[:, h * HEAD : (h + 1) * HEAD], keys) * scale
            old = m_ref[h][:, :1]
            new = jnp.maximum(old, jnp.max(scores, axis=1, keepdims=True))
            expo = jnp.exp(scores - new)
            acc_ref[h] = acc_ref[h] * jnp.exp(old - new) + dot(expo.astype(BF16), values)
            m_ref[h] = jnp.broadcast_to(new, m_ref.shape[1:])

    @pl.when(step == pl.num_programs(0) - 1)
    def _():
        lane = lax.broadcasted_iota(jnp.int32, (BLOCK, 128), 1)
        lse = jnp.zeros((BLOCK, 128), F32)
        for h in range(heads):
            total = acc_ref[h][:, VALUE:]
            out = acc_ref[h][:, :VALUE] / total
            out_ref[:, :, :, h * VALUE : (h + 1) * VALUE] = out.astype(BF16).reshape(
                out_ref.shape[:3] + (VALUE,)
            )
            lse = jnp.where(lane == h, m_ref[h] + jnp.log(total), lse)
        lse_ref[...] = lse


def both_cores(first_ref, second_ref):
    flat = [ref[...].reshape(BLOCK // 2, ref.shape[-1]) for ref in (first_ref, second_ref)]
    return jnp.concatenate(flat, axis=0)


def key_specs(view, y_axis, clamp):
    n_blk = view[0] * view[1] * view[2] // view[y_axis]
    shape = tuple(n if i == y_axis else 1 if i < 3 else n for i, n in enumerate(view))

    def index(step, at):
        step = jnp.minimum(step, at[0]) if clamp else step
        inner, z = at[1 + step], at[1 + n_blk + step]
        return (0, inner, z, 0, 0) if y_axis == 0 else (inner, 0, z, 0, 0)

    return [pl.BlockSpec(shape, index)] * 2


def attention(at, seq, query, lats, up, y_axis, heads):
    n_head, own = query.shape[0], query.shape[2]
    n_blk = (at.shape[0] - 1) // 2
    scale = (NOPE + ROPE) ** -0.5
    row = lambda width, s: pl.BlockSpec((n_head, 1, own, width), lambda b, r: (0, s, 0, 0))
    return pl.pallas_call(
        functools.partial(attention_kernel, heads, scale),
        grid_spec=pltpu.PrefetchScalarGridSpec(
            num_scalar_prefetch=1,
            grid=(n_blk,),
            in_specs=[row(query.shape[3], seq)]
            + key_specs(lats[0].shape, y_axis, True)
            + [pl.BlockSpec(up.shape, lambda b, r: (0, 0))],
            out_specs=[row(heads * VALUE, 0), pl.BlockSpec((BLOCK, 128), lambda b, r: (0, 0))],
            scratch_shapes=[
                pltpu.VMEM((heads, BLOCK, 128), F32),
                pltpu.VMEM((heads, BLOCK, HEAD), F32),
            ],
        ),
        out_shape=[
            jax.ShapeDtypeStruct((n_head, 1, own, heads * VALUE), BF16),
            jax.ShapeDtypeStruct((BLOCK, 128), F32),
        ],
        cost_estimate=pl.CostEstimate(
            flops=n_blk * BLOCK * 2 * (RANK * up.shape[1] + heads * BLOCK * 640),
            bytes_accessed=lats[0].size * 4 + up.size * 2 + query.size * 2,
            transcendentals=n_blk * heads * BLOCK * BLOCK,
        ),
        name="attention",
    )(at, query, *lats, up)


def attention_back_kernel(
    heads, scale, at_ref, q_ref, lata_ref, latb_ref, up_ref, att_ref, datt_ref, lse_ref,
    dq_ref, dlata_ref, dlatb_ref, dup_ref, delta_ref, dq_acc, up_acc,
):
    step = pl.program_id(0)
    last = pl.num_programs(0) - 1

    @pl.when(step == 0)
    def _():
        up_acc[...] = jnp.zeros_like(up_acc)

    @pl.when(step == 0)
    def _():
        dq_acc[...] = jnp.zeros_like(dq_acc)
        prod = att_ref[...].astype(F32) * datt_ref[...].astype(F32)
        prod = prod.reshape(BLOCK, heads * VALUE)
        for h in range(heads):
            delta_ref[h] = jnp.broadcast_to(
                jnp.sum(prod[:, h * VALUE : (h + 1) * VALUE], axis=1, keepdims=True), (BLOCK, 128)
            )

    @pl.when(step <= at_ref[0])
    def _():
        lat = both_cores(lata_ref, latb_ref)
        latn = lat[:, :RANK]
        kv = dot(latn, up_ref[...]).astype(BF16)
        query = q_ref[...].reshape(BLOCK, heads * HEAD)
        d_att = datt_ref[...].reshape(BLOCK, heads * VALUE)
        d_key = jnp.zeros((BLOCK, HEAD - NOPE), F32)
        d_kv = []
        for h in range(heads):
            at = h * (NOPE + VALUE)
            q_h = query[:, h * HEAD : (h + 1) * HEAD]
            d_h = d_att[:, h * VALUE : (h + 1) * VALUE]
            keys = jnp.concatenate([kv[:, at : at + NOPE], lat[:, RANK:]], axis=1)
            prob = jnp.exp(dot_nt(q_h, keys) * scale - lse_ref[:, h : h + 1])
            d_prob = dot_nt(d_h, kv[:, at + NOPE : at + NOPE + VALUE])
            d_score = (prob * (d_prob - delta_ref[h][:, :1]) * scale).astype(BF16)
            dq_acc[h] = dq_acc[h] + dot(d_score, keys)
            d_both = dot_tn(d_score, q_h)
            d_kv.append(d_both[:, :NOPE])
            d_kv.append(dot_tn(prob.astype(BF16), d_h))
            d_key = d_key + d_both[:, NOPE:]
        d_kv = jnp.concatenate(d_kv, axis=1).astype(BF16)
        up_acc[...] += dot_tn(latn, d_kv)
        d_lat = dot_nt(d_kv, up_ref[...]).astype(BF16)
        d_key = d_key.astype(BF16)
        for i, ref in enumerate((dlata_ref, dlatb_ref)):
            here = slice(i * (BLOCK // 2), (i + 1) * (BLOCK // 2))
            shape = ref.shape[:4]
            ref[:, :, :, :, :RANK] = d_lat[here].reshape(shape + (RANK,))
            ref[:, :, :, :, RANK:] = d_key[here].reshape(shape + (-1,))

    @pl.when(step > at_ref[0])
    def _():
        dlata_ref[...] = jnp.zeros_like(dlata_ref)
        dlatb_ref[...] = jnp.zeros_like(dlatb_ref)

    @pl.when(step == last)
    def _():
        for h in range(heads):
            dq_ref[:, :, :, h * HEAD : (h + 1) * HEAD] = (
                dq_acc[h].astype(BF16).reshape(dq_ref.shape[:3] + (HEAD,))
            )

    @pl.when(step == last)
    def _():
        dup_ref[...] = up_acc[...]


def attention_back(at, seq, query, lats, up, att, d_att, lse, y_axis, heads):
    n_head, own = query.shape[0], query.shape[2]
    n_blk = (at.shape[0] - 1) // 2
    scale = (NOPE + ROPE) ** -0.5
    row = lambda width, s: pl.BlockSpec((n_head, 1, own, width), lambda b, r: (0, s, 0, 0))
    whole = lambda x: pl.BlockSpec(x.shape, lambda b, r: (0, 0))
    return pl.pallas_call(
        functools.partial(attention_back_kernel, heads, scale),
        grid_spec=pltpu.PrefetchScalarGridSpec(
            num_scalar_prefetch=1,
            grid=(n_blk,),
            in_specs=[row(query.shape[3], seq)]
            + key_specs(lats[0].shape, y_axis, True)
            + [whole(up), row(heads * VALUE, 0), row(heads * VALUE, seq)]
            + [whole(lse)],
            out_specs=[row(query.shape[3], 0)] + key_specs(lats[0].shape, y_axis, False) + [whole(up)],
            scratch_shapes=[
                pltpu.VMEM((heads, BLOCK, 128), F32),
                pltpu.VMEM((heads, BLOCK, HEAD), F32),
                pltpu.VMEM(up.shape, F32),
            ],
        ),
        out_shape=[
            jax.ShapeDtypeStruct((n_head, 1, own, query.shape[3]), BF16),
            jax.ShapeDtypeStruct(lats[0].shape, BF16),
            jax.ShapeDtypeStruct(lats[0].shape, BF16),
            jax.ShapeDtypeStruct(up.shape, F32),
        ],
        cost_estimate=pl.CostEstimate(
            flops=n_blk * BLOCK * 2 * (3 * RANK * up.shape[1] + heads * BLOCK * 1700),
            bytes_accessed=lats[0].size * 8 + up.size * 6 + query.size * 4,
            transcendentals=n_blk * heads * BLOCK * BLOCK,
        ),
        name="attention_back",
    )(at, query, *lats, up, att, d_att, lse)


def pick(own, first_ref, second_ref, out_ref):
    @pl.when(own)
    def _():
        out_ref[...] = first_ref[...]

    @pl.when(jnp.logical_not(own))
    def _():
        out_ref[...] = second_ref[...]


def put(own, value_ref, first_ref, second_ref):
    @pl.when(own)
    def _():
        first_ref[...] = value_ref[...]

    @pl.when(jnp.logical_not(own))
    def _():
        second_ref[...] = value_ref[...]


def gate_lanes(tail, base, local):
    lane = lax.broadcasted_iota(jnp.int32, tail.shape, 1)
    tail = tail.astype(F32)
    return [
        jnp.sum(jnp.where(lane == base + e, tail, 0.0), axis=1, keepdims=True) for e in range(local)
    ]


def spans(size, step):
    return [(at, min(step, size - at)) for at in range(0, size, step)]


def experts_kernel(
    units, local, base_ref, xa_ref, xb_ref, ta_ref, tb_ref, win_ref, wout_ref,
    *refs,
):
    x_ref, gu_ref, outa_ref, outb_ref, tail_ref, act_ref, sum_ref = refs[-7:]
    own = pl.program_id(0) < pl.num_programs(0) // 2
    pick(own, xa_ref, xb_ref, x_ref)
    pick(own, ta_ref, tb_ref, tail_ref)
    gates = gate_lanes(tail_ref[...], base_ref[0], local)
    padded = wout_ref.shape[0]
    for at, size in spans(padded, 256):
        gate = dot_nt(x_ref[...], win_ref[at : at + size, :])
        up = dot_nt(x_ref[...], win_ref[padded + at : padded + at + size, :])
        gu_ref[:, at : at + size] = gate.astype(BF16)
        gu_ref[:, padded + at : padded + at + size] = up.astype(BF16)
        act = gate * jax.nn.sigmoid(gate) * up
        for here in range(0, size, 128):
            expert = (at + here) // units
            part = act[:, here : here + 128]
            part = part * gates[expert] if expert < local else part
            act_ref[:, at + here : at + here + 128] = part.astype(BF16)
    for at, size in spans(wout_ref.shape[1], 512):
        sum_ref[:, at : at + size] = dot(act_ref[...], wout_ref[:, at : at + size]).astype(BF16)
    put(own, sum_ref, outa_ref, outb_ref)


def half_specs(tile, steps, width, column=0):
    half = steps // 2
    return [
        pl.BlockSpec((tile, width), lambda i, r: (jnp.minimum(i, half - 1), column)),
        pl.BlockSpec((tile, width), lambda i, r: (jnp.maximum(i - half, 0), column)),
    ]


def tile_of(half, start):
    return max(t for t in range(16, 385, 16) if half % t == 0 and start % t == 0)


def resident(x):
    return pl.BlockSpec(x.shape, lambda i, r: (0, 0), pipeline_mode=pl.Buffered(1))


def stored(total, sizes, tile, start, stores, first_in):
    at = start // tile
    specs = [pl.BlockSpec((tile, size), lambda i, r: (i + at, 0)) for size in sizes]
    shapes = [jax.ShapeDtypeStruct((total, size), BF16) for size in sizes]
    aliases = {first_in + i: i for i in range(len(stores))}
    return specs, shapes, [pl.BlockSpec(memory_space=pl.ANY) for _ in stores], aliases


def run_experts(base, pair, win, wout, units, local, total, start, stores):
    half, width, padded = pair[0].shape[0], wout.shape[1], wout.shape[0]
    tile = tile_of(half, start)
    steps = 2 * half // tile
    row = lambda size: pl.BlockSpec((tile, size), lambda i, r: (i, 0))
    rows = 2 * half
    shape = lambda count, size: jax.ShapeDtypeStruct((count, size), BF16)
    store_out, store_shapes, store_in, aliases = stored(total, (width,), tile, start, stores, 7)
    return pl.pallas_call(
        functools.partial(experts_kernel, units, local),
        grid_spec=pltpu.PrefetchScalarGridSpec(
            num_scalar_prefetch=1,
            grid=(steps,),
            in_specs=half_specs(tile, steps, width)
            + half_specs(tile, steps, 128, width // 128)
            + [resident(win), resident(wout)]
            + store_in,
            out_specs=store_out + [row(2 * padded)] + half_specs(tile, steps, width),
            scratch_shapes=[
                pltpu.VMEM((tile, 128), BF16),
                pltpu.VMEM((tile, padded), BF16),
                pltpu.VMEM((tile, width), BF16),
            ],
        ),
        out_shape=store_shapes + [shape(rows, 2 * padded), shape(half, width), shape(half, width)],
        input_output_aliases=aliases,
        cost_estimate=pl.CostEstimate(
            flops=rows * width * padded * 6,
            bytes_accessed=(rows * (3 * width + 2 * padded) + 3 * width * padded) * 2,
            transcendentals=rows * padded,
        ),
        name="experts",
    )(base, *pair, *pair, win, wout, *stores)


def experts_back_kernel(
    units, local, base_ref, ga_ref, gb_ref, ta_ref, tb_ref, gu_ref, win_ref, wout_ref,
    *refs,
):
    hid_ref, act_ref, g_ref, outa_ref, outb_ref, tail_ref, sum_ref = refs[-7:]
    own = pl.program_id(0) < pl.num_programs(0) // 2
    pick(own, ga_ref, gb_ref, g_ref)
    pick(own, ta_ref, tb_ref, tail_ref)
    gates = gate_lanes(tail_ref[...], base_ref[0], local)
    padded, width = wout_ref.shape
    prods = [jnp.zeros(tail_ref.shape, F32) for _ in range(local)]
    for at, size in spans(padded, 256):
        d_acts = dot_nt(g_ref[...], wout_ref[at : at + size, :])
        for here in range(0, size, 128):
            unit = at + here
            expert = unit // units
            d_act = d_acts[:, here : here + 128]
            gate = gu_ref[:, unit : unit + 128].astype(F32)
            up = gu_ref[:, padded + unit : padded + unit + 128].astype(F32)
            sig = jax.nn.sigmoid(gate)
            silu = gate * sig
            act = silu * up
            if expert < local:
                prods[expert] = prods[expert] + act * d_act
                d_act = d_act * gates[expert]
                act = act * gates[expert]
            hid_ref[:, unit : unit + 128] = (d_act * up * (sig + silu * (1.0 - sig))).astype(BF16)
            hid_ref[:, padded + unit : padded + unit + 128] = (d_act * silu).astype(BF16)
            act_ref[:, unit : unit + 128] = act.astype(BF16)
    for at, size in spans(width, 512):
        sum_ref[:, at : at + size] = dot(hid_ref[...], win_ref[:, at : at + size]).astype(BF16)
    lane = lax.broadcasted_iota(jnp.int32, tail_ref.shape, 1)
    extra = jnp.zeros(tail_ref.shape, F32)
    for e in range(local):
        extra = jnp.where(lane == base_ref[0] + e, jnp.sum(prods[e], axis=1, keepdims=True), extra)
    sum_ref[:, width:] = extra.astype(BF16)
    put(own, sum_ref, outa_ref, outb_ref)


def run_experts_back(base, grads, pair, gu, win, wout, units, local, total, start, stores):
    half, width, padded = grads[0].shape[0], wout.shape[1], wout.shape[0]
    tile = tile_of(half, start)
    steps = 2 * half // tile
    row = lambda size: pl.BlockSpec((tile, size), lambda i, r: (i, 0))
    rows = 2 * half
    shape = lambda count, size: jax.ShapeDtypeStruct((count, size), BF16)
    store_out, store_shapes, store_in, aliases = stored(
        total, (2 * padded, padded, width), tile, start, stores, 8
    )
    return pl.pallas_call(
        functools.partial(experts_back_kernel, units, local),
        grid_spec=pltpu.PrefetchScalarGridSpec(
            num_scalar_prefetch=1,
            grid=(steps,),
            in_specs=half_specs(tile, steps, width)
            + half_specs(tile, steps, 128, width // 128)
            + [row(2 * padded), resident(win), resident(wout)]
            + store_in,
            out_specs=store_out + half_specs(tile, steps, width + 128),
            scratch_shapes=[pltpu.VMEM((tile, 128), BF16), pltpu.VMEM((tile, width + 128), BF16)],
        ),
        out_shape=store_shapes + [shape(half, width + 128), shape(half, width + 128)],
        input_output_aliases=aliases,
        cost_estimate=pl.CostEstimate(
            flops=rows * width * padded * 6,
            bytes_accessed=(rows * (3 * width + 5 * padded) + 3 * width * padded) * 2,
            transcendentals=rows * padded,
        ),
        name="experts_back",
    )(base, *grads, *pair, gu, win, wout, *stores)


def on_device(
    states, teacher, valid, routes, norm_in, w_query, w_down_kv, norm_kv, w_up_kv, w_out, norm_ffn,
    w_router, shared_in, shared_out, expert_in, expert_out,
):
    n_blk, n_head = lax.axis_size("blk"), lax.axis_size("head")
    blk, head = lax.axis_index("blk"), lax.axis_index("head")
    own_pos, seqs, width = states.shape
    block_pos = own_pos * n_head
    rows = own_pos * seqs
    block_rows = rows * n_head
    total_rows = block_rows * n_blk
    experts = w_router.shape[1]
    local = expert_in.shape[0]
    eff = expert_in.shape[3]
    shared = shared_in.shape[2] // n_blk
    heads = w_query.shape[1] // (NOPE + ROPE)
    scale = (NOPE + ROPE) ** (-0.5)
    assert block_pos == BLOCK and seqs == 2
    blks, heads_ring = blk_dims(n_blk), head_dims(n_head)

    def gather_head(x):
        return gather_axis(x, heads_ring).reshape((-1,) + x.shape[1:])

    def scatter_head(x):
        return scatter_axis(x.reshape((n_head, -1) + x.shape[1:]), heads_ring)

    def take_own(x):
        own = lax.dynamic_slice_in_dim(x, head * own_pos, own_pos, 0)
        return jnp.moveaxis(own, 1, 0).reshape((rows,) + x.shape[2:])

    part = width // n_blk
    quarter = part // n_head
    lat_width = RANK + ROPE
    small = jnp.concatenate(
        [norm_in, norm_ffn, w_router.reshape(-1), norm_kv, jnp.sum(valid, axis=1).astype(BF16)]
    )
    lines = -(-small.shape[0] // lat_width // 16) * 16
    small = jnp.pad(small, (0, lines * lat_width - small.shape[0])).reshape(lines, lat_width)
    down = lax.dynamic_slice_in_dim(w_down_kv, head * quarter, quarter, 0)
    down = gather_axis(jnp.concatenate([down, small], axis=0), blks)
    small = down[:, quarter:].reshape(n_blk, -1)
    down = jnp.moveaxis(gather_axis(down[:, :quarter], heads_ring), 0, 1).reshape(width, lat_width)
    lanes = heads * ROPE // 2
    wq = w_query.reshape(part, heads, NOPE + ROPE)
    wq = jnp.concatenate(
        [
            wq[:, :, :NOPE].reshape(part, -1),
            wq[:, :, NOPE : NOPE + ROPE // 2].reshape(part, -1),
            wq[:, :, NOPE + ROPE // 2 :].reshape(part, -1),
        ],
        axis=1,
    )
    most = part * 3 // 4
    wq_most = gather_dims(wq[None, :most], blks[:1])
    wq_rest = gather_dims(wq[None, most:], blks[:0:-1])
    states_blk = gather_head(jnp.moveaxis(states, 1, 0).reshape(rows, width))
    down, wq_most, wq_rest = lax.optimization_barrier((down, wq_most, wq_rest))
    wq_most = in_order(gather_dims(wq_most, blks[1:]), blks)
    wq_rest = in_order(gather_dims(wq_rest, blks[:1]), blks[::-1])
    wq = jnp.concatenate([wq_most, wq_rest], axis=1).reshape(width, -1)
    gain_in = small[:, :part].reshape(-1).astype(F32)
    gain_ffn = small[:, part : 2 * part].reshape(-1).astype(F32)
    at = 2 * part
    router = small[:, at : at + part * experts].reshape(width, experts)
    at += part * experts
    gain_kv = small[:, at : at + RANK // n_blk].reshape(-1).astype(F32)
    at += RANK // n_blk
    count = jnp.sum(small[:, at : at + block_pos].astype(F32))
    wup = lax.all_gather(w_up_kv, "blk", axis=0, tiled=True)

    pieces = jnp.concatenate(
        [
            jnp.transpose(shared_in.reshape(part, 2, n_blk, shared), (2, 1, 3, 0)).reshape(
                n_blk, 2 * shared, part
            ),
            shared_out.reshape(n_blk, shared, part),
        ],
        axis=1,
    )
    units = -(-eff // 128) * 128
    shared_units = -(-shared // 128) * 128
    padded = local * units + shared_units
    tall = lambda x, size: jnp.pad(x, ((0, size - x.shape[0]), (0, 0)))

    def expert_weights(values):
        expert_in, expert_out, pieces = values
        mine = jnp.transpose(pieces, (1, 0, 2)).reshape(3, shared, width)
        rows_in = jnp.transpose(expert_in, (0, 2, 3, 1))
        win = [
            block
            for side in range(2)
            for block in [tall(rows_in[e, side], units) for e in range(local)]
            + [tall(mine[side], shared_units)]
        ]
        wout = [tall(expert_out[e], units) for e in range(local)] + [tall(mine[2], shared_units)]
        return jnp.concatenate(win, axis=0), jnp.concatenate(wout, axis=0)

    x_own = jnp.moveaxis(states, 1, 0).reshape(rows, width).astype(F32)
    h1_f, rstd_in = normed(x_own, gain_in)
    h1_own = h1_f.astype(BF16)
    h1_blk = normed(states_blk.astype(F32), gain_in)[0].astype(BF16)
    pos_own = blk * block_pos + head * own_pos + jnp.arange(own_pos, dtype=jnp.int32)
    table_own = jnp.tile(angles(pos_own), (seqs, 1))
    pos_blk = blk * block_pos + jnp.arange(block_pos, dtype=jnp.int32)
    table_blk = jnp.broadcast_to(
        angles(pos_blk).reshape(n_head, 1, own_pos, ROPE // 2), (n_head, seqs, own_pos, ROPE // 2)
    ).reshape(block_rows, ROPE // 2)
    lat = dot(h1_own, down)
    lat_c = lat[:, :RANK]
    latn_f, rstd_kv = normed(lat_c, gain_kv)
    payload = jnp.concatenate(
        [latn_f, rotate(lat[:, RANK:], table_own), jnp.zeros((rows, 128 - ROPE), F32)], axis=1
    ).astype(BF16)
    z, inner, y, _ = split_dims(n_blk, n_head)
    order = [z[2], y[0][2], n_blk // z[2]]
    payload, pieces = phase((by_rows(payload), pieces))
    pieces = lax.all_to_all(pieces, "blk", split_axis=0, concat_axis=0, tiled=True)
    *lats, wup = gather_two(payload, n_blk, n_head, wup)
    lats, wo = phase((lats, w_out))
    wo = lax.all_gather(wo, "blk", axis=1, tiled=True)
    lats = [
        [x.reshape(tuple(shape) + (own_pos, -1)) for x in pair]
        for pair, shape in zip(lats, ([order[2], order[1], order[0]], [order[1], order[2], order[0]]))
    ]
    key_blocks = jnp.arange(n_blk, dtype=jnp.int32)
    key_at = jnp.concatenate(
        [jnp.full((1,), blk, jnp.int32), relative(inner, key_blocks) + 0 * key_blocks, relative([z], key_blocks)]
    ).astype(jnp.int32)
    query = dot(h1_blk, wq)
    cosine = jnp.tile(jnp.cos(table_blk), (1, heads))
    sine = jnp.tile(jnp.sin(table_blk), (1, heads))
    q_first, q_second = query[:, -2 * lanes : -lanes], query[:, -lanes:]
    turned = (q_first * cosine - q_second * sine, q_second * cosine + q_first * sine)
    step = ROPE // 2
    query = jnp.concatenate(
        [
            block
            for h in range(heads)
            for block in (
                query[:, h * NOPE : (h + 1) * NOPE],
                *(half[:, h * step : (h + 1) * step] for half in turned),
                jnp.zeros((block_rows, HEAD - NOPE - ROPE), F32),
            )
        ],
        axis=1,
    ).astype(BF16)
    shape4 = (n_head, seqs, own_pos, -1)
    query = query.reshape(shape4)
    seq_axes = list(zip(range(seqs), lats, (1, 0)))
    att_seqs, lses = zip(*(attention(key_at, s, query, pair, wup, axis, heads) for s, pair, axis in seq_axes))
    att_rows = jnp.concatenate(att_seqs, axis=1).reshape(block_rows, heads * VALUE)
    y_own = x_own + scatter_head(dot(att_rows, wo).astype(BF16)).astype(F32)
    h2_f, rstd_ffn = normed(y_own, gain_ffn)
    h2_own = h2_f.astype(BF16)

    routes_own = take_own(routes)
    mask = jnp.any(routes_own[:, :, None] == jnp.arange(experts, dtype=jnp.int32), axis=1)
    logits = jnp.where(mask, dot(h2_own, router), -1e30)
    gates = jnp.where(mask, jnp.exp(logits - jnp.max(logits, axis=1, keepdims=True)), 0.0)
    gates = gates / jnp.sum(gates, axis=1, keepdims=True)
    assert experts <= 128
    tail = jnp.zeros((rows, 128 - experts), BF16)
    base = jnp.full((1,), blk * local, jnp.int32)
    x_ext = jnp.concatenate([h2_own, gates.astype(BF16), tail], axis=1)
    rounds = max(1, total_rows // 4096)

    def in_turn(run, parts, count):
        outs, sums, stores, start = [], [], (), 0
        total = sum(2 * part[0][0].shape[0] for part in parts)
        for i, part in enumerate(parts):
            if i == 2:
                sums[0], part = phase((sums[0], part))
            outs.append(run(*part, total, start, stores))
            stores = outs[-1][:count]
            start += 2 * part[0][0].shape[0]
            sums.append(sum_cores(outs[-1][-2:], n_blk, n_head))
        return outs, sums

    def forward(x_rows, weights=None):
        if weights is None:
            pairs, (win, wout) = gather_parts(
                x_rows, n_blk, n_head, expert_weights, (expert_in, expert_out, pieces)
            )
        else:
            pairs, (win, wout) = gather_parts(x_rows, n_blk, n_head)[0], weights
        outs, sums = in_turn(
            lambda pair, *rest: run_experts(base, pair, win, wout, units, local, *rest),
            [(pair,) for pair in pairs],
            1,
        )
        kept = [(pair, out[1]) for pair, out in zip(pairs, outs)], outs[-1][0]
        return kept, (win, wout), scatter_parts(sums, n_blk, n_head)[0]

    def products(values):
        return tuple(dot_tn(values[i], values[i + 1]) for i in range(0, len(values), 2))

    def backward(grad_rows, kept, weights):
        win, wout = weights
        parts, x_all = kept
        outs, sums = in_turn(
            lambda grads, pair, gu, *rest: run_experts_back(
                base, grads, pair, gu, win, wout, units, local, *rest
            ),
            [
                (grads, pair, gu)
                for grads, (pair, gu) in zip(gather_parts(grad_rows, n_blk, n_head)[0], parts)
            ],
            3,
        )
        hid_all, act_all, grad_all = outs[-1][:3]
        back, ((d_win,), (d_wout,)) = scatter_parts(
            sums, n_blk, n_head, (products, products), ((hid_all, x_all), (act_all, grad_all))
        )
        return back, d_win, d_wout

    def in_rounds(x):
        return x.reshape((rounds, -1) + x.shape[1:])

    if rounds == 1:
        kept, weights, mixed = forward(x_ext)
    else:
        weights = expert_weights((expert_in, expert_out, pieces))
        mixed = lax.map(lambda x: forward(x, weights)[2], in_rounds(x_ext)).reshape(rows, width)
    mixed = mixed.astype(F32)
    out_own = (y_own + mixed).astype(BF16)
    diff = out_own.astype(F32) - take_own(teacher).astype(F32)
    valid_own = take_own(valid).astype(F32)[:, None]
    loss_part = jnp.sum(valid_own * diff * diff)
    grad_own = diff * valid_own * (total_rows / count)

    grad_own_b = grad_own.astype(BF16)
    if rounds == 1:
        back, d_win, d_wout = backward(grad_own_b, kept, weights)
    else:

        def round_back(sums, both):
            kept, _, _ = forward(both[0], weights)
            back, d_win, d_wout = backward(both[1], kept, weights)
            return (sums[0] + d_win, sums[1] + d_wout), back

        start = (jnp.zeros((2 * padded, width), F32), jnp.zeros((padded, width), F32))
        (d_win, d_wout), back = lax.scan(round_back, start, (in_rounds(x_ext), in_rounds(grad_own_b)))
        back = back.reshape(rows, -1)
    d_sh = jnp.concatenate(
        [d_win[s * padded + local * units :][:shared] for s in range(2)]
        + [d_wout[local * units :][:shared]],
        axis=0,
    )
    d_sh = phase(d_sh).astype(BF16)
    d_sh = jnp.transpose(d_sh.reshape(3 * shared, n_blk, part), (1, 0, 2))
    back, d_win, d_wout, d_sh = lax.optimization_barrier((back, d_win, d_wout, d_sh))
    back = back.astype(F32)

    d_gates = back[:, width : width + experts]
    d_logits = gates * (d_gates - jnp.sum(gates * d_gates, axis=1, keepdims=True))
    d_logits = d_logits.astype(BF16)
    grad_router = dot_tn(h2_own, d_logits)
    dh2 = back[:, :width] + dot_nt(d_logits, router)
    dy_branch, grad_gain_ffn = norm_back(dh2, y_own, rstd_ffn, gain_ffn)
    dy_own = grad_own + dy_branch

    dy_blk = gather_head(dy_own.astype(BF16))
    grad_wo = dot_tn(att_rows, dy_blk).astype(BF16)
    d_att = dot_nt(dy_blk, wo).astype(BF16).reshape(shape4)
    grad_wo, d_att = phase((grad_wo, d_att))
    wo_steps = scatter_columns(grad_wo, n_blk)
    dqs, d_lats, d_ups = [], [], []
    for (s, pair, axis), att, lse in zip(seq_axes, att_seqs, lses):
        dq, first, second, d_up = attention_back(
            key_at, s, query, pair, wup, att, d_att, lse, axis, heads
        )
        if s == 0:
            grad_wo, d_att = phase((next(wo_steps), d_att))
        dqs.append(dq)
        d_lats.append([x.reshape(total_rows // 4, -1) for x in (first, second)])
        d_ups.append(d_up)
    for grad_wo in wo_steps:
        pass
    grad_wo = grad_wo.astype(F32)
    dq = jnp.concatenate(dqs, axis=1)
    d_up = sum(d_ups).astype(BF16)
    dq = dq.reshape(block_rows, heads, HEAD)
    first, second = (
        dq[:, :, at : at + step].reshape(block_rows, lanes).astype(F32) for at in (NOPE, NOPE + step)
    )
    dq = jnp.concatenate(
        [
            dq[:, :, :NOPE].reshape(block_rows, heads * NOPE),
            (first * cosine + second * sine).astype(BF16),
            (second * cosine - first * sine).astype(BF16),
        ],
        axis=1,
    )
    dh1 = scatter_head(dot_nt(dq, wq).astype(BF16)).astype(F32)
    up_rows = w_up_kv.shape[0]
    wide = up_rows * w_up_kv.shape[1] // part
    grad_wq = by_rows(dot_tn(h1_blk, dq).astype(BF16)).reshape(n_blk, part, -1)
    d_up = jnp.moveaxis(d_up.reshape(n_blk, up_rows, -1, wide), 2, 1).reshape(n_blk, part, wide)
    joined = jnp.concatenate([grad_wq, d_up], axis=2)
    joined, d_win, d_wout, d_sh = phase((by_rows(joined), d_win, d_wout, d_sh))
    d_lat, (d_win, d_wout) = scatter_two(*d_lats, n_blk, n_head, (d_win, d_wout))
    d_lat, d_sh = phase((d_lat, d_sh))
    d_lat = by_rows(d_lat)[:, : RANK + ROPE].astype(F32)
    joined = by_rows(lax.psum_scatter(joined, "blk", scatter_dimension=0, tiled=False)).astype(F32)
    grad_wq = joined[:, :-wide]
    grad_up = jnp.moveaxis(joined[:, -wide:].reshape(-1, up_rows, wide), 0, 1).reshape(up_rows, -1)
    grad_ein = jnp.concatenate(
        [d_win[s * padded + e * units :][:eff] for e in range(local) for s in range(2)], axis=0
    )
    grad_ein = jnp.transpose(grad_ein.reshape(local, 2, eff, width), (0, 3, 1, 2))
    grad_eout = jnp.concatenate([d_wout[e * units :][:eff] for e in range(local)], axis=0)
    grad_eout = grad_eout.reshape(local, eff, width)
    d_sh = lax.all_to_all(d_sh, "blk", split_axis=0, concat_axis=0, tiled=True).astype(F32)
    grad_shin = jnp.transpose(d_sh[:, : 2 * shared].reshape(n_blk, 2, shared, part), (3, 1, 0, 2)).reshape(
        part, 2, n_blk * shared
    )
    grad_shout = d_sh[:, 2 * shared :].reshape(n_blk * shared, part)
    grad_wq = jnp.concatenate(
        [
            grad_wq[:, : heads * NOPE].reshape(part, heads, NOPE),
            grad_wq[:, heads * NOPE : -lanes].reshape(part, heads, ROPE // 2),
            grad_wq[:, -lanes:].reshape(part, heads, ROPE // 2),
        ],
        axis=2,
    ).reshape(part, -1)
    d_lat_c, grad_gain_kv = norm_back(d_lat[:, :RANK], lat_c, rstd_kv, gain_kv)
    d_lat_b = jnp.concatenate([d_lat_c, rotate(d_lat[:, RANK : RANK + ROPE], -table_own)], axis=1).astype(BF16)
    d_lat_b = by_rows(d_lat_b)
    d_lat_blk = gather_head(d_lat_b)
    grad_down = by_rows(dot_tn(h1_blk, d_lat_blk).astype(BF16)).reshape(n_blk, n_head, quarter, -1)
    grad_down = lax.dynamic_index_in_dim(grad_down, head, 1, keepdims=False)
    grad_down = gather_head(by_rows(scatter_axis(grad_down, blks))).astype(F32)
    dh1 = dh1 + dot_nt(d_lat_b, down)
    dx_branch, grad_gain_in = norm_back(dh1, x_own, rstd_in, gain_in)
    dx_own = dy_own + dx_branch

    loss_high = loss_part.astype(BF16).astype(F32)
    sums = jnp.concatenate(
        [
            grad_gain_in.reshape(n_blk, -1),
            grad_gain_ffn.reshape(n_blk, -1),
            grad_router.reshape(n_blk, -1),
            grad_gain_kv.reshape(n_blk, -1),
            jnp.full((n_blk, 1), loss_high),
            jnp.full((n_blk, 1), loss_part - loss_high),
        ],
        axis=1,
    )
    sums = scatter_axis(sums, blks)
    for dim in heads_ring:
        sums = sum(ring_gather(sums, dim))
    out_gain_in = sums[:part]
    out_gain_ffn = sums[part : 2 * part]
    at = 2 * part
    out_router = sums[at : at + part * experts].reshape(part, experts)
    at += part * experts
    out_gain_kv = sums[at : at + RANK // n_blk]
    loss = (sums[-2] + sums[-1]) / (width * count)

    def give(x):
        return jnp.moveaxis(x.reshape(seqs, own_pos, width), 0, 1)

    return (
        give(out_own), loss, give(dx_own), out_gain_in, grad_wq, grad_down, out_gain_kv, grad_up,
        grad_wo, out_gain_ffn, out_router, grad_shin, grad_shout, grad_ein, grad_eout,
    )


def solution(mesh):
    in_specs = (
        P(BOTH, None, None), P("blk", None, None), P("blk", None), P("blk", None, None), P("blk"),
        P("blk", "head"), P("blk", None), P("blk"), P("blk", "head"), P("head", "blk"), P("blk"),
        P("blk", None), P("blk", None, "head"), P("head", "blk"), P("blk", None, None, "head"),
        P("blk", "head", None),
    )
    out_specs = (
        P(BOTH, None, None), P(), P(BOTH, None, None), P("blk"), P("blk", "head"), P("blk", None),
        P("blk"), P("blk", "head"), P("head", "blk"), P("blk"), P("blk", None), P("blk", None, "head"),
        P("head", "blk"), P("blk", None, None, "head"), P("blk", "head", None),
    )
    return jax.shard_map(on_device, mesh=mesh, in_specs=in_specs, out_specs=out_specs, check_vma=False)
```
